256 devices in a mesh: frame: 64 (over y, x_lo, z), patch: 4 (over x_hi, core).
Axes of the slice: x: 4 (x_hi: 2, x_lo: 2; x = x_hi * 2 + x_lo), y: 4, z: 8, core: 2. Of those that a mesh axis runs over, the one named last changes fastest.
Arguments:
- sky_image: float32 [64, 512, 1024], P('frame', None, 'patch'), may hold values from 0.5 to 1.5
- coefficients: float32 [64, 32, 64], P('frame', 'patch'), may hold values from -0.9 to 0.9
- mode_basis: float32 [64, 20736], replicated, may hold values from -6 to 6
- aperture: int32 [144, 144], replicated, may hold values from 0 to 1, as said below
Outputs:
- mode_gradient: float32 [64, 32, 64], P('frame', 'patch')
- object_spectrum: float32 [32, 2, 20736], P('patch', None, 'frame')
The draws below stay inside these ranges and needn't reach their ends.
Inputs may be any that keep to these rules, and one draw needn't show every extreme that they name: `aperture`: 0 outside an annulus centred at (72, 72) with outer radius between 28 and 36 pixels and a central obstruction; inside it, each pixel is 1 except for randomly placed dead pixels, which are 0.
All inputs are finite; a program needn't handle non-finite values.
Results may differ from the reference program's by a relative error of at most 0.0003.
Values sent between devices are 32-bit elements; how exact they have to be, the bound alone decides.
A program may use at most 128 MiB of HBM per device.

```python
import math
import jax
import jax.numpy as jnp
from jax import lax

P_SIZE = 144
RIM = 8
NZ = 64
PR = 4
FRAMES = 64
PATCHES = 32
ROWS = 512
COLS = 1024


def draw_aperture(key, part):
    base_key = jax.random.fold_in(key, 11)
    key_outer, key_inner, key_dead = jax.random.split(base_key, 3)
    radius = jax.random.randint(key_outer, (), P_SIZE // 5, P_SIZE // 4 + 1)
    inner_radius = jax.random.randint(key_inner, (), 1, P_SIZE // 16 + 2)
    offsets = jnp.arange(P_SIZE, dtype=jnp.int32) - P_SIZE // 2
    squared = offsets[:, None] * offsets[:, None] + offsets[None, :] * offsets[None, :]
    inside = jnp.logical_and(squared <= radius * radius, squared > inner_radius * inner_radius)
    alive = jax.random.randint(key_dead, (P_SIZE, P_SIZE), 0, 8) > 0
    return jnp.logical_and(inside, alive).astype(jnp.int32)


def level_of(stream_key, dims, shards, low, largest):
    factor_of, own = 1.0, jax.random.fold_in(stream_key, 6)
    for axis_at, parts in shards:
        heights = jnp.exp(jax.random.uniform(jax.random.fold_in(own, axis_at), (parts,), jnp.float32, low / len(shards), largest / len(shards)))
        factor_of = factor_of * jnp.repeat(heights, dims[axis_at] // parts).reshape([-1 if axis == axis_at else 1 for axis in range(len(dims))])
    return factor_of


def noise(own_key, extent, width, bound, cuts=(), held_as=jnp.bfloat16):
    drawn = width * jax.random.normal(own_key, extent, jnp.float32)
    if cuts:
        drawn = drawn * level_of(own_key, extent, cuts, -0.22, 0.18)
    return jnp.clip(drawn, -bound, bound).astype(held_as)


def setup_inputs(seed: int = 0) -> dict:
    key_of = jax.random.split(jax.random.key(seed), 5)
    return {
        "sky_image": jnp.clip(0.5 + 1.0 * jax.random.uniform(key_of[0], (FRAMES, ROWS, COLS), jnp.float32) ** level_of(key_of[0], (FRAMES, ROWS, COLS), ((0, 64), (2, 4)), -0.2, 0.2), 0.5, 1.5),
        "coefficients": noise(key_of[1], (FRAMES, PATCHES, NZ), 0.15, 0.9, ((0, 64), (1, 4)), jnp.float32),
        "mode_basis": noise(key_of[2], (NZ, P_SIZE * P_SIZE), 1.0, 6.0, (), jnp.float32),
        "aperture": draw_aperture(jax.random.fold_in(key_of[4], 71), 0),
    }


reg_weight = 0.02

def window_table():
    offsets = jnp.arange(P_SIZE, dtype=jnp.float32)
    distance = jnp.minimum(offsets, P_SIZE - 1 - offsets)
    taper_value = 0.3 + 0.7 * jnp.sin(math.pi * (distance + 1.0) / (2.0 * (RIM + 1))) ** 2
    profile = jnp.where(distance < RIM, taper_value, 1.0)
    return profile[:, None] * profile[None, :]

def reference(sky_image, coefficients, mode_basis, aperture):
    tile_side = P_SIZE - 2 * RIM
    frame_total = sky_image.shape[0]
    padded = jnp.pad(sky_image, ((0, 0), (RIM, RIM), (RIM, RIM)))
    window = window_table()
    pupil_mask = aperture.astype(jnp.float32)
    pupil_area = jnp.sum(pupil_mask)
    damping = reg_weight * frame_total

    def one_patch(patch_item):
        position, mode_weights = patch_item
        row_start = (position % PR * tile_side).astype(jnp.int32)
        column_start = (position // PR * tile_side).astype(jnp.int32)
        block = lax.dynamic_slice(padded, (jnp.int32(0), row_start, column_start), (frame_total, P_SIZE, P_SIZE))
        data = jnp.fft.fft2(window * block) / P_SIZE

        def metric(weights_now):
            phase_map = jnp.dot(weights_now, mode_basis, precision=lax.Precision.HIGHEST).reshape(frame_total, P_SIZE, P_SIZE)
            pupil = pupil_mask * jnp.cos(phase_map) + 1j * (pupil_mask * jnp.sin(phase_map))
            focal_field = jnp.fft.fft2(pupil)
            intensity = (jnp.real(focal_field) ** 2 + jnp.imag(focal_field) ** 2) / (P_SIZE * P_SIZE * pupil_area)
            transfer = jnp.fft.fft2(intensity)
            numerator = lax.optimization_barrier(jnp.sum(jnp.conj(transfer) * data, axis=0))
            power = lax.optimization_barrier(jnp.sum(jnp.real(transfer) ** 2 + jnp.imag(transfer) ** 2, axis=0)) + damping
            energy = jnp.sum(jnp.real(data) ** 2 + jnp.imag(data) ** 2)
            fitted = jnp.sum((jnp.real(numerator) ** 2 + jnp.imag(numerator) ** 2) / power)
            return ((energy - fitted) / (P_SIZE * P_SIZE), (numerator, power))
        gradient, (numerator, power) = jax.grad(metric, has_aux=True)(mode_weights)
        estimate = numerator / power
        gradient = gradient - lax.optimization_barrier(jnp.mean(gradient, axis=0, keepdims=True))
        return (gradient, jnp.stack([jnp.real(estimate).reshape(-1), jnp.imag(estimate).reshape(-1)]))
    gradient, objects = lax.map(one_patch, (jnp.arange(PATCHES, dtype=jnp.int32), jnp.transpose(coefficients, (1, 0, 2))))
    return (jnp.transpose(gradient, (1, 0, 2)), objects)
```

```python
import math

import jax
import jax.numpy as jnp
import ml_dtypes
import numpy as np
from jax import lax
from jax.experimental import pallas as pl
from jax.experimental.pallas import tpu as pltpu
from jax.sharding import PartitionSpec as P

SIDE = 144
RIM = 8
TILE = SIDE - 2 * RIM
LOW, BOX = 32, 80
GROUP = 8
DEPTH = 8
STRIPS = 4
FRAMES = GROUP * DEPTH
HALF = SIDE // 2 + 1
CHUNK = SIDE // DEPTH
FLAT = BOX * SIDE
PERIOD = 8 * SIDE
MODES = 64
SHARE = SIDE * SIDE // FRAMES
DAMPING = 0.02 * FRAMES
MESH = pl.DeviceIdType.MESH
f32, bf16 = jnp.float32, jnp.bfloat16


def profile():
    at = np.arange(SIDE, dtype=np.float64)
    distance = np.minimum(at, SIDE - 1 - at)
    taper = 0.3 + 0.7 * np.sin(math.pi * (distance + 1.0) / (2.0 * (RIM + 1))) ** 2
    return np.where(distance < RIM, taper, 1.0)


def tables():
    k = np.arange(SIDE)
    u = np.arange(BOX) + LOW - SIDE // 2
    turn = 2.0 * math.pi / SIDE

    def pair(a, b):
        angle = turn * (np.outer(a, b) % SIDE)
        return np.cos(angle), np.sin(angle)

    parts = {}
    c, s = pair(k, u)
    parts["pupil_left"] = np.concatenate([c, s])
    t = np.zeros((256, 256))
    t[:BOX, :SIDE], t[128 : 128 + BOX, :SIDE] = c.T, s.T
    parts["pupil_right"] = t
    t = np.zeros((SIDE, 256))
    t[:, :BOX], t[:, 128 : 128 + BOX] = c, s
    parts["back_right"] = t
    parts["back_left"] = np.concatenate([c.T, s.T])
    c, s = pair(k, k)
    parts["left"] = np.concatenate([c, s])
    t = np.zeros((SIDE, 256))
    t[:, :HALF], t[:, 128 : 128 + HALF] = c[:, :HALF], -s[:, :HALF]
    parts["right"] = t
    order = np.concatenate([k[RIM:-RIM], k[:RIM], k[-RIM:]])
    t = np.zeros((256, 256))
    w = profile()[:, None]
    t[:SIDE, :HALF], t[:SIDE, 128 : 128 + HALF] = (w * c)[order, :HALF], -(w * s)[order, :HALF]
    parts["data_right"] = t
    t = np.zeros((256, 256))
    twice = np.full((HALF, 1), 2.0)
    twice[0], twice[-1] = 1.0, 1.0
    t[:HALF, :SIDE], t[128 : 128 + HALF, :SIDE] = twice * c[:HALF], -twice * s[:HALF]
    parts["focal_right"] = t
    first, rows = {}, []
    for name, part in parts.items():
        first[name] = (sum(r.shape[0] for r in rows), part.shape[0], part.shape[1])
        rows.append(np.pad(part, ((0, 0), (0, 256 - part.shape[1]))))
    whole = np.concatenate(rows)
    high = whole.astype(ml_dtypes.bfloat16)
    rest = (whole - high.astype(np.float64)).astype(ml_dtypes.bfloat16)
    return np.stack([high, rest]), first


TABLE, FIRST = tables()


def split(x):
    high = x.astype(bf16)
    return high, (x - high.astype(f32)).astype(bf16)


def mm(a, b):
    return jnp.dot(a, b, preferred_element_type=f32)


def mm3(a, b):
    return mm(a[0], b[0]) + (mm(a[0], b[1]) + mm(a[1], b[0]))


def lanes(*parts):
    return jnp.concatenate(parts, axis=1)


def sine_cosine(x):
    quarter = jnp.floor(x * (2.0 / math.pi) + 0.5)
    r = x - quarter * 1.5703125
    r = r - quarter * 4.837512969970703125e-4
    r = r - quarter * 7.54978995489188216e-8
    z = r * r
    sine = ((-1.9515295891e-4 * z + 8.3321608736e-3) * z - 1.6666654611e-1) * z * r + r
    cosine = ((2.443315711809948e-5 * z - 1.388731625493765e-3) * z + 4.166664568298827e-2) * z * z - 0.5 * z + 1.0
    halves = jnp.floor(quarter * 0.5)
    odd = quarter - 2.0 * halves
    minus = 1.0 - 2.0 * (halves - 2.0 * jnp.floor(halves * 0.5))
    swap = odd > 0.5
    return (
        jnp.where(swap, cosine, sine) * minus,
        jnp.where(swap, -sine, cosine) * minus,
    )


def kernel(
    sky, coef, basis, aperture, table_hbm, window_hbm,
    gradient_out, object_out,
    tab, win, skyp, coef_v, coef_send, coef_recv, mask_v, base, base3,
    edges, img, halo, turned, pre, pim, fre, fim, tre, tim, dre, dim_,
    sums, sum_send, sum_recv, sum_v, obj_send, obj_all, ore, oim, dph,
    full, out_send, out_recv, grad_send, grad_recv, ret_send, ret_recv,
    local_sem, coef_ss, coef_rs, img_ss, img_rs, own_ss, own_rs, cross_ss, cross_rs,
    sum_ss, sum_rs, obj_ss, obj_rs, out_ss, out_rs, grad_ss, grad_rs, ret_ss, ret_rs,
):
    place, strip = lax.axis_index("frame"), lax.axis_index("patch")
    me, z = place // DEPTH, place % DEPTH

    def at(group, depth, which=None):
        return {"frame": group * DEPTH + depth, "patch": strip if which is None else which}

    def remote(src, dst, send, recv, device):
        return pltpu.make_async_remote_copy(
            src_ref=src, dst_ref=dst, send_sem=send, recv_sem=recv, device_id=device, device_id_type=MESH
        )

    def table(name):
        row, count, width = FIRST[name]
        return tab[0, row : row + count, :width], tab[1, row : row + count, :width]

    loads = [
        pltpu.make_async_copy(coef.at[0], coef_v, local_sem.at[0]),
        pltpu.make_async_copy(basis.at[:, pl.ds(LOW * SIDE, FLAT)], base, local_sem.at[1]),
        pltpu.make_async_copy(sky.at[0], skyp.at[pl.ds(RIM, 512)], local_sem.at[2]),
        pltpu.make_async_copy(table_hbm, tab, local_sem.at[3]),
        pltpu.make_async_copy(window_hbm, win, local_sem.at[4]),
        pltpu.make_async_copy(aperture, mask_v, local_sem.at[5]),
    ]
    for load in loads:
        load.start()

    barrier = pltpu.get_barrier_semaphore()
    beside = lax.rem(strip + jnp.where(me < 4, STRIPS - 1, 1), STRIPS)

    def greet(device):
        pl.semaphore_signal(barrier, inc=1, device_id=device, device_id_type=MESH)

    for d in range(1, GROUP):
        greet(at(lax.rem(me + d, GROUP), z))
    for d in range(1, DEPTH):
        greet(at(me, lax.rem(z + d, DEPTH)))
    for j in range(GROUP):
        greet(at(j, z, beside))

    skyp[pl.ds(0, RIM), :] = jnp.zeros((RIM, 256), f32)
    skyp[pl.ds(512 + RIM, 120), :] = jnp.zeros((120, 256), f32)
    loads[0].wait()
    for p in range(GROUP):
        row = jnp.broadcast_to(coef_v[p : p + 1, :], (8, MODES))
        coef_send[p * 8 : p * 8 + 8, :] = lanes(row, row)
    loads[2].wait()
    for half in range(2):
        strip_t = skyp[:, half * 128 : half * 128 + 128].T
        edges[2 * half] = strip_t[:8]
        edges[2 * half + 1] = strip_t[120:]
    pl.semaphore_wait(barrier, GROUP - 1 + DEPTH - 1 + GROUP)

    sends = []
    def rows8(ref, j):
        return ref.at[pl.ds(pl.multiple_of(j * 8, 8), 8)]

    for d in range(1, GROUP):
        t = lax.rem(me + d, GROUP)
        c = remote(rows8(coef_send, t), rows8(coef_recv, me), coef_ss.at[t], coef_rs.at[me], at(t, z))
        c.start()
        sends.append(c)
    coef_recv[pl.ds(pl.multiple_of(me * 8, 8), 8), :] = coef_send[pl.ds(pl.multiple_of(me * 8, 8), 8), :]

    def main_of(t):
        return skyp.at[
            pl.ds(pl.multiple_of(lax.rem(t, 4) * TILE, TILE), SIDE), pl.ds(pl.multiple_of((t // 4) * 128, 128), 128)
        ]

    def edge_of(kind, t):
        return edges.at[kind, :, pl.ds(pl.multiple_of(lax.rem(t, 4) * TILE, TILE), 256)]

    for d in range(1, GROUP):
        t = lax.rem(me + d, GROUP)
        c = remote(main_of(t), img.at[me], img_ss.at[t], img_rs.at[me], at(t, z))
        c.start()
        sends.append(c)
        kind, side = jnp.where(t < 4, 2, 1), jnp.where(t < 4, 1, 0)
        c = remote(edge_of(kind, t), halo.at[me, side], own_ss.at[t], own_rs.at[me], at(t, z))
        c.start()
        sends.append(c)
    for p in range(GROUP):
        kind, side, step = (3, 0, 1) if p < 4 else (0, 1, STRIPS - 1)
        c = remote(
            edge_of(kind, p), halo.at[me, side], cross_ss.at[p], cross_rs.at[me],
            at(p, z, lax.rem(strip + step, STRIPS)),
        )
        c.start()
        sends.append(c)
    own_side = jnp.where(me < 4, 1, 0)
    mine = [
        pltpu.make_async_copy(main_of(me), img.at[me], local_sem.at[6]),
        pltpu.make_async_copy(edge_of(jnp.where(me < 4, 2, 1), me), halo.at[me, own_side], local_sem.at[7]),
    ]
    for c in mine:
        c.start()

    loads[1].wait()

    def cut(g, carry):
        at_g = pl.ds(pl.multiple_of(g * PERIOD, 128), PERIOD)
        x = base[:, at_g]
        h, r = split(x)
        base3[0:MODES, at_g] = h
        base3[MODES : 2 * MODES, at_g] = r
        base3[2 * MODES :, at_g] = (x - h.astype(f32) - r.astype(f32)).astype(bf16)
        return carry

    lax.fori_loop(0, BOX // 8, cut, 0)
    for load in loads[3:]:
        load.wait()

    lane = lax.broadcasted_iota(jnp.int32, (8, 128), 1)
    mask = mask_v[LOW : LOW + BOX, 0:128].astype(f32)
    mask = pltpu.roll(mask, 128 - LOW, 1)
    mask = jnp.where(lax.broadcasted_iota(jnp.int32, (BOX, 128), 1) < BOX, mask, 0.0)
    area = jnp.sum(mask)
    intensity_scale = 1.0 / (SIDE * SIDE * area)
    dph[0:BOX, :] = mask

    for d in range(1, GROUP):
        j = lax.rem(me + GROUP - d, GROUP)
        remote(rows8(coef_send, j), rows8(coef_recv, j), coef_ss.at[j], coef_rs.at[j], at(j, z)).wait_recv()
    weights = coef_recv[pl.ds(0, GROUP, stride=8), :]
    w0 = weights.astype(bf16).astype(f32)
    w1 = (weights - w0).astype(bf16).astype(f32)
    w2 = weights - w0 - w1
    weights = jnp.concatenate([lanes(w, w[:, :MODES]) for w in (w0, w1, w2)]).astype(bf16)

    starts = [divmod(SIDE * r + LOW, 128) for r in range(8)]

    def pupils(g, carry):
        ph = mm(weights, base3[:, pl.ds(pl.multiple_of(g * PERIOD, 128), PERIOD)])
        ph = ph[0:8] + (ph[8:16] + ph[16:24])
        rows = []
        for tile, off in starts:
            x = ph[:, tile * 128 : tile * 128 + 128]
            if off:
                x = pltpu.roll(x, 128 - off, 1)
            if off + BOX > 128:
                y = pltpu.roll(ph[:, tile * 128 + 128 : tile * 128 + 256], 128 - off, 1)
                x = jnp.where(lane < 128 - off, x, y)
            rows.append(x)
        m = dph[pl.ds(pl.multiple_of(g * 8, 8), 8), :]
        m = jnp.concatenate([jnp.broadcast_to(m[r : r + 1], (8, 128)) for r in range(8)])
        sine, cosine = sine_cosine(jnp.concatenate(rows))
        at_g = pl.ds(pl.multiple_of(g * 64, 64), 64)
        pre[at_g, :] = m * cosine
        pim[at_g, :] = m * sine
        return carry

    lax.fori_loop(0, BOX // 8, pupils, 0)

    def of_frame(ref, f):
        return ref[pl.ds(f, BOX, stride=GROUP), :]

    def left_forward(x):
        y = mm3(table("left"), split(x))
        return y[:SIDE, :128] + y[SIDE:, 128:], y[:SIDE, 128:] - y[SIDE:, :128]

    def transfers(f, carry):
        b = mm3(table("pupil_left"), split(lanes(of_frame(pre, f), of_frame(pim, f))))
        b_re = b[:SIDE, :128] + b[SIDE:, 128:]
        b_im = b[:SIDE, 128:] - b[SIDE:, :128]
        (rh, rl), (ih, il) = split(b_re), split(b_im)
        field = mm3(
            (
                jnp.concatenate([lanes(rh, ih), lanes(ih, -rh)]),
                jnp.concatenate([lanes(rl, il), lanes(il, -rl)]),
            ),
            table("pupil_right"),
        )
        field_re, field_im = field[:SIDE], field[SIDE:]
        fre[f] = field_re
        fim[f] = field_im
        intensity = (field_re * field_re + field_im * field_im) * intensity_scale
        tre[f], tim[f] = left_forward(mm3(split(intensity[:, :SIDE]), table("right")))
        return carry

    lax.fori_loop(0, GROUP, transfers, 0)

    for c in mine:
        c.wait()
    for j in range(GROUP):
        remote(edge_of(0, 0), halo.at[j, 1 - own_side], cross_ss.at[j], cross_rs.at[j], at(j, z, beside)).wait_recv()
    for d in range(1, GROUP):
        j = lax.rem(me + GROUP - d, GROUP)
        remote(main_of(j), img.at[j], img_ss.at[j], img_rs.at[j], at(j, z)).wait_recv()
        remote(edge_of(0, j), halo.at[j, own_side], own_ss.at[j], own_rs.at[j], at(j, z)).wait_recv()
    row = lax.broadcasted_iota(jnp.int32, (128, 256), 0)
    left_on = jnp.where(jnp.logical_and(strip == 0, me < 4), 0.0, 1.0)
    right_on = jnp.where(jnp.logical_and(strip == STRIPS - 1, me >= 4), 0.0, 1.0)
    rims = halo[...].reshape(128, 256) * jnp.where(lax.rem(row, 16) < 8, left_on, right_on)
    rims = rims.T[:SIDE]
    for f in range(GROUP):
        turned[f] = pltpu.roll(rims, (128 - 16 * f) % 128, 1) if f else rims

    sums[...] = jnp.zeros_like(sums)

    def data(f, carry):
        w = win[...]
        x = lanes(img[f] * w, turned[f] * w)
        d_re, d_im = left_forward(mm3(split(x), table("data_right")))
        dre[f] = d_re
        dim_[f] = d_im
        t_re, t_im = tre[f], tim[f]
        sums[0:SIDE, :] += t_re * d_re + t_im * d_im
        sums[SIDE : 2 * SIDE, :] += t_re * d_im - t_im * d_re
        sums[2 * SIDE :, :] += t_re * t_re + t_im * t_im
        return carry

    lax.fori_loop(0, GROUP, data, 0)

    for d in range(DEPTH):
        for part in range(3):
            sum_send[d, part * CHUNK : part * CHUNK + CHUNK, :] = sums[
                part * SIDE + d * CHUNK : part * SIDE + d * CHUNK + CHUNK, :
            ]
        sum_send[d, 3 * CHUNK :, :] = jnp.zeros((2, 128), f32)
    for d in range(1, DEPTH):
        t = lax.rem(z + d, DEPTH)
        c = remote(sum_send.at[t], sum_recv.at[z], sum_ss.at[t], sum_rs.at[z], at(me, t))
        c.start()
        sends.append(c)
    sum_recv[z] = sum_send[z]
    for d in range(1, DEPTH):
        j = lax.rem(z + DEPTH - d, DEPTH)
        remote(sum_send.at[j], sum_recv.at[j], sum_ss.at[j], sum_rs.at[j], at(me, j)).wait_recv()
    total = sum_recv[0]
    for j in range(1, DEPTH):
        total = total + sum_recv[j]
    sum_v[...] = total
    power = sum_v[2 * CHUNK : 3 * CHUNK, :] + DAMPING
    obj_send[0:CHUNK, :] = sum_v[0:CHUNK, :] / power
    obj_send[CHUNK : 2 * CHUNK, :] = sum_v[CHUNK : 2 * CHUNK, :] / power
    obj_send[2 * CHUNK :, :] = jnp.zeros((4, 128), f32)
    for d in range(1, DEPTH):
        t = lax.rem(z + d, DEPTH)
        c = remote(obj_send, obj_all.at[z], obj_ss.at[t], obj_rs.at[z], at(me, t))
        c.start()
        sends.append(c)
    obj_all[z] = obj_send[...]
    for d in range(1, DEPTH):
        j = lax.rem(z + DEPTH - d, DEPTH)
        remote(obj_send, obj_all.at[j], obj_ss.at[j], obj_rs.at[j], at(me, j)).wait_recv()
    for d in range(DEPTH):
        ore[d * CHUNK : d * CHUNK + CHUNK, :] = obj_all[d, 0:CHUNK, :]
        oim[d * CHUNK : d * CHUNK + CHUNK, :] = obj_all[d, CHUNK : 2 * CHUNK, :]

    r_at = lax.broadcasted_iota(jnp.int32, (SIDE, SIDE), 0)
    c_at = lax.broadcasted_iota(jnp.int32, (SIDE, SIDE), 1)
    flip_rows = jnp.where(lax.rem(r_at + c_at, SIDE) == 0, 1.0, 0.0).astype(bf16)
    r_at = lax.broadcasted_iota(jnp.int32, (128, 256), 0)
    c_at = lax.broadcasted_iota(jnp.int32, (128, 256), 1)
    flip_columns = jnp.where(
        jnp.logical_and(r_at + c_at == SIDE, jnp.logical_and(c_at >= HALF, c_at < SIDE)), 1.0, 0.0
    ).astype(bf16)
    parts = split(lanes(ore[...], oim[...]))
    parts = [mm(flip_rows, part).astype(bf16) for part in parts]
    lane_full = lax.broadcasted_iota(jnp.int32, (SIDE, 128), 1)
    for n, sign in ((0, 1.0), (1, -1.0)):
        mirror = mm(parts[0][:, n * 128 : n * 128 + 128], flip_columns)
        mirror = sign * (mirror + mm(parts[1][:, n * 128 : n * 128 + 128], flip_columns))
        half = (ore, oim)[n][...]
        full[2 * n] = jnp.where(lane_full < HALF, half, mirror[:, :128])
        full[2 * n + 1] = mirror[:, 128:]
    first_row = z * 9 // 4
    for n in range(2):
        placed = [jnp.zeros((8, 128), f32) for _ in range(6)]
        for t in range(3):
            for piece in range(2):
                x = full[2 * n + piece, pl.ds(first_row + t, GROUP, stride=CHUNK), :]
                tile, off = divmod(SIDE * t + 128 * piece, 128)
                if off:
                    x = pltpu.roll(x, off, 1)
                    placed[tile + 1] += jnp.where(lane < off, x, 0.0)
                    x = jnp.where(lane < off, 0.0, x)
                placed[tile] += x
        placed = lanes(*placed)
        picked = jnp.zeros((8, 384), f32)
        for m in range(4):
            moved = pltpu.roll(placed, 768 - 36 * m, 1) if m else placed
            picked = picked + jnp.where(lax.rem(z, 4) == m, 1.0, 0.0) * moved[:, :384]
        for i in range(GROUP):
            out_send[i, n : n + 1, :] = picked[i : i + 1]
    for d in range(1, GROUP):
        t = lax.rem(me + d, GROUP)
        c = remote(out_send.at[t], out_recv.at[me], out_ss.at[t], out_rs.at[me], at(t, z))
        c.start()
        sends.append(c)
    out_recv[me] = out_send[me]

    scale = 2.0 / (SIDE * SIDE)

    def back(f, carry):
        o_re, o_im, t_re, t_im = ore[...], oim[...], tre[f], tim[f]
        e_re = dre[f] - (o_re * t_re - o_im * t_im)
        e_im = dim_[f] - (o_re * t_im + o_im * t_re)
        g_re = -scale * (e_re * o_re + e_im * o_im)
        g_im = scale * (e_re * o_im - e_im * o_re)
        y = mm3(table("left"), split(lanes(g_re, g_im)))
        h = lanes(y[:SIDE, :128] - y[SIDE:, 128:], y[:SIDE, 128:] + y[SIDE:, :128])
        focal = mm3(split(h), table("focal_right")) * (2.0 * intensity_scale)
        g = jnp.concatenate([focal * fre[f], focal * fim[f]])
        y = mm3(split(g[:, :SIDE]), table("back_right"))
        q = lanes(y[:SIDE, :128] - y[SIDE:, 128:], y[:SIDE, 128:] + y[SIDE:, :128])
        y = mm3(table("back_left"), split(q))
        g_re, g_im = y[:BOX, :128] - y[BOX:, 128:], y[:BOX, 128:] + y[BOX:, :128]
        dph[pl.ds(f, BOX, stride=GROUP), :] = of_frame(pre, f) * g_im - of_frame(pim, f) * g_re
        return carry

    lax.fori_loop(0, GROUP, back, 0)

    def project(g, total):
        tiles = [jnp.zeros((8, 128), f32) for _ in range(9)]
        for r, (tile, off) in enumerate(starts):
            x = dph[pl.ds(pl.multiple_of(g * 64, 64) + 8 * r, 8), :]
            if off:
                x = pltpu.roll(x, off, 1)
            if off + BOX > 128:
                tiles[tile + 1] += jnp.where(lane < off, x, 0.0)
                x = jnp.where(lane < off, 0.0, x)
            tiles[tile] += x
        x = jnp.concatenate(split(lanes(*tiles)))
        modes = base3[0 : 2 * MODES, pl.ds(pl.multiple_of(g * PERIOD, 128), PERIOD)]
        return total + lax.dot_general(x, modes, (((1,), (1,)), ((), ())), preferred_element_type=f32)

    total = lax.fori_loop(0, BOX // 8, project, jnp.zeros((16, 128), f32))
    total = total[:8] + total[8:]
    gradient = total + pltpu.roll(total, MODES, 1)

    grad_send[...] = gradient
    for d in range(1, DEPTH):
        t = lax.rem(z + d, DEPTH)
        c = remote(grad_send, grad_recv.at[z], grad_ss.at[t], grad_rs.at[z], at(me, t))
        c.start()
        sends.append(c)
    grad_recv[z] = gradient
    for d in range(1, DEPTH):
        j = lax.rem(z + DEPTH - d, DEPTH)
        remote(grad_send, grad_recv.at[j], grad_ss.at[j], grad_rs.at[j], at(me, j)).wait_recv()
    mean = jnp.sum(grad_recv[...].reshape(64, 128), axis=0, keepdims=True) * (1.0 / FRAMES)
    gradient = gradient - mean
    for j in range(GROUP):
        ret_send[8 * j : 8 * j + 8, :] = jnp.broadcast_to(gradient[j : j + 1], (8, 128))
    for d in range(1, GROUP):
        t = lax.rem(me + d, GROUP)
        c = remote(rows8(ret_send, t), rows8(ret_recv, me), ret_ss.at[t], ret_rs.at[me], at(t, z))
        c.start()
        sends.append(c)
    ret_recv[pl.ds(pl.multiple_of(me * 8, 8), 8), :] = ret_send[pl.ds(pl.multiple_of(me * 8, 8), 8), :]

    for d in range(1, GROUP):
        j = lax.rem(me + GROUP - d, GROUP)
        remote(out_send.at[j], out_recv.at[j], out_ss.at[j], out_rs.at[j], at(j, z)).wait_recv()
    for p in range(GROUP):
        object_out[p] = out_recv[p, 0:2, :SHARE]
    for d in range(1, GROUP):
        j = lax.rem(me + GROUP - d, GROUP)
        remote(rows8(ret_send, j), rows8(ret_recv, j), ret_ss.at[j], ret_rs.at[j], at(j, z)).wait_recv()
    gradient_out[0] = ret_recv[pl.ds(0, GROUP, stride=8), :][:, :MODES]
    for c in sends:
        c.wait_send()


def body(sky_image, coefficients, mode_basis, aperture):
    window = np.broadcast_to((profile() / SIDE).astype(np.float32)[:, None], (SIDE, 128))
    vmem, dma = pltpu.VMEM, pltpu.SemaphoreType.DMA
    scratch = [
        vmem(TABLE.shape, bf16), vmem((SIDE, 128), f32), vmem((640, 256), f32), vmem((GROUP, MODES), f32),
        vmem((64, 128), f32), vmem((64, 128), f32), vmem((SIDE, SIDE), jnp.int32), vmem((MODES, FLAT), f32),
        vmem((3 * MODES, FLAT), bf16),
        vmem((4, 8, 640), f32), vmem((GROUP, SIDE, 128), f32), vmem((GROUP, 2, 8, 256), f32),
        vmem((GROUP, SIDE, 128), f32), vmem((8 * BOX, 128), f32), vmem((8 * BOX, 128), f32),
        vmem((GROUP, SIDE, 256), f32), vmem((GROUP, SIDE, 256), f32),
        *[vmem((GROUP, SIDE, 128), f32)] * 4,
        vmem((3 * SIDE, 128), f32), vmem((DEPTH, 56, 128), f32), vmem((DEPTH, 56, 128), f32), vmem((56, 128), f32),
        vmem((40, 128), f32), vmem((DEPTH, 40, 128), f32), vmem((SIDE, 128), f32), vmem((SIDE, 128), f32),
        vmem((8 * BOX, 128), f32), vmem((4, SIDE, 128), f32), vmem((GROUP, 8, 384), f32), vmem((GROUP, 8, 384), f32),
        vmem((8, 128), f32), vmem((DEPTH, 8, 128), f32), vmem((64, 128), f32), vmem((64, 128), f32),
        *[dma((8,))] * 19,
    ]
    return pl.pallas_call(
        kernel,
        out_shape=(
            jax.ShapeDtypeStruct((1, GROUP, MODES), f32),
            jax.ShapeDtypeStruct((GROUP, 2, SHARE), f32),
        ),
        in_specs=[pl.BlockSpec(memory_space=pl.ANY)] * 6,
        out_specs=[pl.BlockSpec(memory_space=pltpu.VMEM)] * 2,
        scratch_shapes=scratch,
        compiler_params=pltpu.CompilerParams(collective_id=0, has_side_effects=True, vmem_limit_bytes=60 * 2**20),
    )(sky_image, coefficients, mode_basis, aperture, jnp.asarray(TABLE), jnp.asarray(window))


def solution(mesh):
    in_specs = (P("frame", None, "patch"), P("frame", "patch", None), P(), P())
    out_specs = (P("frame", "patch", None), P("patch", None, "frame"))
    return jax.shard_map(body, mesh=mesh, in_specs=in_specs, out_specs=out_specs, check_vma=False)
```

```python
import math

import jax
import jax.numpy as jnp
import ml_dtypes
import numpy as np
from jax import lax
from jax.experimental import pallas as pl
from jax.experimental.pallas import tpu as pltpu
from jax.sharding import PartitionSpec as P

SIDE = 144
RIM = 8
TILE = SIDE - 2 * RIM
LOW, BOX = 32, 80
GROUP = 8
DEPTH = 8
STRIPS = 4
FRAMES = GROUP * DEPTH
HALF = SIDE // 2 + 1
CHUNK = BOX // DEPTH
MAIN, REST = 64, HALF - 64
REST_ROWS = 40
REST_CHUNK = REST_ROWS // DEPTH
SUMS = 3 * CHUNK + REST_CHUNK
OBJECTS = 2 * CHUNK + REST_CHUNK
FLAT = BOX * SIDE
PERIOD = 8 * SIDE
MODES = 64
UNROLL = 2
SHARE = SIDE * SIDE // FRAMES
DAMPING = 0.02 * FRAMES
MESH = pl.DeviceIdType.MESH
f32, bf16 = jnp.float32, jnp.bfloat16


def profile():
    at = np.arange(SIDE, dtype=np.float64)
    distance = np.minimum(at, SIDE - 1 - at)
    taper = 0.3 + 0.7 * np.sin(math.pi * (distance + 1.0) / (2.0 * (RIM + 1))) ** 2
    return np.where(distance < RIM, taper, 1.0)


def tables():
    k = np.arange(HALF)
    y = np.arange(SIDE)
    u = np.arange(BOX) + LOW - SIDE // 2
    weight = np.ones(HALF)
    weight[0] = weight[-1] = 0.5

    def pair(a, b):
        angle = 2.0 * math.pi / SIDE * (np.outer(a, b) % SIDE)
        return np.cos(angle), np.sin(angle)

    def beside(c, s):
        t = np.zeros((-(-c.shape[0] // 16) * 16, 256))
        t[: c.shape[0], : c.shape[1]], t[: c.shape[0], 128 : 128 + c.shape[1]] = c, s
        return t

    def below(c, s):
        t = np.zeros((2 * BOX, 256))
        t[:HALF, : c.shape[1]], t[BOX : BOX + HALF, : c.shape[1]] = c, s
        return t

    parts = {}
    c, s = pair(k, u)
    parts["pupil_rows"] = below(c, s)
    parts["pupil_columns"] = beside(c.T, s.T)
    parts["back_columns"] = beside(weight[:, None] * c, weight[:, None] * s)
    parts["back_rows"] = beside(c.T * weight, s.T * weight)
    c, s = pair(k, k)
    parts["focal_columns"] = beside(weight[:, None] * c, -weight[:, None] * s)
    parts["focal_rows"] = beside(c * weight, s * weight)
    w = profile()
    c, s = pair(k, y)
    parts["data_rows"] = below(c * w / SIDE, s * w / SIDE)
    order = np.concatenate([y[RIM:-RIM], y[:RIM], y[-RIM:]])
    parts["data_columns"] = beside((w[:, None] * c.T)[order], -(w[:, None] * s.T)[order])
    first, rows, total = {}, [], 0
    for name, part in parts.items():
        first[name] = (total, part.shape[0])
        total += part.shape[0]
        rows.append(part)
    whole = np.concatenate(rows)
    high = whole.astype(ml_dtypes.bfloat16)
    rest = (whole - high.astype(np.float64)).astype(ml_dtypes.bfloat16)
    return np.stack([high, rest]), first


TABLE, FIRST = tables()


def split(x):
    high = x.astype(bf16)
    return high, (x - high.astype(f32)).astype(bf16)


def mm(a, b):
    return jnp.dot(a, b, preferred_element_type=f32)


def mm3(a, b):
    return mm(a[0], b[0]) + (mm(a[0], b[1]) + mm(a[1], b[0]))


def lanes(*parts):
    return jnp.concatenate(parts, axis=1)


def sine_cosine(x):
    quarter = jnp.floor(x * (2.0 / math.pi) + 0.5)
    r = x - quarter * 1.5703125
    r = r - quarter * 4.837512969970703125e-4
    r = r - quarter * 7.54978995489188216e-8
    z = r * r
    sine = ((-1.9515295891e-4 * z + 8.3321608736e-3) * z - 1.6666654611e-1) * z * r + r
    cosine = ((2.443315711809948e-5 * z - 1.388731625493765e-3) * z + 4.166664568298827e-2) * z * z - 0.5 * z + 1.0
    halves = jnp.floor(quarter * 0.5)
    odd = quarter - 2.0 * halves
    minus = 1.0 - 2.0 * (halves - 2.0 * jnp.floor(halves * 0.5))
    swap = odd > 0.5
    return (
        jnp.where(swap, cosine, sine) * minus,
        jnp.where(swap, -sine, cosine) * minus,
    )


def kernel(
    sky, coef, basis, aperture, table_hbm,
    gradient_out, object_out,
    tab, skyp, coef_v, coef_send, coef_recv, mask_v, base, base3,
    edges, img, halo, turned, pre, pim, fpr, fpi, fmr, fmi, tre, tim, dre, dim_,
    sums, packed, sum_send, sum_recv, sum_v, obj_send, obj_all, ore, oim, dph,
    full, out_send, out_recv, grad_send, grad_recv, ret_send, ret_recv,
    local_sem, coef_ss, coef_rs, img_ss, img_rs, own_ss, own_rs, cross_ss, cross_rs,
    sum_ss, sum_rs, obj_ss, obj_rs, out_ss, out_rs, grad_ss, grad_rs, ret_ss, ret_rs,
):
    place, strip = lax.axis_index("frame"), lax.axis_index("patch")
    me, z = place // DEPTH, place % DEPTH

    def at(group, depth, which=None):
        return {"frame": group * DEPTH + depth, "patch": strip if which is None else which}

    def remote(src, dst, send, recv, device):
        return pltpu.make_async_remote_copy(
            src_ref=src, dst_ref=dst, send_sem=send, recv_sem=recv, device_id=device, device_id_type=MESH
        )

    def table(name, start, width):
        row, count = FIRST[name]
        return tuple(tab[n, row : row + count, start : start + width] for n in range(2))

    loads = [
        pltpu.make_async_copy(coef.at[0], coef_v, local_sem.at[0]),
        pltpu.make_async_copy(basis.at[:, pl.ds(LOW * SIDE, FLAT)], base, local_sem.at[1]),
        pltpu.make_async_copy(sky.at[0], skyp.at[pl.ds(RIM, 512)], local_sem.at[2]),
        pltpu.make_async_copy(table_hbm, tab, local_sem.at[3]),
        pltpu.make_async_copy(aperture, mask_v, local_sem.at[4]),
    ]
    for load in loads:
        load.start()

    barrier = pltpu.get_barrier_semaphore()
    beside = lax.rem(strip + jnp.where(me < 4, STRIPS - 1, 1), STRIPS)

    def greet(device):
        pl.semaphore_signal(barrier, inc=1, device_id=device, device_id_type=MESH)

    for d in range(1, GROUP):
        greet(at(lax.rem(me + d, GROUP), z))
    for d in range(1, DEPTH):
        greet(at(me, lax.rem(z + d, DEPTH)))
    for j in range(GROUP):
        greet(at(j, z, beside))

    skyp[pl.ds(0, RIM), :] = jnp.zeros((RIM, 256), f32)
    skyp[pl.ds(512 + RIM, 120), :] = jnp.zeros((120, 256), f32)
    loads[0].wait()
    for p in range(GROUP):
        row = jnp.broadcast_to(coef_v[p : p + 1, :], (8, MODES))
        coef_send[p * 8 : p * 8 + 8, :] = lanes(row, row)
    loads[2].wait()
    for half in range(2):
        strip_t = skyp[:, half * 128 : half * 128 + 128].T
        edges[2 * half] = strip_t[:8]
        edges[2 * half + 1] = strip_t[120:]
    pl.semaphore_wait(barrier, GROUP - 1 + DEPTH - 1 + GROUP)

    sends = []
    def rows8(ref, j):
        return ref.at[pl.ds(pl.multiple_of(j * 8, 8), 8)]

    for d in range(1, GROUP):
        t = lax.rem(me + d, GROUP)
        c = remote(rows8(coef_send, t), rows8(coef_recv, me), coef_ss.at[t], coef_rs.at[me], at(t, z))
        c.start()
        sends.append(c)
    coef_recv[pl.ds(pl.multiple_of(me * 8, 8), 8), :] = coef_send[pl.ds(pl.multiple_of(me * 8, 8), 8), :]

    def main_of(t):
        return skyp.at[
            pl.ds(pl.multiple_of(lax.rem(t, 4) * TILE, TILE), SIDE), pl.ds(pl.multiple_of((t // 4) * 128, 128), 128)
        ]

    def edge_of(kind, t):
        return edges.at[kind, :, pl.ds(pl.multiple_of(lax.rem(t, 4) * TILE, TILE), 256)]

    for d in range(1, GROUP):
        t = lax.rem(me + d, GROUP)
        c = remote(main_of(t), img.at[me], img_ss.at[t], img_rs.at[me], at(t, z))
        c.start()
        sends.append(c)
        kind, side = jnp.where(t < 4, 2, 1), jnp.where(t < 4, 1, 0)
        c = remote(edge_of(kind, t), halo.at[me, side], own_ss.at[t], own_rs.at[me], at(t, z))
        c.start()
        sends.append(c)
    for p in range(GROUP):
        kind, side, step = (3, 0, 1) if p < 4 else (0, 1, STRIPS - 1)
        c = remote(
            edge_of(kind, p), halo.at[me, side], cross_ss.at[p], cross_rs.at[me],
            at(p, z, lax.rem(strip + step, STRIPS)),
        )
        c.start()
        sends.append(c)
    own_side = jnp.where(me < 4, 1, 0)
    mine = [
        pltpu.make_async_copy(main_of(me), img.at[me], local_sem.at[6]),
        pltpu.make_async_copy(edge_of(jnp.where(me < 4, 2, 1), me), halo.at[me, own_side], local_sem.at[7]),
    ]
    for c in mine:
        c.start()

    loads[1].wait()

    def cut(g, carry):
        at_g = pl.ds(pl.multiple_of(g * PERIOD, 128), PERIOD)
        x = base[:, at_g]
        h, r = split(x)
        base3[0:MODES, at_g] = h
        base3[MODES : 2 * MODES, at_g] = r
        base3[2 * MODES :, at_g] = (x - h.astype(f32) - r.astype(f32)).astype(bf16)
        return carry

    lax.fori_loop(0, BOX // 8, cut, 0)
    for load in loads[3:]:
        load.wait()

    lane = lax.broadcasted_iota(jnp.int32, (8, 128), 1)
    mask = mask_v[LOW : LOW + BOX, 0:128].astype(f32)
    mask = pltpu.roll(mask, 128 - LOW, 1)
    mask = jnp.where(lax.broadcasted_iota(jnp.int32, (BOX, 128), 1) < BOX, mask, 0.0)
    area = jnp.sum(mask)
    intensity_scale = 1.0 / (SIDE * SIDE * area)
    dph[0:BOX, :] = mask

    for d in range(1, GROUP):
        j = lax.rem(me + GROUP - d, GROUP)
        remote(rows8(coef_send, j), rows8(coef_recv, j), coef_ss.at[j], coef_rs.at[j], at(j, z)).wait_recv()
    weights = coef_recv[pl.ds(0, GROUP, stride=8), :]
    w0 = weights.astype(bf16).astype(f32)
    w1 = (weights - w0).astype(bf16).astype(f32)
    w2 = weights - w0 - w1
    weights = jnp.concatenate([lanes(w, w[:, :MODES]) for w in (w0, w1, w2)]).astype(bf16)

    starts = [divmod(SIDE * r + LOW, 128) for r in range(8)]

    def pupils(g, carry):
        ph = mm(weights, base3[:, pl.ds(pl.multiple_of(g * PERIOD, 128), PERIOD)])
        ph = ph[0:8] + (ph[8:16] + ph[16:24])
        rows = []
        for tile, off in starts:
            x = ph[:, tile * 128 : tile * 128 + 128]
            if off:
                x = pltpu.roll(x, 128 - off, 1)
            if off + BOX > 128:
                y = pltpu.roll(ph[:, tile * 128 + 128 : tile * 128 + 256], 128 - off, 1)
                x = jnp.where(lane < 128 - off, x, y)
            rows.append(x)
        m = dph[pl.ds(pl.multiple_of(g * 8, 8), 8), :]
        m = jnp.concatenate([jnp.broadcast_to(m[r : r + 1], (8, 128)) for r in range(8)])
        sine, cosine = sine_cosine(jnp.concatenate(rows))
        at_g = pl.ds(pl.multiple_of(g * 64, 64), 64)
        pre[at_g, :] = m * cosine
        pim[at_g, :] = m * sine
        return carry

    lax.fori_loop(0, BOX // 8, pupils, 0)

    def of_frame(ref, f):
        return ref[pl.ds(f, BOX, stride=GROUP), :]

    def fold(x):
        return x[:BOX] + x[BOX:], x[:BOX] - x[BOX:]

    def both(x):
        h, r = split(x)
        return h[:, :BOX], r[:, :BOX]

    def stack(*parts):
        return jnp.concatenate(parts)

    def transfers(n, carry):
        fs = [n * UNROLL + m for m in range(UNROLL)]
        rows = []
        for f in fs:
            y = mm3(table("pupil_rows", 0, BOX), split(lanes(of_frame(pre, f), of_frame(pim, f))))
            cr, ci, sr, si = y[:BOX, :128], y[:BOX, 128:], y[BOX:, :128], y[BOX:, 128:]
            rows += [cr + si, cr - si, ci - sr, ci + sr]
        y = mm3(both(stack(*rows)), table("pupil_columns", 0, 256))
        even, odd = [], []
        for m, f in enumerate(fs):
            r, i = y[4 * m * BOX : (4 * m + 2) * BOX], y[(4 * m + 2) * BOX : (4 * m + 4) * BOX]
            p_re, p_im = r[:, :128] + i[:, 128:], i[:, :128] - r[:, 128:]
            m_re, m_im = r[:, :128] - i[:, 128:], i[:, :128] + r[:, 128:]
            fpr[f], fpi[f], fmr[f], fmi[f] = p_re, p_im, m_re, m_im
            plus = (p_re * p_re + p_im * p_im) * intensity_scale
            minus = (m_re * m_re + m_im * m_im) * intensity_scale
            even += fold(plus + minus)
            odd += fold(plus - minus)
        x_re = mm3(both(stack(*even)), table("focal_columns", 0, 128))
        x_im = mm3(both(stack(*odd)), table("focal_columns", 128, 128))
        for m, f in enumerate(fs):
            x = lanes(x_re[2 * m * BOX : 2 * (m + 1) * BOX], x_im[2 * m * BOX : 2 * (m + 1) * BOX])
            c = mm3(table("focal_rows", 0, BOX), split(x[:BOX]))
            s = mm3(table("focal_rows", 128, BOX), split(x[BOX:]))
            cr, ci, sr, si = c[:, :128], c[:, 128:], s[:, :128], s[:, 128:]
            tre[f] = stack(cr + si, cr - si)
            tim[f] = stack(ci - sr, ci + sr)
        return carry

    lax.fori_loop(0, GROUP // UNROLL, transfers, 0)

    for c in mine:
        c.wait()
    for j in range(GROUP):
        remote(edge_of(0, 0), halo.at[j, 1 - own_side], cross_ss.at[j], cross_rs.at[j], at(j, z, beside)).wait_recv()
    for d in range(1, GROUP):
        j = lax.rem(me + GROUP - d, GROUP)
        remote(main_of(j), img.at[j], img_ss.at[j], img_rs.at[j], at(j, z)).wait_recv()
        remote(edge_of(0, j), halo.at[j, own_side], own_ss.at[j], own_rs.at[j], at(j, z)).wait_recv()
    row = lax.broadcasted_iota(jnp.int32, (128, 256), 0)
    left_on = jnp.where(jnp.logical_and(strip == 0, me < 4), 0.0, 1.0)
    right_on = jnp.where(jnp.logical_and(strip == STRIPS - 1, me >= 4), 0.0, 1.0)
    rims = halo[...].reshape(128, 256) * jnp.where(lax.rem(row, 16) < 8, left_on, right_on)
    rims = rims.T[:SIDE]
    for f in range(GROUP):
        turned[f] = pltpu.roll(rims, (128 - 16 * f) % 128, 1) if f else rims

    sums[...] = jnp.zeros_like(sums)

    def data(n, carry):
        fs = [n * UNROLL + m for m in range(UNROLL)]
        h, r = split(stack(*[lanes(img[f], turned[f]) for f in fs]))
        x = mm3((h[:, :SIDE], r[:, :SIDE]), table("data_columns", 0, 256))
        n_re, n_im, power = sums[0], sums[1], sums[2]
        for m, f in enumerate(fs):
            y = mm3(table("data_rows", 0, SIDE), split(x[m * SIDE : (m + 1) * SIDE]))
            cr, ci, sr, si = y[:BOX, :128], y[:BOX, 128:], y[BOX:, :128], y[BOX:, 128:]
            d_re, d_im = stack(cr + si, cr - si), stack(ci - sr, ci + sr)
            dre[f] = d_re
            dim_[f] = d_im
            t_re, t_im = tre[f], tim[f]
            n_re = n_re + (t_re * d_re + t_im * d_im)
            n_im = n_im + (t_re * d_im - t_im * d_re)
            power = power + (t_re * t_re + t_im * t_im)
        sums[0], sums[1], sums[2] = n_re, n_im, power
        return carry

    lax.fori_loop(0, GROUP // UNROLL, data, 0)

    lane80 = lax.broadcasted_iota(jnp.int32, (BOX, 128), 1)
    lane40 = lax.broadcasted_iota(jnp.int32, (REST_ROWS, 128), 1)
    rest = jnp.zeros((REST_ROWS, 128), f32)
    for part in range(3):
        plus, minus = sums[part, :BOX], sums[part, BOX:]
        packed[part * BOX : (part + 1) * BOX, :] = jnp.where(lane80 < MAIN, plus, pltpu.roll(minus, MAIN, 1))
        for sign, x in enumerate((plus, minus)):
            j = (2 * part + sign) * REST
            x = pltpu.roll(x[:REST_ROWS], (j - MAIN) % 128, 1)
            rest = jnp.where(jnp.logical_and(lane40 >= j, lane40 < j + REST), x, rest)
    packed[3 * BOX :, :] = rest
    for d in range(DEPTH):
        for part in range(3):
            sum_send[d, part * CHUNK : (part + 1) * CHUNK, :] = packed[
                part * BOX + d * CHUNK : part * BOX + (d + 1) * CHUNK, :
            ]
        sum_send[d, 3 * CHUNK :, :] = packed[3 * BOX + d * REST_CHUNK : 3 * BOX + (d + 1) * REST_CHUNK, :]
    for d in range(1, DEPTH):
        t = lax.rem(z + d, DEPTH)
        c = remote(sum_send.at[t], sum_recv.at[z], sum_ss.at[t], sum_rs.at[z], at(me, t))
        c.start()
        sends.append(c)
    sum_recv[z] = sum_send[z]
    for d in range(1, DEPTH):
        j = lax.rem(z + DEPTH - d, DEPTH)
        remote(sum_send.at[j], sum_recv.at[j], sum_ss.at[j], sum_rs.at[j], at(me, j)).wait_recv()
    total = sum_recv[0]
    for j in range(1, DEPTH):
        total = total + sum_recv[j]
    sum_v[...] = total
    power = sum_v[2 * CHUNK : 3 * CHUNK, :] + DAMPING
    obj_send[0:CHUNK, :] = sum_v[0:CHUNK, :] / power
    obj_send[CHUNK : 2 * CHUNK, :] = sum_v[CHUNK : 2 * CHUNK, :] / power
    rest = sum_v[3 * CHUNK :, :]
    lane5 = lax.broadcasted_iota(jnp.int32, (REST_CHUNK, 128), 1)
    power = jnp.where(lane5 < 2 * REST, pltpu.roll(rest, 128 - 4 * REST, 1), pltpu.roll(rest, 128 - 2 * REST, 1))
    power = jnp.where(lane5 < 4 * REST, power, 0.0) + DAMPING
    obj_send[2 * CHUNK :, :] = rest / power
    for d in range(1, DEPTH):
        t = lax.rem(z + d, DEPTH)
        c = remote(obj_send, obj_all.at[z], obj_ss.at[t], obj_rs.at[z], at(me, t))
        c.start()
        sends.append(c)
    obj_all[z] = obj_send[...]
    for d in range(1, DEPTH):
        j = lax.rem(z + DEPTH - d, DEPTH)
        remote(obj_send, obj_all.at[j], obj_ss.at[j], obj_rs.at[j], at(me, j)).wait_recv()
    for d in range(DEPTH):
        for part in range(2):
            packed[part * BOX + d * CHUNK : part * BOX + (d + 1) * CHUNK, :] = obj_all[
                d, part * CHUNK : (part + 1) * CHUNK, :
            ]
        packed[3 * BOX + d * REST_CHUNK : 3 * BOX + (d + 1) * REST_CHUNK, :] = obj_all[d, 2 * CHUNK :, :]
    rest = packed[3 * BOX :, :]
    for part, ref in enumerate((ore, oim)):
        main = packed[part * BOX : (part + 1) * BOX, :]
        for sign in range(2):
            j = (2 * part + sign) * REST
            x = stack(pltpu.roll(rest, (MAIN - j) % 128, 1), jnp.zeros((BOX - REST_ROWS, 128), f32))
            x = jnp.where(lane80 < HALF, x, 0.0)
            ref[sign * BOX : (sign + 1) * BOX, :] = jnp.where(
                lane80 < MAIN, pltpu.roll(main, MAIN, 1) if sign else main, x
            )

    r_at = lax.broadcasted_iota(jnp.int32, (2 * SIDE, 2 * BOX), 0)
    c_at = lax.broadcasted_iota(jnp.int32, (2 * SIDE, 2 * BOX), 1)
    mirrored = r_at >= SIDE
    k = jnp.where(mirrored, r_at - SIDE, r_at)
    minus = (k >= HALF) != mirrored
    k = jnp.where(k >= HALF, SIDE - k, k) + jnp.where(minus, BOX, 0)
    pick_rows = jnp.where(k == c_at, 1.0, 0.0).astype(bf16)
    r_at = lax.broadcasted_iota(jnp.int32, (128, 256), 0)
    c_at = lax.broadcasted_iota(jnp.int32, (128, 256), 1)
    flip_columns = jnp.where(
        jnp.logical_and(r_at + c_at == SIDE, jnp.logical_and(c_at >= HALF, c_at < SIDE)), 1.0, 0.0
    ).astype(bf16)
    parts = [mm(pick_rows, part) for part in split(lanes(ore[...], oim[...]))]
    lane_full = lax.broadcasted_iota(jnp.int32, (SIDE, 128), 1)
    for n, sign in ((0, 1.0), (1, -1.0)):
        at_n = slice(n * 128, n * 128 + 128)
        half = parts[0][:SIDE, at_n] + parts[1][:SIDE, at_n]
        mirror = [mm(part[SIDE:, at_n].astype(bf16), flip_columns) for part in parts]
        mirror = sign * (mirror[0] + mirror[1])
        full[2 * n] = jnp.where(lane_full < HALF, half, mirror[:, :128])
        full[2 * n + 1] = mirror[:, 128:]
    first_row = z * 9 // 4
    for n in range(2):
        placed = [jnp.zeros((8, 128), f32) for _ in range(6)]
        for t in range(3):
            for piece in range(2):
                x = full[2 * n + piece, pl.ds(first_row + t, GROUP, stride=SIDE // GROUP), :]
                tile, off = divmod(SIDE * t + 128 * piece, 128)
                if off:
                    x = pltpu.roll(x, off, 1)
                    placed[tile + 1] += jnp.where(lane < off, x, 0.0)
                    x = jnp.where(lane < off, 0.0, x)
                placed[tile] += x
        placed = lanes(*placed)
        picked = jnp.zeros((8, 384), f32)
        for m in range(4):
            moved = pltpu.roll(placed, 768 - 36 * m, 1) if m else placed
            picked = picked + jnp.where(lax.rem(z, 4) == m, 1.0, 0.0) * moved[:, :384]
        for i in range(GROUP):
            out_send[i, n : n + 1, :] = picked[i : i + 1]
    for d in range(1, GROUP):
        t = lax.rem(me + d, GROUP)
        c = remote(out_send.at[t], out_recv.at[me], out_ss.at[t], out_rs.at[me], at(t, z))
        c.start()
        sends.append(c)
    out_recv[me] = out_send[me]

    scale = 2.0 / (SIDE * SIDE)

    def back(n, carry):
        fs = [n * UNROLL + m for m in range(UNROLL)]
        o_re, o_im = ore[...], oim[...]
        h_re, h_im = [], []
        for f in fs:
            t_re, t_im = tre[f], tim[f]
            e_re = dre[f] - (o_re * t_re - o_im * t_im)
            e_im = dim_[f] - (o_re * t_im + o_im * t_re)
            re_even, re_odd = fold(-scale * (e_re * o_re + e_im * o_im))
            im_even, im_odd = fold(scale * (e_re * o_im - e_im * o_re))
            c = mm3(table("focal_rows", 0, BOX), split(lanes(re_even, im_even)))
            s = mm3(table("focal_rows", 128, BOX), split(lanes(re_odd, im_odd)))
            cr, ci, sr, si = c[:, :128], c[:, 128:], s[:, :128], s[:, 128:]
            h_re += [cr - si, cr + si]
            h_im += [ci + sr, ci - sr]
        even = mm3(both(stack(*h_re)), table("focal_columns", 0, 128)) * (4.0 * intensity_scale)
        odd = mm3(both(stack(*h_im)), table("focal_columns", 128, 128)) * (4.0 * intensity_scale)
        sum_rows, gap_rows = [], []
        for m, f in enumerate(fs):
            at_m = slice(2 * m * BOX, 2 * (m + 1) * BOX)
            plus, minus = even[at_m] + odd[at_m], even[at_m] - odd[at_m]
            p_re, p_im, m_re, m_im = plus * fpr[f], plus * fpi[f], minus * fmr[f], minus * fmi[f]
            sum_rows += [p_re + m_re, p_im + m_im]
            gap_rows += [p_re - m_re, p_im - m_im]
        qc = mm3(both(stack(*sum_rows)), table("back_columns", 0, 128))
        qs = mm3(both(stack(*gap_rows)), table("back_columns", 128, 128))
        for m, f in enumerate(fs):
            at_re, at_im = slice(4 * m * BOX, (4 * m + 2) * BOX), slice((4 * m + 2) * BOX, (4 * m + 4) * BOX)
            re_even, re_odd = fold(qc[at_re] - qs[at_im])
            im_even, im_odd = fold(qc[at_im] + qs[at_re])
            c = mm3(table("back_rows", 0, BOX), split(lanes(re_even, im_even)))
            s = mm3(table("back_rows", 128, BOX), split(lanes(re_odd, im_odd)))
            g_re, g_im = c[:, :128] - s[:, 128:], c[:, 128:] + s[:, :128]
            dph[pl.ds(f, BOX, stride=GROUP), :] = of_frame(pre, f) * g_im - of_frame(pim, f) * g_re
        return carry

    lax.fori_loop(0, GROUP // UNROLL, back, 0)

    def project(g, total):
        tiles = [jnp.zeros((8, 128), f32) for _ in range(9)]
        for r, (tile, off) in enumerate(starts):
            x = dph[pl.ds(pl.multiple_of(g * 64, 64) + 8 * r, 8), :]
            if off:
                x = pltpu.roll(x, off, 1)
            if off + BOX > 128:
                tiles[tile + 1] += jnp.where(lane < off, x, 0.0)
                x = jnp.where(lane < off, 0.0, x)
            tiles[tile] += x
        x = jnp.concatenate(split(lanes(*tiles)))
        modes = base3[0 : 2 * MODES, pl.ds(pl.multiple_of(g * PERIOD, 128), PERIOD)]
        return total + lax.dot_general(x, modes, (((1,), (1,)), ((), ())), preferred_element_type=f32)

    total = lax.fori_loop(0, BOX // 8, project, jnp.zeros((16, 128), f32))
    total = total[:8] + total[8:]
    gradient = total + pltpu.roll(total, MODES, 1)

    grad_send[...] = gradient
    for d in range(1, DEPTH):
        t = lax.rem(z + d, DEPTH)
        c = remote(grad_send, grad_recv.at[z], grad_ss.at[t], grad_rs.at[z], at(me, t))
        c.start()
        sends.append(c)
    grad_recv[z] = gradient
    for d in range(1, DEPTH):
        j = lax.rem(z + DEPTH - d, DEPTH)
        remote(grad_send, grad_recv.at[j], grad_ss.at[j], grad_rs.at[j], at(me, j)).wait_recv()
    mean = jnp.sum(grad_recv[...].reshape(64, 128), axis=0, keepdims=True) * (1.0 / FRAMES)
    gradient = gradient - mean
    for j in range(GROUP):
        ret_send[8 * j : 8 * j + 8, :] = jnp.broadcast_to(gradient[j : j + 1], (8, 128))
    for d in range(1, GROUP):
        t = lax.rem(me + d, GROUP)
        c = remote(rows8(ret_send, t), rows8(ret_recv, me), ret_ss.at[t], ret_rs.at[me], at(t, z))
        c.start()
        sends.append(c)
    ret_recv[pl.ds(pl.multiple_of(me * 8, 8), 8), :] = ret_send[pl.ds(pl.multiple_of(me * 8, 8), 8), :]

    for d in range(1, GROUP):
        j = lax.rem(me + GROUP - d, GROUP)
        remote(out_send.at[j], out_recv.at[j], out_ss.at[j], out_rs.at[j], at(j, z)).wait_recv()
    for p in range(GROUP):
        object_out[p] = out_recv[p, 0:2, :SHARE]
    for d in range(1, GROUP):
        j = lax.rem(me + GROUP - d, GROUP)
        remote(rows8(ret_send, j), rows8(ret_recv, j), ret_ss.at[j], ret_rs.at[j], at(j, z)).wait_recv()
    gradient_out[0] = ret_recv[pl.ds(0, GROUP, stride=8), :][:, :MODES]
    for c in sends:
        c.wait_send()


def body(sky_image, coefficients, mode_basis, aperture):
    vmem, dma = pltpu.VMEM, pltpu.SemaphoreType.DMA
    scratch = [
        vmem(TABLE.shape, bf16), vmem((640, 256), f32), vmem((GROUP, MODES), f32),
        vmem((64, 128), f32), vmem((64, 128), f32), vmem((SIDE, SIDE), jnp.int32), vmem((MODES, FLAT), f32),
        vmem((3 * MODES, FLAT), bf16),
        vmem((4, 8, 640), f32), vmem((GROUP, SIDE, 128), f32), vmem((GROUP, 2, 8, 256), f32),
        vmem((GROUP, SIDE, 128), f32), vmem((8 * BOX, 128), f32), vmem((8 * BOX, 128), f32),
        *[vmem((GROUP, 2 * BOX, 128), f32)] * 8,
        vmem((3, 2 * BOX, 128), f32), vmem((3 * BOX + REST_ROWS, 128), f32),
        vmem((DEPTH, SUMS, 128), f32), vmem((DEPTH, SUMS, 128), f32), vmem((SUMS, 128), f32),
        vmem((OBJECTS, 128), f32), vmem((DEPTH, OBJECTS, 128), f32), vmem((2 * BOX, 128), f32), vmem((2 * BOX, 128), f32),
        vmem((8 * BOX, 128), f32), vmem((4, SIDE, 128), f32), vmem((GROUP, 8, 384), f32), vmem((GROUP, 8, 384), f32),
        vmem((8, 128), f32), vmem((DEPTH, 8, 128), f32), vmem((64, 128), f32), vmem((64, 128), f32),
        *[dma((8,))] * 19,
    ]
    return pl.pallas_call(
        kernel,
        out_shape=(
            jax.ShapeDtypeStruct((1, GROUP, MODES), f32),
            jax.ShapeDtypeStruct((GROUP, 2, SHARE), f32),
        ),
        in_specs=[pl.BlockSpec(memory_space=pl.ANY)] * 5,
        out_specs=[pl.BlockSpec(memory_space=pltpu.VMEM)] * 2,
        scratch_shapes=scratch,
        compiler_params=pltpu.CompilerParams(collective_id=0, has_side_effects=True, vmem_limit_bytes=60 * 2**20),
    )(sky_image, coefficients, mode_basis, aperture, jnp.asarray(TABLE))


def solution(mesh):
    in_specs = (P("frame", None, "patch"), P("frame", "patch", None), P(), P())
    out_specs = (P("frame", "patch", None), P("patch", None, "frame"))
    return jax.shard_map(body, mesh=mesh, in_specs=in_specs, out_specs=out_specs, check_vma=False)
```

```python
import math

import jax
import jax.numpy as jnp
import ml_dtypes
import numpy as np
from jax import lax
from jax.experimental import pallas as pl
from jax.experimental.pallas import tpu as pltpu
from jax.sharding import PartitionSpec as P

SIDE = 144
RIM = 8
TILE = SIDE - 2 * RIM
LOW, BOX = 32, 80
GROUP = 8
DEPTH = 8
STRIPS = 4
FRAMES = GROUP * DEPTH
HALF = SIDE // 2 + 1
CHUNK = BOX // DEPTH
MAIN, REST = 64, HALF - 64
REST_ROWS = 40
REST_CHUNK = REST_ROWS // DEPTH
SUMS = 3 * CHUNK + REST_CHUNK
OBJECTS = 2 * CHUNK + REST_CHUNK
FLAT = BOX * SIDE
PERIOD = 8 * SIDE
MODES = 64
UNROLL = GROUP
SHARE = SIDE * SIDE // FRAMES
DAMPING = 0.02 * FRAMES
MESH = pl.DeviceIdType.MESH
f32, bf16 = jnp.float32, jnp.bfloat16


def profile():
    at = np.arange(SIDE, dtype=np.float64)
    distance = np.minimum(at, SIDE - 1 - at)
    taper = 0.3 + 0.7 * np.sin(math.pi * (distance + 1.0) / (2.0 * (RIM + 1))) ** 2
    return np.where(distance < RIM, taper, 1.0)


def tables():
    k = np.arange(HALF)
    y = np.arange(SIDE)
    u = np.arange(BOX) + LOW - SIDE // 2
    weight = np.ones(HALF)
    weight[0] = weight[-1] = 0.5

    def pair(a, b):
        angle = 2.0 * math.pi / SIDE * (np.outer(a, b) % SIDE)
        return np.cos(angle), np.sin(angle)

    def cut(t):
        high = t.astype(ml_dtypes.bfloat16)
        return high, (t - high.astype(np.float64)).astype(ml_dtypes.bfloat16)

    def rows_of(*blocks):
        t = np.zeros((BOX * len(blocks), blocks[0].shape[1]))
        for n, block in enumerate(blocks):
            t[n * BOX : n * BOX + block.shape[0]] = block
        high, low = cut(t)
        return np.concatenate([high, high, low], axis=1)

    def columns_of(c, s):
        t = np.zeros((-(-c.shape[0] // 16) * 16, 256))
        t[: c.shape[0], : c.shape[1]], t[: c.shape[0], 128 : 128 + c.shape[1]] = c, s
        return cut(t)

    def twice(c, s):
        high, low = columns_of(c, s)
        return np.concatenate([high, np.zeros((128 - BOX, 256), high.dtype), high]), low

    parts = {}
    c, s = pair(k, u)
    parts["pupil_rows"] = rows_of(c, s)
    parts["pupil_columns"], parts["pupil_columns_low"] = twice(c.T, s.T)
    parts["back_columns"], parts["back_columns_low"] = twice(weight[:, None] * c, weight[:, None] * s)

    def wide(t):
        return np.pad(t, ((0, BOX - t.shape[0]), (0, BOX - t.shape[1])))

    parts["back_even"], parts["back_odd"] = rows_of(wide(c.T * weight)), rows_of(wide(s.T * weight))
    c, s = pair(k, k)
    parts["focal_columns"], parts["focal_columns_low"] = twice(weight[:, None] * c, -weight[:, None] * s)
    parts["focal_even"], parts["focal_odd"] = rows_of(wide(c * weight)), rows_of(wide(s * weight))
    w = profile()
    c, s = pair(k, y)
    t = rows_of(c * w / SIDE, s * w / SIDE)
    parts["data_rows"], parts["data_rows_end"] = t[:, :256], t[:, 256:]
    order = np.concatenate([y[RIM:-RIM], y[:RIM], y[-RIM:]])
    parts["data_columns"], parts["data_columns_low"] = columns_of(
        (w[:, None] * c.T)[order], -(w[:, None] * s.T)[order]
    )
    first, rows, total = {}, [], 0
    for name, part in parts.items():
        first[name] = (total, *part.shape)
        total += part.shape[0]
        rows.append(np.pad(part, ((0, 0), (0, 256 - part.shape[1]))))
    return np.concatenate(rows), first


TABLE, FIRST = tables()


def split(x):
    high = x.astype(bf16)
    return high, (x - high.astype(f32)).astype(bf16)


def mm(a, b):
    return jnp.dot(a, b, preferred_element_type=f32)


def mm3(a, b):
    return mm(a[0], b[0]) + (mm(a[0], b[1]) + mm(a[1], b[0]))


def lanes(*parts):
    return jnp.concatenate(parts, axis=1)


def sine_cosine(x):
    quarter = jnp.floor(x * (2.0 / math.pi) + 0.5)
    r = x - quarter * 1.5703125
    r = r - quarter * 4.837512969970703125e-4
    r = r - quarter * 7.54978995489188216e-8
    z = r * r
    sine = ((-1.9515295891e-4 * z + 8.3321608736e-3) * z - 1.6666654611e-1) * z * r + r
    cosine = ((2.443315711809948e-5 * z - 1.388731625493765e-3) * z + 4.166664568298827e-2) * z * z - 0.5 * z + 1.0
    halves = jnp.floor(quarter * 0.5)
    odd = quarter - 2.0 * halves
    minus = 1.0 - 2.0 * (halves - 2.0 * jnp.floor(halves * 0.5))
    swap = odd > 0.5
    return (
        jnp.where(swap, cosine, sine) * minus,
        jnp.where(swap, -sine, cosine) * minus,
    )


def kernel(
    sky, coef, basis, aperture, table_hbm,
    gradient_out, object_out,
    tab, skyp, coef_v, coef_send, coef_recv, mask_v, base, base3,
    edges, img, halo, turned, pre, pim, fpr, fpi, fmr, fmi, tre, tim, dre, dim_,
    sums, packed, sum_send, sum_recv, sum_v, obj_send, obj_all, ore, oim, dph,
    full, out_send, out_recv, grad_send, grad_recv, ret_send, ret_recv,
    local_sem, coef_ss, coef_rs, img_ss, img_rs, own_ss, own_rs, cross_ss, cross_rs,
    sum_ss, sum_rs, obj_ss, obj_rs, out_ss, out_rs, grad_ss, grad_rs, ret_ss, ret_rs,
):
    place, strip = lax.axis_index("frame"), lax.axis_index("patch")
    me, z = place // DEPTH, place % DEPTH

    def at(group, depth, which=None):
        return {"frame": group * DEPTH + depth, "patch": strip if which is None else which}

    def remote(src, dst, send, recv, device):
        return pltpu.make_async_remote_copy(
            src_ref=src, dst_ref=dst, send_sem=send, recv_sem=recv, device_id=device, device_id_type=MESH
        )

    def table(name, half=None):
        row, count, width = FIRST[name]
        if half is None:
            return tab[row : row + count, :width]
        return tab[row : row + count, half * 128 : half * 128 + 128]

    def from_left(name, x):
        h, r = split(x)
        return mm(table(name), jnp.concatenate([h, r, h]))

    def from_right(x, name, half=None):
        h, r = split(x)
        return mm(lanes(h, r)[:, : 128 + BOX], table(name, half)) + mm(h[:, :BOX], table(name + "_low", half))

    loads = [
        pltpu.make_async_copy(coef.at[0], coef_v, local_sem.at[0]),
        pltpu.make_async_copy(basis.at[:, pl.ds(LOW * SIDE, FLAT)], base, local_sem.at[1]),
        pltpu.make_async_copy(sky.at[0], skyp.at[pl.ds(RIM, 512)], local_sem.at[2]),
        pltpu.make_async_copy(table_hbm, tab, local_sem.at[3]),
        pltpu.make_async_copy(aperture, mask_v, local_sem.at[4]),
    ]
    for load in loads:
        load.start()

    barrier = pltpu.get_barrier_semaphore()
    beside = lax.rem(strip + jnp.where(me < 4, STRIPS - 1, 1), STRIPS)

    def greet(device):
        pl.semaphore_signal(barrier, inc=1, device_id=device, device_id_type=MESH)

    for d in range(1, GROUP):
        greet(at(lax.rem(me + d, GROUP), z))
    for d in range(1, DEPTH):
        greet(at(me, lax.rem(z + d, DEPTH)))
    for j in range(GROUP):
        greet(at(j, z, beside))

    skyp[pl.ds(0, RIM), :] = jnp.zeros((RIM, 256), f32)
    skyp[pl.ds(512 + RIM, 120), :] = jnp.zeros((120, 256), f32)
    loads[0].wait()
    for p in range(GROUP):
        row = jnp.broadcast_to(coef_v[p : p + 1, :], (8, MODES))
        coef_send[p * 8 : p * 8 + 8, :] = lanes(row, row)
    loads[2].wait()
    for half in range(2):
        strip_t = skyp[:, half * 128 : half * 128 + 128].T
        edges[2 * half] = strip_t[:8]
        edges[2 * half + 1] = strip_t[120:]
    pl.semaphore_wait(barrier, GROUP - 1 + DEPTH - 1 + GROUP)

    sends = []
    def rows8(ref, j):
        return ref.at[pl.ds(pl.multiple_of(j * 8, 8), 8)]

    for d in range(1, GROUP):
        t = lax.rem(me + d, GROUP)
        c = remote(rows8(coef_send, t), rows8(coef_recv, me), coef_ss.at[t], coef_rs.at[me], at(t, z))
        c.start()
        sends.append(c)
    coef_recv[pl.ds(pl.multiple_of(me * 8, 8), 8), :] = coef_send[pl.ds(pl.multiple_of(me * 8, 8), 8), :]

    def main_of(t):
        return skyp.at[
            pl.ds(pl.multiple_of(lax.rem(t, 4) * TILE, TILE), SIDE), pl.ds(pl.multiple_of((t // 4) * 128, 128), 128)
        ]

    def edge_of(kind, t):
        return edges.at[kind, :, pl.ds(pl.multiple_of(lax.rem(t, 4) * TILE, TILE), 256)]

    for d in range(1, GROUP):
        t = lax.rem(me + d, GROUP)
        c = remote(main_of(t), img.at[me], img_ss.at[t], img_rs.at[me], at(t, z))
        c.start()
        sends.append(c)
        kind, side = jnp.where(t < 4, 2, 1), jnp.where(t < 4, 1, 0)
        c = remote(edge_of(kind, t), halo.at[me, side], own_ss.at[t], own_rs.at[me], at(t, z))
        c.start()
        sends.append(c)
    for p in range(GROUP):
        kind, side, step = (3, 0, 1) if p < 4 else (0, 1, STRIPS - 1)
        c = remote(
            edge_of(kind, p), halo.at[me, side], cross_ss.at[p], cross_rs.at[me],
            at(p, z, lax.rem(strip + step, STRIPS)),
        )
        c.start()
        sends.append(c)
    own_side = jnp.where(me < 4, 1, 0)
    mine = [
        pltpu.make_async_copy(main_of(me), img.at[me], local_sem.at[6]),
        pltpu.make_async_copy(edge_of(jnp.where(me < 4, 2, 1), me), halo.at[me, own_side], local_sem.at[7]),
    ]
    for c in mine:
        c.start()

    loads[1].wait()

    def cut(g, carry):
        at_g = pl.ds(pl.multiple_of(g * PERIOD, 128), PERIOD)
        x = base[:, at_g]
        h, r = split(x)
        base3[0:MODES, at_g] = h
        base3[MODES : 2 * MODES, at_g] = r
        base3[2 * MODES :, at_g] = (x - h.astype(f32) - r.astype(f32)).astype(bf16)
        return carry

    lax.fori_loop(0, BOX // 8, cut, 0)
    for load in loads[3:]:
        load.wait()

    lane = lax.broadcasted_iota(jnp.int32, (8, 128), 1)
    mask = mask_v[LOW : LOW + BOX, 0:128].astype(f32)
    mask = pltpu.roll(mask, 128 - LOW, 1)
    mask = jnp.where(lax.broadcasted_iota(jnp.int32, (BOX, 128), 1) < BOX, mask, 0.0)
    area = jnp.sum(mask)
    intensity_scale = 1.0 / (SIDE * SIDE * area)
    dph[0:BOX, :] = mask

    for d in range(1, GROUP):
        j = lax.rem(me + GROUP - d, GROUP)
        remote(rows8(coef_send, j), rows8(coef_recv, j), coef_ss.at[j], coef_rs.at[j], at(j, z)).wait_recv()
    weights = coef_recv[pl.ds(0, GROUP, stride=8), :]
    w0 = weights.astype(bf16).astype(f32)
    w1 = (weights - w0).astype(bf16).astype(f32)
    w2 = weights - w0 - w1
    weights = jnp.concatenate([lanes(w, w[:, :MODES]) for w in (w0, w1, w2)]).astype(bf16)

    starts = [divmod(SIDE * r + LOW, 128) for r in range(8)]

    def pupils(g, carry):
        ph = mm(weights, base3[:, pl.ds(pl.multiple_of(g * PERIOD, 128), PERIOD)])
        ph = ph[0:8] + (ph[8:16] + ph[16:24])
        rows = []
        for tile, off in starts:
            x = ph[:, tile * 128 : tile * 128 + 128]
            if off:
                x = pltpu.roll(x, 128 - off, 1)
            if off + BOX > 128:
                y = pltpu.roll(ph[:, tile * 128 + 128 : tile * 128 + 256], 128 - off, 1)
                x = jnp.where(lane < 128 - off, x, y)
            rows.append(x)
        m = dph[pl.ds(pl.multiple_of(g * 8, 8), 8), :]
        m = jnp.concatenate([jnp.broadcast_to(m[r : r + 1], (8, 128)) for r in range(8)])
        sine, cosine = sine_cosine(jnp.concatenate(rows))
        at_g = pl.ds(pl.multiple_of(g * 64, 64), 64)
        pre[at_g, :] = m * cosine
        pim[at_g, :] = m * sine
        return carry

    lax.fori_loop(0, BOX // 8, pupils, 0, unroll=2)

    def of_frame(ref, f):
        return ref[pl.ds(f, BOX, stride=GROUP), :]

    def fold(x):
        return x[:BOX] + x[BOX:], x[:BOX] - x[BOX:]

    def stack(*parts):
        return jnp.concatenate(parts)

    def transfers(n, carry):
        fs = [n * UNROLL + m for m in range(UNROLL)]
        rows = []
        for f in fs:
            y = from_left("pupil_rows", lanes(of_frame(pre, f), of_frame(pim, f)))
            cr, ci, sr, si = y[:BOX, :128], y[:BOX, 128:], y[BOX:, :128], y[BOX:, 128:]
            rows += [cr + si, cr - si, ci - sr, ci + sr]
        y = from_right(stack(*rows), "pupil_columns")
        even, odd = [], []
        for m, f in enumerate(fs):
            r, i = y[4 * m * BOX : (4 * m + 2) * BOX], y[(4 * m + 2) * BOX : (4 * m + 4) * BOX]
            p_re, p_im = r[:, :128] + i[:, 128:], i[:, :128] - r[:, 128:]
            m_re, m_im = r[:, :128] - i[:, 128:], i[:, :128] + r[:, 128:]
            fpr[f], fpi[f], fmr[f], fmi[f] = p_re, p_im, m_re, m_im
            plus = (p_re * p_re + p_im * p_im) * intensity_scale
            minus = (m_re * m_re + m_im * m_im) * intensity_scale
            even += fold(plus + minus)
            odd += fold(plus - minus)
        x_re = from_right(stack(*even), "focal_columns", 0)
        x_im = from_right(stack(*odd), "focal_columns", 1)
        for m, f in enumerate(fs):
            x = lanes(x_re[2 * m * BOX : 2 * (m + 1) * BOX], x_im[2 * m * BOX : 2 * (m + 1) * BOX])
            c = from_left("focal_even", x[:BOX])
            s = from_left("focal_odd", x[BOX:])
            cr, ci, sr, si = c[:, :128], c[:, 128:], s[:, :128], s[:, 128:]
            tre[f] = stack(cr + si, cr - si)
            tim[f] = stack(ci - sr, ci + sr)
        return carry

    lax.fori_loop(0, GROUP // UNROLL, transfers, 0)

    for c in mine:
        c.wait()
    for j in range(GROUP):
        remote(edge_of(0, 0), halo.at[j, 1 - own_side], cross_ss.at[j], cross_rs.at[j], at(j, z, beside)).wait_recv()
    for d in range(1, GROUP):
        j = lax.rem(me + GROUP - d, GROUP)
        remote(main_of(j), img.at[j], img_ss.at[j], img_rs.at[j], at(j, z)).wait_recv()
        remote(edge_of(0, j), halo.at[j, own_side], own_ss.at[j], own_rs.at[j], at(j, z)).wait_recv()
    row = lax.broadcasted_iota(jnp.int32, (128, 256), 0)
    left_on = jnp.where(jnp.logical_and(strip == 0, me < 4), 0.0, 1.0)
    right_on = jnp.where(jnp.logical_and(strip == STRIPS - 1, me >= 4), 0.0, 1.0)
    rims = halo[...].reshape(128, 256) * jnp.where(lax.rem(row, 16) < 8, left_on, right_on)
    rims = rims.T[:SIDE]
    for f in range(GROUP):
        turned[f] = pltpu.roll(rims, (128 - 16 * f) % 128, 1) if f else rims

    sums[...] = jnp.zeros_like(sums)

    def data(n, carry):
        fs = [n * UNROLL + m for m in range(UNROLL)]
        h, r = split(stack(*[lanes(img[f], turned[f]) for f in fs]))
        x = mm3((h[:, :SIDE], r[:, :SIDE]), (table("data_columns"), table("data_columns_low")))
        n_re, n_im, power = sums[0], sums[1], sums[2]
        for m, f in enumerate(fs):
            h, r = split(x[m * SIDE : (m + 1) * SIDE])
            h = stack(h, r, h)
            y = mm(table("data_rows"), h[:256]) + mm(table("data_rows_end"), h[256:])
            cr, ci, sr, si = y[:BOX, :128], y[:BOX, 128:], y[BOX:, :128], y[BOX:, 128:]
            d_re, d_im = stack(cr + si, cr - si), stack(ci - sr, ci + sr)
            dre[f] = d_re
            dim_[f] = d_im
            t_re, t_im = tre[f], tim[f]
            n_re = n_re + (t_re * d_re + t_im * d_im)
            n_im = n_im + (t_re * d_im - t_im * d_re)
            power = power + (t_re * t_re + t_im * t_im)
        sums[0], sums[1], sums[2] = n_re, n_im, power
        return carry

    lax.fori_loop(0, GROUP // UNROLL, data, 0)

    lane80 = lax.broadcasted_iota(jnp.int32, (BOX, 128), 1)
    lane40 = lax.broadcasted_iota(jnp.int32, (REST_ROWS, 128), 1)
    rest = jnp.zeros((REST_ROWS, 128), f32)
    for part in range(3):
        plus, minus = sums[part, :BOX], sums[part, BOX:]
        packed[part * BOX : (part + 1) * BOX, :] = jnp.where(lane80 < MAIN, plus, pltpu.roll(minus, MAIN, 1))
        for sign, x in enumerate((plus, minus)):
            j = (2 * part + sign) * REST
            x = pltpu.roll(x[:REST_ROWS], (j - MAIN) % 128, 1)
            rest = jnp.where(jnp.logical_and(lane40 >= j, lane40 < j + REST), x, rest)
    packed[3 * BOX :, :] = rest
    for d in range(DEPTH):
        for part in range(3):
            sum_send[d, part * CHUNK : (part + 1) * CHUNK, :] = packed[
                part * BOX + d * CHUNK : part * BOX + (d + 1) * CHUNK, :
            ]
        sum_send[d, 3 * CHUNK :, :] = packed[3 * BOX + d * REST_CHUNK : 3 * BOX + (d + 1) * REST_CHUNK, :]
    for d in range(1, DEPTH):
        t = lax.rem(z + d, DEPTH)
        c = remote(sum_send.at[t], sum_recv.at[z], sum_ss.at[t], sum_rs.at[z], at(me, t))
        c.start()
        sends.append(c)
    sum_recv[z] = sum_send[z]
    for d in range(1, DEPTH):
        j = lax.rem(z + DEPTH - d, DEPTH)
        remote(sum_send.at[j], sum_recv.at[j], sum_ss.at[j], sum_rs.at[j], at(me, j)).wait_recv()
    total = sum_recv[0]
    for j in range(1, DEPTH):
        total = total + sum_recv[j]
    sum_v[...] = total
    power = sum_v[2 * CHUNK : 3 * CHUNK, :] + DAMPING
    obj_send[0:CHUNK, :] = sum_v[0:CHUNK, :] / power
    obj_send[CHUNK : 2 * CHUNK, :] = sum_v[CHUNK : 2 * CHUNK, :] / power
    rest = sum_v[3 * CHUNK :, :]
    lane5 = lax.broadcasted_iota(jnp.int32, (REST_CHUNK, 128), 1)
    power = jnp.where(lane5 < 2 * REST, pltpu.roll(rest, 128 - 4 * REST, 1), pltpu.roll(rest, 128 - 2 * REST, 1))
    power = jnp.where(lane5 < 4 * REST, power, 0.0) + DAMPING
    obj_send[2 * CHUNK :, :] = rest / power
    for d in range(1, DEPTH):
        t = lax.rem(z + d, DEPTH)
        c = remote(obj_send, obj_all.at[z], obj_ss.at[t], obj_rs.at[z], at(me, t))
        c.start()
        sends.append(c)
    obj_all[z] = obj_send[...]
    for d in range(1, DEPTH):
        j = lax.rem(z + DEPTH - d, DEPTH)
        remote(obj_send, obj_all.at[j], obj_ss.at[j], obj_rs.at[j], at(me, j)).wait_recv()
    for d in range(DEPTH):
        for part in range(2):
            packed[part * BOX + d * CHUNK : part * BOX + (d + 1) * CHUNK, :] = obj_all[
                d, part * CHUNK : (part + 1) * CHUNK, :
            ]
        packed[3 * BOX + d * REST_CHUNK : 3 * BOX + (d + 1) * REST_CHUNK, :] = obj_all[d, 2 * CHUNK :, :]
    rest = packed[3 * BOX :, :]
    for part, ref in enumerate((ore, oim)):
        main = packed[part * BOX : (part + 1) * BOX, :]
        for sign in range(2):
            j = (2 * part + sign) * REST
            x = stack(pltpu.roll(rest, (MAIN - j) % 128, 1), jnp.zeros((BOX - REST_ROWS, 128), f32))
            x = jnp.where(lane80 < HALF, x, 0.0)
            ref[sign * BOX : (sign + 1) * BOX, :] = jnp.where(
                lane80 < MAIN, pltpu.roll(main, MAIN, 1) if sign else main, x
            )

    scale = 2.0 / (SIDE * SIDE)

    def back(n, carry):
        fs = [n * UNROLL + m for m in range(UNROLL)]
        o_re, o_im = ore[...], oim[...]
        h_re, h_im = [], []
        for f in fs:
            t_re, t_im = tre[f], tim[f]
            e_re = dre[f] - (o_re * t_re - o_im * t_im)
            e_im = dim_[f] - (o_re * t_im + o_im * t_re)
            re_even, re_odd = fold(-scale * (e_re * o_re + e_im * o_im))
            im_even, im_odd = fold(scale * (e_re * o_im - e_im * o_re))
            c = from_left("focal_even", lanes(re_even, im_even))
            s = from_left("focal_odd", lanes(re_odd, im_odd))
            cr, ci, sr, si = c[:, :128], c[:, 128:], s[:, :128], s[:, 128:]
            h_re += [cr - si, cr + si]
            h_im += [ci + sr, ci - sr]
        even = from_right(stack(*h_re), "focal_columns", 0) * (4.0 * intensity_scale)
        odd = from_right(stack(*h_im), "focal_columns", 1) * (4.0 * intensity_scale)
        sum_rows, gap_rows = [], []
        for m, f in enumerate(fs):
            at_m = slice(2 * m * BOX, 2 * (m + 1) * BOX)
            plus, minus = even[at_m] + odd[at_m], even[at_m] - odd[at_m]
            p_re, p_im, m_re, m_im = plus * fpr[f], plus * fpi[f], minus * fmr[f], minus * fmi[f]
            sum_rows += [p_re + m_re, p_im + m_im]
            gap_rows += [p_re - m_re, p_im - m_im]
        qc = from_right(stack(*sum_rows), "back_columns", 0)
        qs = from_right(stack(*gap_rows), "back_columns", 1)
        for m, f in enumerate(fs):
            at_re, at_im = slice(4 * m * BOX, (4 * m + 2) * BOX), slice((4 * m + 2) * BOX, (4 * m + 4) * BOX)
            re_even, re_odd = fold(qc[at_re] - qs[at_im])
            im_even, im_odd = fold(qc[at_im] + qs[at_re])
            c = from_left("back_even", lanes(re_even, im_even))
            s = from_left("back_odd", lanes(re_odd, im_odd))
            g_re, g_im = c[:, :128] - s[:, 128:], c[:, 128:] + s[:, :128]
            dph[pl.ds(f, BOX, stride=GROUP), :] = of_frame(pre, f) * g_im - of_frame(pim, f) * g_re
        return carry

    lax.fori_loop(0, GROUP // UNROLL, back, 0)

    def project(g, total):
        tiles = [jnp.zeros((8, 128), f32) for _ in range(9)]
        for r, (tile, off) in enumerate(starts):
            x = dph[pl.ds(pl.multiple_of(g * 64, 64) + 8 * r, 8), :]
            if off:
                x = pltpu.roll(x, off, 1)
            if off + BOX > 128:
                tiles[tile + 1] += jnp.where(lane < off, x, 0.0)
                x = jnp.where(lane < off, 0.0, x)
            tiles[tile] += x
        x = jnp.concatenate(split(lanes(*tiles)))
        modes = base3[0 : 2 * MODES, pl.ds(pl.multiple_of(g * PERIOD, 128), PERIOD)]
        return total + lax.dot_general(x, modes, (((1,), (1,)), ((), ())), preferred_element_type=f32)

    total = lax.fori_loop(0, BOX // 8, project, jnp.zeros((16, 128), f32), unroll=5)
    total = total[:8] + total[8:]
    gradient = total + pltpu.roll(total, MODES, 1)

    grad_send[...] = gradient
    for d in range(1, DEPTH):
        t = lax.rem(z + d, DEPTH)
        c = remote(grad_send, grad_recv.at[z], grad_ss.at[t], grad_rs.at[z], at(me, t))
        c.start()
        sends.append(c)
    grad_recv[z] = gradient

    r_at = lax.broadcasted_iota(jnp.int32, (2 * SIDE, 2 * BOX), 0)
    c_at = lax.broadcasted_iota(jnp.int32, (2 * SIDE, 2 * BOX), 1)
    mirrored = r_at >= SIDE
    k = jnp.where(mirrored, r_at - SIDE, r_at)
    minus = (k >= HALF) != mirrored
    k = jnp.where(k >= HALF, SIDE - k, k) + jnp.where(minus, BOX, 0)
    pick_rows = jnp.where(k == c_at, 1.0, 0.0).astype(bf16)
    r_at = lax.broadcasted_iota(jnp.int32, (128, 256), 0)
    c_at = lax.broadcasted_iota(jnp.int32, (128, 256), 1)
    flip_columns = jnp.where(
        jnp.logical_and(r_at + c_at == SIDE, jnp.logical_and(c_at >= HALF, c_at < SIDE)), 1.0, 0.0
    ).astype(bf16)
    parts = [mm(pick_rows, part) for part in split(lanes(ore[...], oim[...]))]
    lane_full = lax.broadcasted_iota(jnp.int32, (SIDE, 128), 1)
    for n, sign in ((0, 1.0), (1, -1.0)):
        at_n = slice(n * 128, n * 128 + 128)
        half = parts[0][:SIDE, at_n] + parts[1][:SIDE, at_n]
        mirror = [mm(part[SIDE:, at_n].astype(bf16), flip_columns) for part in parts]
        mirror = sign * (mirror[0] + mirror[1])
        full[2 * n] = jnp.where(lane_full < HALF, half, mirror[:, :128])
        full[2 * n + 1] = mirror[:, 128:]
    first_row = z * 9 // 4
    for n in range(2):
        placed = [jnp.zeros((8, 128), f32) for _ in range(6)]
        for t in range(3):
            for piece in range(2):
                x = full[2 * n + piece, pl.ds(first_row + t, GROUP, stride=SIDE // GROUP), :]
                tile, off = divmod(SIDE * t + 128 * piece, 128)
                if off:
                    x = pltpu.roll(x, off, 1)
                    placed[tile + 1] += jnp.where(lane < off, x, 0.0)
                    x = jnp.where(lane < off, 0.0, x)
                placed[tile] += x
        placed = lanes(*placed)
        picked = jnp.zeros((8, 384), f32)
        for m in range(4):
            moved = pltpu.roll(placed, 768 - 36 * m, 1) if m else placed
            picked = picked + jnp.where(lax.rem(z, 4) == m, 1.0, 0.0) * moved[:, :384]
        for i in range(GROUP):
            out_send[i, n : n + 1, :] = picked[i : i + 1]
    for d in range(1, GROUP):
        t = lax.rem(me + d, GROUP)
        c = remote(out_send.at[t], out_recv.at[me], out_ss.at[t], out_rs.at[me], at(t, z))
        c.start()
        sends.append(c)
    out_recv[me] = out_send[me]

    for d in range(1, DEPTH):
        j = lax.rem(z + DEPTH - d, DEPTH)
        remote(grad_send, grad_recv.at[j], grad_ss.at[j], grad_rs.at[j], at(me, j)).wait_recv()
    mean = jnp.sum(grad_recv[...].reshape(64, 128), axis=0, keepdims=True) * (1.0 / FRAMES)
    gradient = gradient - mean
    for j in range(GROUP):
        ret_send[8 * j : 8 * j + 8, :] = jnp.broadcast_to(gradient[j : j + 1], (8, 128))
    for d in range(1, GROUP):
        t = lax.rem(me + d, GROUP)
        c = remote(rows8(ret_send, t), rows8(ret_recv, me), ret_ss.at[t], ret_rs.at[me], at(t, z))
        c.start()
        sends.append(c)
    ret_recv[pl.ds(pl.multiple_of(me * 8, 8), 8), :] = ret_send[pl.ds(pl.multiple_of(me * 8, 8), 8), :]

    for d in range(1, GROUP):
        j = lax.rem(me + GROUP - d, GROUP)
        remote(out_send.at[j], out_recv.at[j], out_ss.at[j], out_rs.at[j], at(j, z)).wait_recv()
    for p in range(GROUP):
        object_out[p] = out_recv[p, 0:2, :SHARE]
    for d in range(1, GROUP):
        j = lax.rem(me + GROUP - d, GROUP)
        remote(rows8(ret_send, j), rows8(ret_recv, j), ret_ss.at[j], ret_rs.at[j], at(j, z)).wait_recv()
    gradient_out[0] = ret_recv[pl.ds(0, GROUP, stride=8), :][:, :MODES]
    for c in sends:
        c.wait_send()


def body(sky_image, coefficients, mode_basis, aperture):
    vmem, dma = pltpu.VMEM, pltpu.SemaphoreType.DMA
    scratch = [
        vmem(TABLE.shape, bf16), vmem((640, 256), f32), vmem((GROUP, MODES), f32),
        vmem((64, 128), f32), vmem((64, 128), f32), vmem((SIDE, SIDE), jnp.int32), vmem((MODES, FLAT), f32),
        vmem((3 * MODES, FLAT), bf16),
        vmem((4, 8, 640), f32), vmem((GROUP, SIDE, 128), f32), vmem((GROUP, 2, 8, 256), f32),
        vmem((GROUP, SIDE, 128), f32), vmem((8 * BOX, 128), f32), vmem((8 * BOX, 128), f32),
        *[vmem((GROUP, 2 * BOX, 128), f32)] * 8,
        vmem((3, 2 * BOX, 128), f32), vmem((3 * BOX + REST_ROWS, 128), f32),
        vmem((DEPTH, SUMS, 128), f32), vmem((DEPTH, SUMS, 128), f32), vmem((SUMS, 128), f32),
        vmem((OBJECTS, 128), f32), vmem((DEPTH, OBJECTS, 128), f32), vmem((2 * BOX, 128), f32), vmem((2 * BOX, 128), f32),
        vmem((8 * BOX, 128), f32), vmem((4, SIDE, 128), f32), vmem((GROUP, 8, 384), f32), vmem((GROUP, 8, 384), f32),
        vmem((8, 128), f32), vmem((DEPTH, 8, 128), f32), vmem((64, 128), f32), vmem((64, 128), f32),
        *[dma((8,))] * 19,
    ]
    return pl.pallas_call(
        kernel,
        out_shape=(
            jax.ShapeDtypeStruct((1, GROUP, MODES), f32),
            jax.ShapeDtypeStruct((GROUP, 2, SHARE), f32),
        ),
        in_specs=[pl.BlockSpec(memory_space=pl.ANY)] * 5,
        out_specs=[pl.BlockSpec(memory_space=pltpu.VMEM)] * 2,
        scratch_shapes=scratch,
        compiler_params=pltpu.CompilerParams(collective_id=0, has_side_effects=True, vmem_limit_bytes=60 * 2**20),
    )(sky_image, coefficients, mode_basis, aperture, jnp.asarray(TABLE))


def solution(mesh):
    in_specs = (P("frame", None, "patch"), P("frame", "patch", None), P(), P())
    out_specs = (P("frame", "patch", None), P("patch", None, "frame"))
    return jax.shard_map(body, mesh=mesh, in_specs=in_specs, out_specs=out_specs, check_vma=False)
```

```python
import math

import jax
import jax.numpy as jnp
import ml_dtypes
import numpy as np
from jax import lax
from jax.experimental import pallas as pl
from jax.experimental.pallas import tpu as pltpu
from jax.sharding import PartitionSpec as P

SIDE = 144
RIM = 8
TILE = SIDE - 2 * RIM
LOW, BOX = 32, 80
GROUP = 8
DEPTH = 8
STRIPS = 4
FRAMES = GROUP * DEPTH
HALF = SIDE // 2 + 1
CHUNK = BOX // DEPTH
MAIN, REST = 64, HALF - 64
REST_ROWS = 40
REST_CHUNK = REST_ROWS // DEPTH
SUMS = 3 * CHUNK + REST_CHUNK
OBJECTS = 2 * CHUNK + REST_CHUNK
FLAT = BOX * SIDE
PERIOD = 8 * SIDE
MODES = 64
UNROLL = GROUP
SHARE = SIDE * SIDE // FRAMES
DAMPING = 0.02 * FRAMES
MESH = pl.DeviceIdType.MESH
f32, bf16 = jnp.float32, jnp.bfloat16


def profile():
    at = np.arange(SIDE, dtype=np.float64)
    distance = np.minimum(at, SIDE - 1 - at)
    taper = 0.3 + 0.7 * np.sin(math.pi * (distance + 1.0) / (2.0 * (RIM + 1))) ** 2
    return np.where(distance < RIM, taper, 1.0)


def tables():
    k = np.arange(HALF)
    y = np.arange(SIDE)
    u = np.arange(BOX) + LOW - SIDE // 2
    weight = np.ones(HALF)
    weight[0] = weight[-1] = 0.5

    def pair(a, b):
        angle = 2.0 * math.pi / SIDE * (np.outer(a, b) % SIDE)
        return np.cos(angle), np.sin(angle)

    def cut(t):
        high = t.astype(ml_dtypes.bfloat16)
        return high, (t - high.astype(np.float64)).astype(ml_dtypes.bfloat16)

    def rows_of(*blocks):
        t = np.zeros((BOX * len(blocks), blocks[0].shape[1]))
        for n, block in enumerate(blocks):
            t[n * BOX : n * BOX + block.shape[0]] = block
        high, low = cut(t)
        return np.concatenate([high, high, low], axis=1)

    def columns_of(c, s):
        t = np.zeros((-(-c.shape[0] // 16) * 16, 256))
        t[: c.shape[0], : c.shape[1]], t[: c.shape[0], 128 : 128 + c.shape[1]] = c, s
        return cut(t)

    def twice(c, s):
        high, low = columns_of(c, s)
        return np.concatenate([high, np.zeros((128 - BOX, 256), high.dtype), high]), low

    parts = {}
    c, s = pair(k, u)
    parts["pupil_rows"] = rows_of(c, s)
    parts["pupil_columns"], parts["pupil_columns_low"] = twice(c.T, s.T)
    parts["back_columns"], parts["back_columns_low"] = twice(weight[:, None] * c, weight[:, None] * s)

    def wide(t):
        return np.pad(t, ((0, BOX - t.shape[0]), (0, BOX - t.shape[1])))

    parts["back_even"], parts["back_odd"] = rows_of(wide(c.T * weight)), rows_of(wide(s.T * weight))
    c, s = pair(k, k)
    parts["focal_columns"], parts["focal_columns_low"] = twice(weight[:, None] * c, -weight[:, None] * s)
    parts["focal_even"], parts["focal_odd"] = rows_of(wide(c * weight)), rows_of(wide(s * weight))
    w = profile()
    c, s = pair(k, y)
    t = rows_of(c * w / SIDE, s * w / SIDE)
    parts["data_rows"], parts["data_rows_end"] = t[:, :256], t[:, 256:]
    order = np.concatenate([y[RIM:-RIM], y[:RIM], y[-RIM:]])
    parts["data_columns"], parts["data_columns_low"] = columns_of(
        (w[:, None] * c.T)[order], -(w[:, None] * s.T)[order]
    )
    first, rows, total = {}, [], 0
    for name, part in parts.items():
        first[name] = (total, *part.shape)
        total += part.shape[0]
        rows.append(np.pad(part, ((0, 0), (0, 256 - part.shape[1]))))
    return np.concatenate(rows), first


TABLE, FIRST = tables()


def split(x):
    high = x.astype(bf16)
    return high, (x - high.astype(f32)).astype(bf16)


def mm(a, b):
    return jnp.dot(a, b, preferred_element_type=f32)


def mm3(a, b):
    return mm(a[0], b[0]) + (mm(a[0], b[1]) + mm(a[1], b[0]))


def lanes(*parts):
    return jnp.concatenate(parts, axis=1)


def sine_cosine(x):
    quarter = jnp.floor(x * (2.0 / math.pi) + 0.5)
    r = x - quarter * 1.5703125
    r = r - quarter * 4.837512969970703125e-4
    r = r - quarter * 7.54978995489188216e-8
    z = r * r
    sine = ((-1.9515295891e-4 * z + 8.3321608736e-3) * z - 1.6666654611e-1) * z * r + r
    cosine = ((2.443315711809948e-5 * z - 1.388731625493765e-3) * z + 4.166664568298827e-2) * z * z - 0.5 * z + 1.0
    halves = jnp.floor(quarter * 0.5)
    odd = quarter - 2.0 * halves
    minus = 1.0 - 2.0 * (halves - 2.0 * jnp.floor(halves * 0.5))
    swap = odd > 0.5
    return (
        jnp.where(swap, cosine, sine) * minus,
        jnp.where(swap, -sine, cosine) * minus,
    )


def kernel(
    sky, coef, basis, aperture, table_hbm,
    gradient_out, object_out,
    tab, skyp, coef_v, coef_send, coef_recv, mask_v, base, base3,
    edges, img, halo, turned, pre, pim, fpr, fpi, fmr, fmi, tre, tim, dre, dim_,
    sums, packed, sum_send, sum_recv, sum_v, obj_send, obj_all, ore, oim, dph,
    full, out_send, out_recv, part_send, part_recv, ret_send, ret_recv,
    local_sem, coef_ss, coef_rs, img_ss, img_rs, own_ss, own_rs, cross_ss, cross_rs,
    sum_ss, sum_rs, obj_ss, obj_rs, out_ss, out_rs, ret_ss, ret_rs, part_sem,
):
    place, strip = lax.axis_index("frame"), lax.axis_index("patch")
    me, z = place // DEPTH, place % DEPTH

    y, x = me // 2, me % 2
    other = 1 - x
    near, far, back_y = y + 1 - 2 * (y % 2), 3 - y, (y + 2) % 4
    close = [near * 2 + x, far * 2 + x, y * 2 + other]
    distant = [near * 2 + other, far * 2 + other, back_y * 2 + x, back_y * 2 + other]
    peers = distant[::-1] + close[::-1]

    def at(group, depth, which=None):
        return {"frame": group * DEPTH + depth, "patch": strip if which is None else which}

    def remote(src, dst, send, recv, device):
        return pltpu.make_async_remote_copy(
            src_ref=src, dst_ref=dst, send_sem=send, recv_sem=recv, device_id=device, device_id_type=MESH
        )

    def table(name, half=None):
        row, count, width = FIRST[name]
        if half is None:
            return tab[row : row + count, :width]
        return tab[row : row + count, half * 128 : half * 128 + 128]

    def from_left(name, x):
        h, r = split(x)
        return mm(table(name), jnp.concatenate([h, r, h]))

    def from_right(x, name, half=None):
        h, r = split(x)
        return mm(lanes(h, r)[:, : 128 + BOX], table(name, half)) + mm(h[:, :BOX], table(name + "_low", half))

    loads = [
        pltpu.make_async_copy(coef.at[0], coef_v, local_sem.at[0]),
        pltpu.make_async_copy(basis.at[:, pl.ds(LOW * SIDE, FLAT)], base, local_sem.at[1]),
        pltpu.make_async_copy(sky.at[0], skyp.at[pl.ds(RIM, 512)], local_sem.at[2]),
        pltpu.make_async_copy(table_hbm, tab, local_sem.at[3]),
        pltpu.make_async_copy(aperture, mask_v, local_sem.at[4]),
    ]
    for load in loads:
        load.start()

    barrier = pltpu.get_barrier_semaphore()
    beside = lax.rem(strip + jnp.where(me < 4, STRIPS - 1, 1), STRIPS)

    def greet(device):
        pl.semaphore_signal(barrier, inc=1, device_id=device, device_id_type=MESH)

    for t in peers:
        greet(at(t, z))
    for d in range(1, DEPTH):
        greet(at(me, lax.rem(z + d, DEPTH)))
    for j in range(GROUP):
        greet(at(j, z, beside))

    skyp[pl.ds(0, RIM), :] = jnp.zeros((RIM, 256), f32)
    skyp[pl.ds(512 + RIM, 120), :] = jnp.zeros((120, 256), f32)
    loads[0].wait()
    for p in range(GROUP):
        row = jnp.broadcast_to(coef_v[p : p + 1, :], (8, MODES))
        coef_send[p * 8 : p * 8 + 8, :] = lanes(row, row)
    loads[2].wait()
    for half in range(2):
        strip_t = skyp[:, half * 128 : half * 128 + 128].T
        edges[2 * half] = strip_t[:8]
        edges[2 * half + 1] = strip_t[120:]
    pl.semaphore_wait(barrier, GROUP - 1 + DEPTH - 1 + GROUP)

    sends = []
    def rows8(ref, j):
        return ref.at[pl.ds(pl.multiple_of(j * 8, 8), 8)]

    for t in peers:
        c = remote(rows8(coef_send, t), rows8(coef_recv, me), coef_ss.at[t], coef_rs.at[me], at(t, z))
        c.start()
        sends.append(c)
    coef_recv[pl.ds(pl.multiple_of(me * 8, 8), 8), :] = coef_send[pl.ds(pl.multiple_of(me * 8, 8), 8), :]

    def main_of(t):
        return skyp.at[
            pl.ds(pl.multiple_of(lax.rem(t, 4) * TILE, TILE), SIDE), pl.ds(pl.multiple_of((t // 4) * 128, 128), 128)
        ]

    def edge_of(kind, t):
        return edges.at[kind, :, pl.ds(pl.multiple_of(lax.rem(t, 4) * TILE, TILE), 256)]

    for t in peers:
        kind, side = jnp.where(t < 4, 2, 1), jnp.where(t < 4, 1, 0)
        c = remote(edge_of(kind, t), halo.at[me, side], own_ss.at[t], own_rs.at[me], at(t, z))
        c.start()
        sends.append(c)
    for p in range(GROUP):
        kind, side, step = (3, 0, 1) if p < 4 else (0, 1, STRIPS - 1)
        c = remote(
            edge_of(kind, p), halo.at[me, side], cross_ss.at[p], cross_rs.at[me],
            at(p, z, lax.rem(strip + step, STRIPS)),
        )
        c.start()
        sends.append(c)
    for t in close + distant:
        c = remote(main_of(t), img.at[me], img_ss.at[t], img_rs.at[me], at(t, z))
        c.start()
        sends.append(c)
    own_side = jnp.where(me < 4, 1, 0)
    mine = [
        pltpu.make_async_copy(main_of(me), img.at[me], local_sem.at[6]),
        pltpu.make_async_copy(edge_of(jnp.where(me < 4, 2, 1), me), halo.at[me, own_side], local_sem.at[7]),
    ]
    for c in mine:
        c.start()

    loads[1].wait()

    def cut(g, carry):
        at_g = pl.ds(pl.multiple_of(g * PERIOD, 128), PERIOD)
        x = base[:, at_g]
        h, r = split(x)
        base3[0:MODES, at_g] = h
        base3[MODES : 2 * MODES, at_g] = r
        base3[2 * MODES :, at_g] = (x - h.astype(f32) - r.astype(f32)).astype(bf16)
        return carry

    lax.fori_loop(0, BOX // 8, cut, 0)
    for load in loads[3:]:
        load.wait()

    lane = lax.broadcasted_iota(jnp.int32, (8, 128), 1)
    mask = mask_v[LOW : LOW + BOX, 0:128].astype(f32)
    mask = pltpu.roll(mask, 128 - LOW, 1)
    mask = jnp.where(lax.broadcasted_iota(jnp.int32, (BOX, 128), 1) < BOX, mask, 0.0)
    area = jnp.sum(mask)
    intensity_scale = 1.0 / (SIDE * SIDE * area)
    dph[0:BOX, :] = mask

    for j in peers:
        remote(rows8(coef_send, j), rows8(coef_recv, j), coef_ss.at[j], coef_rs.at[j], at(j, z)).wait_recv()
    weights = coef_recv[pl.ds(0, GROUP, stride=8), :]
    w0 = weights.astype(bf16).astype(f32)
    w1 = (weights - w0).astype(bf16).astype(f32)
    w2 = weights - w0 - w1
    weights = jnp.concatenate([lanes(w, w[:, :MODES]) for w in (w0, w1, w2)]).astype(bf16)

    starts = [divmod(SIDE * r + LOW, 128) for r in range(8)]

    def pupils(g, carry):
        ph = mm(weights, base3[:, pl.ds(pl.multiple_of(g * PERIOD, 128), PERIOD)])
        ph = ph[0:8] + (ph[8:16] + ph[16:24])
        rows = []
        for tile, off in starts:
            x = ph[:, tile * 128 : tile * 128 + 128]
            if off:
                x = pltpu.roll(x, 128 - off, 1)
            if off + BOX > 128:
                y = pltpu.roll(ph[:, tile * 128 + 128 : tile * 128 + 256], 128 - off, 1)
                x = jnp.where(lane < 128 - off, x, y)
            rows.append(x)
        m = dph[pl.ds(pl.multiple_of(g * 8, 8), 8), :]
        m = jnp.concatenate([jnp.broadcast_to(m[r : r + 1], (8, 128)) for r in range(8)])
        sine, cosine = sine_cosine(jnp.concatenate(rows))
        at_g = pl.ds(pl.multiple_of(g * 64, 64), 64)
        pre[at_g, :] = m * cosine
        pim[at_g, :] = m * sine
        return carry

    lax.fori_loop(0, BOX // 8, pupils, 0, unroll=2)

    def of_frame(ref, f):
        return ref[pl.ds(f, BOX, stride=GROUP), :]

    def fold(x):
        return x[:BOX] + x[BOX:], x[:BOX] - x[BOX:]

    def stack(*parts):
        return jnp.concatenate(parts)

    def transfers(n, carry):
        fs = [n * UNROLL + m for m in range(UNROLL)]
        rows = []
        for f in fs:
            y = from_left("pupil_rows", lanes(of_frame(pre, f), of_frame(pim, f)))
            cr, ci, sr, si = y[:BOX, :128], y[:BOX, 128:], y[BOX:, :128], y[BOX:, 128:]
            rows += [cr + si, cr - si, ci - sr, ci + sr]
        y = from_right(stack(*rows), "pupil_columns")
        even, odd = [], []
        for m, f in enumerate(fs):
            r, i = y[4 * m * BOX : (4 * m + 2) * BOX], y[(4 * m + 2) * BOX : (4 * m + 4) * BOX]
            p_re, p_im = r[:, :128] + i[:, 128:], i[:, :128] - r[:, 128:]
            m_re, m_im = r[:, :128] - i[:, 128:], i[:, :128] + r[:, 128:]
            fpr[f], fpi[f], fmr[f], fmi[f] = p_re, p_im, m_re, m_im
            plus = (p_re * p_re + p_im * p_im) * intensity_scale
            minus = (m_re * m_re + m_im * m_im) * intensity_scale
            even += fold(plus + minus)
            odd += fold(plus - minus)
        x_re = from_right(stack(*even), "focal_columns", 0)
        x_im = from_right(stack(*odd), "focal_columns", 1)
        for m, f in enumerate(fs):
            x = lanes(x_re[2 * m * BOX : 2 * (m + 1) * BOX], x_im[2 * m * BOX : 2 * (m + 1) * BOX])
            c = from_left("focal_even", x[:BOX])
            s = from_left("focal_odd", x[BOX:])
            cr, ci, sr, si = c[:, :128], c[:, 128:], s[:, :128], s[:, 128:]
            tre[f] = stack(cr + si, cr - si)
            tim[f] = stack(ci - sr, ci + sr)
        return carry

    lax.fori_loop(0, GROUP // UNROLL, transfers, 0)

    for c in mine:
        c.wait()
    for j in range(GROUP):
        remote(edge_of(0, 0), halo.at[j, 1 - own_side], cross_ss.at[j], cross_rs.at[j], at(j, z, beside)).wait_recv()
    for j in peers:
        remote(edge_of(0, j), halo.at[j, own_side], own_ss.at[j], own_rs.at[j], at(j, z)).wait_recv()
    row = lax.broadcasted_iota(jnp.int32, (128, 256), 0)
    left_on = jnp.where(jnp.logical_and(strip == 0, me < 4), 0.0, 1.0)
    right_on = jnp.where(jnp.logical_and(strip == STRIPS - 1, me >= 4), 0.0, 1.0)
    rims = halo[...].reshape(128, 256) * jnp.where(lax.rem(row, 16) < 8, left_on, right_on)
    rims = rims.T[:SIDE]
    for f in range(GROUP):
        turned[f] = pltpu.roll(rims, (128 - 16 * f) % 128, 1) if f else rims

    sums[...] = jnp.zeros_like(sums)

    def data(fs):
        h, r = split(stack(*[lanes(img[f], turned[f]) for f in fs]))
        x = mm3((h[:, :SIDE], r[:, :SIDE]), (table("data_columns"), table("data_columns_low")))
        n_re, n_im, power = sums[0], sums[1], sums[2]
        for m, f in enumerate(fs):
            h, r = split(x[m * SIDE : (m + 1) * SIDE])
            h = stack(h, r, h)
            y = mm(table("data_rows"), h[:256]) + mm(table("data_rows_end"), h[256:])
            cr, ci, sr, si = y[:BOX, :128], y[:BOX, 128:], y[BOX:, :128], y[BOX:, 128:]
            d_re, d_im = stack(cr + si, cr - si), stack(ci - sr, ci + sr)
            dre[f] = d_re
            dim_[f] = d_im
            t_re, t_im = tre[f], tim[f]
            n_re = n_re + (t_re * d_re + t_im * d_im)
            n_im = n_im + (t_re * d_im - t_im * d_re)
            power = power + (t_re * t_re + t_im * t_im)
        sums[0], sums[1], sums[2] = n_re, n_im, power

    def arrive(js):
        for j in js:
            remote(main_of(j), img.at[j], img_ss.at[j], img_rs.at[j], at(j, z)).wait_recv()

    arrive(close)
    data([me, *close])
    arrive(distant)
    data(distant)

    lane80 = lax.broadcasted_iota(jnp.int32, (BOX, 128), 1)
    lane40 = lax.broadcasted_iota(jnp.int32, (REST_ROWS, 128), 1)
    rest = jnp.zeros((REST_ROWS, 128), f32)
    for part in range(3):
        plus, minus = sums[part, :BOX], sums[part, BOX:]
        packed[part * BOX : (part + 1) * BOX, :] = jnp.where(lane80 < MAIN, plus, pltpu.roll(minus, MAIN, 1))
        for sign, x in enumerate((plus, minus)):
            j = (2 * part + sign) * REST
            x = pltpu.roll(x[:REST_ROWS], (j - MAIN) % 128, 1)
            rest = jnp.where(jnp.logical_and(lane40 >= j, lane40 < j + REST), x, rest)
    packed[3 * BOX :, :] = rest
    for d in range(DEPTH):
        for part in range(3):
            sum_send[d, part * CHUNK : (part + 1) * CHUNK, :] = packed[
                part * BOX + d * CHUNK : part * BOX + (d + 1) * CHUNK, :
            ]
        sum_send[d, 3 * CHUNK :, :] = packed[3 * BOX + d * REST_CHUNK : 3 * BOX + (d + 1) * REST_CHUNK, :]
    for d in range(1, DEPTH):
        t = lax.rem(z + d, DEPTH)
        c = remote(sum_send.at[t], sum_recv.at[z], sum_ss.at[t], sum_rs.at[z], at(me, t))
        c.start()
        sends.append(c)
    sum_recv[z] = sum_send[z]
    for d in range(1, DEPTH):
        j = lax.rem(z + DEPTH - d, DEPTH)
        remote(sum_send.at[j], sum_recv.at[j], sum_ss.at[j], sum_rs.at[j], at(me, j)).wait_recv()
    total = sum_recv[0]
    for j in range(1, DEPTH):
        total = total + sum_recv[j]
    sum_v[...] = total
    power = sum_v[2 * CHUNK : 3 * CHUNK, :] + DAMPING
    obj_send[0:CHUNK, :] = sum_v[0:CHUNK, :] / power
    obj_send[CHUNK : 2 * CHUNK, :] = sum_v[CHUNK : 2 * CHUNK, :] / power
    rest = sum_v[3 * CHUNK :, :]
    lane5 = lax.broadcasted_iota(jnp.int32, (REST_CHUNK, 128), 1)
    power = jnp.where(lane5 < 2 * REST, pltpu.roll(rest, 128 - 4 * REST, 1), pltpu.roll(rest, 128 - 2 * REST, 1))
    power = jnp.where(lane5 < 4 * REST, power, 0.0) + DAMPING
    obj_send[2 * CHUNK :, :] = rest / power
    for d in range(1, DEPTH):
        t = lax.rem(z + d, DEPTH)
        c = remote(obj_send, obj_all.at[z], obj_ss.at[t], obj_rs.at[z], at(me, t))
        c.start()
        sends.append(c)
    obj_all[z] = obj_send[...]
    for d in range(1, DEPTH):
        j = lax.rem(z + DEPTH - d, DEPTH)
        remote(obj_send, obj_all.at[j], obj_ss.at[j], obj_rs.at[j], at(me, j)).wait_recv()
    for d in range(DEPTH):
        for part in range(2):
            packed[part * BOX + d * CHUNK : part * BOX + (d + 1) * CHUNK, :] = obj_all[
                d, part * CHUNK : (part + 1) * CHUNK, :
            ]
        packed[3 * BOX + d * REST_CHUNK : 3 * BOX + (d + 1) * REST_CHUNK, :] = obj_all[d, 2 * CHUNK :, :]
    rest = packed[3 * BOX :, :]
    for part, ref in enumerate((ore, oim)):
        main = packed[part * BOX : (part + 1) * BOX, :]
        for sign in range(2):
            j = (2 * part + sign) * REST
            x = stack(pltpu.roll(rest, (MAIN - j) % 128, 1), jnp.zeros((BOX - REST_ROWS, 128), f32))
            x = jnp.where(lane80 < HALF, x, 0.0)
            ref[sign * BOX : (sign + 1) * BOX, :] = jnp.where(
                lane80 < MAIN, pltpu.roll(main, MAIN, 1) if sign else main, x
            )

    scale = 2.0 / (SIDE * SIDE)

    def back(n, carry):
        fs = [n * UNROLL + m for m in range(UNROLL)]
        o_re, o_im = ore[...], oim[...]
        h_re, h_im = [], []
        for f in fs:
            t_re, t_im = tre[f], tim[f]
            e_re = dre[f] - (o_re * t_re - o_im * t_im)
            e_im = dim_[f] - (o_re * t_im + o_im * t_re)
            re_even, re_odd = fold(-scale * (e_re * o_re + e_im * o_im))
            im_even, im_odd = fold(scale * (e_re * o_im - e_im * o_re))
            c = from_left("focal_even", lanes(re_even, im_even))
            s = from_left("focal_odd", lanes(re_odd, im_odd))
            cr, ci, sr, si = c[:, :128], c[:, 128:], s[:, :128], s[:, 128:]
            h_re += [cr - si, cr + si]
            h_im += [ci + sr, ci - sr]
        even = from_right(stack(*h_re), "focal_columns", 0) * (4.0 * intensity_scale)
        odd = from_right(stack(*h_im), "focal_columns", 1) * (4.0 * intensity_scale)
        sum_rows, gap_rows = [], []
        for m, f in enumerate(fs):
            at_m = slice(2 * m * BOX, 2 * (m + 1) * BOX)
            plus, minus = even[at_m] + odd[at_m], even[at_m] - odd[at_m]
            p_re, p_im, m_re, m_im = plus * fpr[f], plus * fpi[f], minus * fmr[f], minus * fmi[f]
            sum_rows += [p_re + m_re, p_im + m_im]
            gap_rows += [p_re - m_re, p_im - m_im]
        qc = from_right(stack(*sum_rows), "back_columns", 0)
        qs = from_right(stack(*gap_rows), "back_columns", 1)
        for m, f in enumerate(fs):
            at_re, at_im = slice(4 * m * BOX, (4 * m + 2) * BOX), slice((4 * m + 2) * BOX, (4 * m + 4) * BOX)
            re_even, re_odd = fold(qc[at_re] - qs[at_im])
            im_even, im_odd = fold(qc[at_im] + qs[at_re])
            c = from_left("back_even", lanes(re_even, im_even))
            s = from_left("back_odd", lanes(re_odd, im_odd))
            g_re, g_im = c[:, :128] - s[:, 128:], c[:, 128:] + s[:, :128]
            dph[pl.ds(f, BOX, stride=GROUP), :] = of_frame(pre, f) * g_im - of_frame(pim, f) * g_re
        return carry

    lax.fori_loop(0, GROUP // UNROLL, back, 0)

    def project(g, total):
        tiles = [jnp.zeros((8, 128), f32) for _ in range(9)]
        for r, (tile, off) in enumerate(starts):
            x = dph[pl.ds(pl.multiple_of(g * 64, 64) + 8 * r, 8), :]
            if off:
                x = pltpu.roll(x, off, 1)
            if off + BOX > 128:
                tiles[tile + 1] += jnp.where(lane < off, x, 0.0)
                x = jnp.where(lane < off, 0.0, x)
            tiles[tile] += x
        x = jnp.concatenate(split(lanes(*tiles)))
        modes = base3[0 : 2 * MODES, pl.ds(pl.multiple_of(g * PERIOD, 128), PERIOD)]
        return total + lax.dot_general(x, modes, (((1,), (1,)), ((), ())), preferred_element_type=f32)

    total = lax.fori_loop(0, BOX // 8, project, jnp.zeros((16, 128), f32), unroll=5)
    total = total[:8] + total[8:]
    gradient = total + pltpu.roll(total, MODES, 1)

    for j in range(GROUP):
        ret_send[j] = gradient[j : j + 1]
    part_send[0] = jnp.sum(gradient, axis=0, keepdims=True)

    groups = list(zip([*peers, me], (3, 2, 2, 2, 1, 1, 1, 0)))
    depths = [(z, 0)] + [(lax.rem(z + d, DEPTH), min(d, DEPTH - d)) for d in range(1, DEPTH)]
    ways = [(a + b, group, depth) for group, a in groups for depth, b in depths if a + b]
    for _, group, depth in sorted(ways, key=lambda way: -way[0]):
        remote(part_send, part_recv.at[pl.ds(place, 1)], part_sem.at[0], part_sem.at[1], at(group, depth)).start()
    for t in peers:
        c = remote(ret_send.at[t], ret_recv.at[me], ret_ss.at[t], ret_rs.at[me], at(t, z))
        c.start()
        sends.append(c)
    part_recv[place] = part_send[0]
    ret_recv[me] = ret_send[me]

    r_at = lax.broadcasted_iota(jnp.int32, (2 * SIDE, 2 * BOX), 0)
    c_at = lax.broadcasted_iota(jnp.int32, (2 * SIDE, 2 * BOX), 1)
    mirrored = r_at >= SIDE
    k = jnp.where(mirrored, r_at - SIDE, r_at)
    minus = (k >= HALF) != mirrored
    k = jnp.where(k >= HALF, SIDE - k, k) + jnp.where(minus, BOX, 0)
    pick_rows = jnp.where(k == c_at, 1.0, 0.0).astype(bf16)
    r_at = lax.broadcasted_iota(jnp.int32, (128, 256), 0)
    c_at = lax.broadcasted_iota(jnp.int32, (128, 256), 1)
    flip_columns = jnp.where(
        jnp.logical_and(r_at + c_at == SIDE, jnp.logical_and(c_at >= HALF, c_at < SIDE)), 1.0, 0.0
    ).astype(bf16)
    parts = [mm(pick_rows, part) for part in split(lanes(ore[...], oim[...]))]
    lane_full = lax.broadcasted_iota(jnp.int32, (SIDE, 128), 1)
    for n, sign in ((0, 1.0), (1, -1.0)):
        at_n = slice(n * 128, n * 128 + 128)
        half = parts[0][:SIDE, at_n] + parts[1][:SIDE, at_n]
        mirror = [mm(part[SIDE:, at_n].astype(bf16), flip_columns) for part in parts]
        mirror = sign * (mirror[0] + mirror[1])
        full[2 * n] = jnp.where(lane_full < HALF, half, mirror[:, :128])
        full[2 * n + 1] = mirror[:, 128:]
    first_row = z * 9 // 4
    for n in range(2):
        placed = [jnp.zeros((8, 128), f32) for _ in range(6)]
        for t in range(3):
            for piece in range(2):
                x = full[2 * n + piece, pl.ds(first_row + t, GROUP, stride=SIDE // GROUP), :]
                tile, off = divmod(SIDE * t + 128 * piece, 128)
                if off:
                    x = pltpu.roll(x, off, 1)
                    placed[tile + 1] += jnp.where(lane < off, x, 0.0)
                    x = jnp.where(lane < off, 0.0, x)
                placed[tile] += x
        placed = lanes(*placed)
        picked = jnp.zeros((8, 384), f32)
        for m in range(4):
            moved = pltpu.roll(placed, 768 - 36 * m, 1) if m else placed
            picked = picked + jnp.where(lax.rem(z, 4) == m, 1.0, 0.0) * moved[:, :384]
        for i in range(GROUP):
            out_send[i, n : n + 1, :] = picked[i : i + 1]
    for t in peers:
        c = remote(out_send.at[t], out_recv.at[me], out_ss.at[t], out_rs.at[me], at(t, z))
        c.start()
        sends.append(c)
    out_recv[me] = out_send[me]

    for j in peers:
        remote(out_send.at[j], out_recv.at[j], out_ss.at[j], out_rs.at[j], at(j, z)).wait_recv()
    for p in range(GROUP):
        object_out[p] = out_recv[p, 0:2, :SHARE]
    for j in peers:
        remote(ret_send.at[j], ret_recv.at[j], ret_ss.at[j], ret_rs.at[j], at(j, z)).wait_recv()
    arrived = part_recv.at[pl.ds(0, FRAMES - 1)]
    arrived = remote(arrived, arrived, part_sem.at[0], part_sem.at[1], at(peers[0], z))
    arrived.wait_recv()
    for p in range(GROUP):
        mean = part_recv[p * DEPTH]
        for n in range(1, DEPTH):
            mean = mean + part_recv[p * DEPTH + n]
        gradient_out[0, p : p + 1, :] = (ret_recv[p] - mean * (1.0 / FRAMES))[:, :MODES]
    arrived.wait_send()
    for c in sends:
        c.wait_send()


def body(sky_image, coefficients, mode_basis, aperture):
    vmem, dma = pltpu.VMEM, pltpu.SemaphoreType.DMA
    scratch = [
        vmem(TABLE.shape, bf16), vmem((640, 256), f32), vmem((GROUP, MODES), f32),
        vmem((64, 128), f32), vmem((64, 128), f32), vmem((SIDE, SIDE), jnp.int32), vmem((MODES, FLAT), f32),
        vmem((3 * MODES, FLAT), bf16),
        vmem((4, 8, 640), f32), vmem((GROUP, SIDE, 128), f32), vmem((GROUP, 2, 8, 256), f32),
        vmem((GROUP, SIDE, 128), f32), vmem((8 * BOX, 128), f32), vmem((8 * BOX, 128), f32),
        *[vmem((GROUP, 2 * BOX, 128), f32)] * 8,
        vmem((3, 2 * BOX, 128), f32), vmem((3 * BOX + REST_ROWS, 128), f32),
        vmem((DEPTH, SUMS, 128), f32), vmem((DEPTH, SUMS, 128), f32), vmem((SUMS, 128), f32),
        vmem((OBJECTS, 128), f32), vmem((DEPTH, OBJECTS, 128), f32), vmem((2 * BOX, 128), f32), vmem((2 * BOX, 128), f32),
        vmem((8 * BOX, 128), f32), vmem((4, SIDE, 128), f32), vmem((GROUP, 8, 384), f32), vmem((GROUP, 8, 384), f32),
        vmem((1, 1, 128), f32), vmem((FRAMES, 1, 128), f32), vmem((GROUP, 1, 128), f32), vmem((GROUP, 1, 128), f32),
        *[dma((8,))] * 17, dma((2,)),
    ]
    return pl.pallas_call(
        kernel,
        out_shape=(
            pltpu.VMEM((1, GROUP, MODES), f32),
            pltpu.VMEM((GROUP, 2, SHARE), f32),
        ),
        in_specs=[pl.BlockSpec(memory_space=pl.ANY)] * 5,
        out_specs=[pl.BlockSpec(memory_space=pltpu.VMEM)] * 2,
        scratch_shapes=scratch,
        compiler_params=pltpu.CompilerParams(collective_id=0, has_side_effects=True, vmem_limit_bytes=60 * 2**20),
    )(sky_image, coefficients, mode_basis, aperture, jnp.asarray(TABLE))


def solution(mesh):
    in_specs = (P("frame", None, "patch"), P("frame", "patch", None), P(), P())
    out_specs = (P("frame", "patch", None), P("patch", None, "frame"))
    return jax.shard_map(body, mesh=mesh, in_specs=in_specs, out_specs=out_specs, check_vma=False)
```

```python
import math

import jax
import jax.numpy as jnp
import ml_dtypes
import numpy as np
from jax import lax
from jax.experimental import pallas as pl
from jax.experimental.pallas import tpu as pltpu
from jax.sharding import PartitionSpec as P

SIDE = 144
RIM = 8
TILE = SIDE - 2 * RIM
LOW, BOX = 32, 80
GROUP = 8
DEPTH = 8
STRIPS = 4
FRAMES = GROUP * DEPTH
HALF = SIDE // 2 + 1
CHUNK = BOX // DEPTH
MAIN, REST = 64, HALF - 64
REST_ROWS = 40
REST_CHUNK = REST_ROWS // DEPTH
SUMS = 3 * CHUNK + REST_CHUNK
OBJECTS = 2 * CHUNK + REST_CHUNK
FLAT = BOX * SIDE
PERIOD = 8 * SIDE
MODES = 64
UNROLL = GROUP
SHARE = SIDE * SIDE // FRAMES
DAMPING = 0.02 * FRAMES
FAR_FIRST = (4, 3, 5, 2, 6, 1, 7)
MESH = pl.DeviceIdType.MESH
f32, bf16 = jnp.float32, jnp.bfloat16


def profile():
    at = np.arange(SIDE, dtype=np.float64)
    distance = np.minimum(at, SIDE - 1 - at)
    taper = 0.3 + 0.7 * np.sin(math.pi * (distance + 1.0) / (2.0 * (RIM + 1))) ** 2
    return np.where(distance < RIM, taper, 1.0)


def tables():
    k = np.arange(HALF)
    y = np.arange(SIDE)
    u = np.arange(BOX) + LOW - SIDE // 2
    weight = np.ones(HALF)
    weight[0] = weight[-1] = 0.5

    def pair(a, b):
        angle = 2.0 * math.pi / SIDE * (np.outer(a, b) % SIDE)
        return np.cos(angle), np.sin(angle)

    def cut(t):
        high = t.astype(ml_dtypes.bfloat16)
        return high, (t - high.astype(np.float64)).astype(ml_dtypes.bfloat16)

    def rows_of(*blocks):
        t = np.zeros((BOX * len(blocks), blocks[0].shape[1]))
        for n, block in enumerate(blocks):
            t[n * BOX : n * BOX + block.shape[0]] = block
        high, low = cut(t)
        return np.concatenate([high, high, low], axis=1)

    def columns_of(c, s):
        t = np.zeros((-(-c.shape[0] // 16) * 16, 256))
        t[: c.shape[0], : c.shape[1]], t[: c.shape[0], 128 : 128 + c.shape[1]] = c, s
        return cut(t)

    def twice(c, s):
        t = np.zeros((BOX, 256))
        t[: c.shape[0], : c.shape[1]], t[: c.shape[0], 128 : 128 + c.shape[1]] = c, s
        high, low = cut(t)
        return np.concatenate([high, high, low])

    parts = {}
    c, s = pair(k, u)
    parts["pupil_rows"] = rows_of(c, s)
    parts["pupil_columns"] = twice(c.T, s.T)
    parts["back_columns"] = twice(weight[:, None] * c, weight[:, None] * s)

    def wide(t):
        return np.pad(t, ((0, BOX - t.shape[0]), (0, BOX - t.shape[1])))

    parts["back_even"], parts["back_odd"] = rows_of(wide(c.T * weight)), rows_of(wide(s.T * weight))
    c, s = pair(k, k)
    parts["focal_columns"] = twice(weight[:, None] * c, -weight[:, None] * s)
    parts["focal_even"], parts["focal_odd"] = rows_of(wide(c * weight)), rows_of(wide(s * weight))
    w = profile()
    c, s = pair(k, y)
    t = rows_of(c * w / SIDE, s * w / SIDE)
    parts["data_rows"], parts["data_rows_end"] = t[:, :256], t[:, 256:]
    order = np.concatenate([y[RIM:-RIM], y[:RIM], y[-RIM:]])
    parts["data_columns"], parts["data_columns_low"] = columns_of(
        (w[:, None] * c.T)[order], -(w[:, None] * s.T)[order]
    )
    first, rows, total = {}, [], 0
    for name, part in parts.items():
        first[name] = (total, *part.shape)
        total += part.shape[0]
        rows.append(np.pad(part, ((0, 0), (0, 256 - part.shape[1]))))
    return np.concatenate(rows), first


TABLE, FIRST = tables()


def split(x):
    high = x.astype(bf16)
    return high, (x - high.astype(f32)).astype(bf16)


def mm(a, b):
    return jnp.dot(a, b, preferred_element_type=f32)


def mm3(a, b):
    return mm(a[0], b[0]) + (mm(a[0], b[1]) + mm(a[1], b[0]))


def lanes(*parts):
    return jnp.concatenate(parts, axis=1)


def sine_cosine(x):
    quarter = jnp.floor(x * (2.0 / math.pi) + 0.5)
    r = x - quarter * 1.5703125
    r = r - quarter * 4.837512969970703125e-4
    r = r - quarter * 7.54978995489188216e-8
    z = r * r
    sine = ((-1.9515295891e-4 * z + 8.3321608736e-3) * z - 1.6666654611e-1) * z * r + r
    cosine = ((2.443315711809948e-5 * z - 1.388731625493765e-3) * z + 4.166664568298827e-2) * z * z - 0.5 * z + 1.0
    halves = jnp.floor(quarter * 0.5)
    odd = quarter - 2.0 * halves
    minus = 1.0 - 2.0 * (halves - 2.0 * jnp.floor(halves * 0.5))
    swap = odd > 0.5
    return (
        jnp.where(swap, cosine, sine) * minus,
        jnp.where(swap, -sine, cosine) * minus,
    )


def kernel(
    sky, coef, basis, aperture, table_hbm,
    gradient_out, object_out,
    tab, skyp, coef_v, coef_send, coef_recv, mask_v, base, base3,
    edges, img, halo, turned, pre, pim, fpr, fpi, fmr, fmi, tre, tim, dre, dim_,
    sums, packed, sum_send, sum_recv, sum_v, obj_send, obj_all, ore, oim, dph,
    full, out_send, out_recv, part_send, part_recv, ret_send, ret_recv,
    local_sem, coef_ss, coef_rs, img_ss, img_rs, own_ss, own_rs, cross_ss, cross_rs,
    sum_ss, sum_rs, obj_ss, obj_rs, out_ss, out_rs, ret_ss, ret_rs, part_sem,
):
    place, strip = lax.axis_index("frame"), lax.axis_index("patch")
    me, z = place // DEPTH, place % DEPTH

    y, x = me // 2, me % 2
    other = 1 - x
    near, far, back_y = y + 1 - 2 * (y % 2), 3 - y, (y + 2) % 4
    close = [near * 2 + x, far * 2 + x, y * 2 + other]
    distant = [near * 2 + other, far * 2 + other, back_y * 2 + x, back_y * 2 + other]
    peers = distant[::-1] + close[::-1]

    def at(group, depth, which=None):
        return {"frame": group * DEPTH + depth, "patch": strip if which is None else which}

    def remote(src, dst, send, recv, device):
        return pltpu.make_async_remote_copy(
            src_ref=src, dst_ref=dst, send_sem=send, recv_sem=recv, device_id=device, device_id_type=MESH
        )

    def table(name, half=None):
        row, count, width = FIRST[name]
        if half is None:
            return tab[row : row + count, :width]
        return tab[row : row + count, half * 128 : half * 128 + 128]

    def from_left(name, x):
        h, r = split(x)
        return mm(table(name), jnp.concatenate([h, r, h]))

    def from_right(x, name, half=None):
        h, r = split(x)
        return mm(lanes(h[:, :BOX], r[:, :BOX], h[:, :BOX]), table(name, half))

    loads = [
        pltpu.make_async_copy(coef.at[0], coef_v, local_sem.at[0]),
        pltpu.make_async_copy(basis.at[:, pl.ds(LOW * SIDE, FLAT)], base, local_sem.at[1]),
        pltpu.make_async_copy(sky.at[0], skyp.at[pl.ds(RIM, 512)], local_sem.at[2]),
        pltpu.make_async_copy(table_hbm, tab, local_sem.at[3]),
        pltpu.make_async_copy(aperture, mask_v, local_sem.at[4]),
    ]
    for load in loads:
        load.start()

    barrier = pltpu.get_barrier_semaphore()
    beside = lax.rem(strip + jnp.where(me < 4, STRIPS - 1, 1), STRIPS)

    def greet(device):
        pl.semaphore_signal(barrier, inc=1, device_id=device, device_id_type=MESH)

    for d in FAR_FIRST:
        greet(at(me, lax.rem(z + d, DEPTH)))
    for t in [*peers, me]:
        greet(at(t, z, beside))
    for t in peers:
        greet(at(t, z))

    skyp[pl.ds(0, RIM), :] = jnp.zeros((RIM, 256), f32)
    skyp[pl.ds(512 + RIM, 120), :] = jnp.zeros((120, 256), f32)
    loads[0].wait()
    for p in range(GROUP):
        row = jnp.broadcast_to(coef_v[p : p + 1, :], (8, MODES))
        coef_send[p * 8 : p * 8 + 8, :] = lanes(row, row)
    loads[2].wait()
    for half in range(2):
        strip_t = skyp[:, half * 128 : half * 128 + 128].T
        for r in range(4):
            edges[2 * half, r] = strip_t[:8, r * TILE : r * TILE + SIDE]
            edges[2 * half + 1, r] = strip_t[120:, r * TILE : r * TILE + SIDE]
    pl.semaphore_wait(barrier, GROUP - 1 + DEPTH - 1 + GROUP)

    sends = []
    def rows8(ref, j):
        return ref.at[pl.ds(pl.multiple_of(j * 8, 8), 8)]

    for t in peers:
        c = remote(rows8(coef_send, t), rows8(coef_recv, me), coef_ss.at[t], coef_rs.at[me], at(t, z))
        c.start()
        sends.append(c)
    coef_recv[pl.ds(pl.multiple_of(me * 8, 8), 8), :] = coef_send[pl.ds(pl.multiple_of(me * 8, 8), 8), :]

    def main_of(t):
        return skyp.at[
            pl.ds(pl.multiple_of(lax.rem(t, 4) * TILE, TILE), SIDE), pl.ds(pl.multiple_of((t // 4) * 128, 128), 128)
        ]

    def edge_of(kind, t):
        return edges.at[kind, lax.rem(t, 4)]

    for t in peers:
        kind, side = jnp.where(t < 4, 2, 1), jnp.where(t < 4, 1, 0)
        c = remote(edge_of(kind, t), halo.at[me, side], own_ss.at[t], own_rs.at[me], at(t, z))
        c.start()
        sends.append(c)
    for p in range(GROUP):
        kind, side, step = (3, 0, 1) if p < 4 else (0, 1, STRIPS - 1)
        c = remote(
            edge_of(kind, p), halo.at[me, side], cross_ss.at[p], cross_rs.at[me],
            at(p, z, lax.rem(strip + step, STRIPS)),
        )
        c.start()
        sends.append(c)
    for t in close + distant:
        c = remote(main_of(t), img.at[me], img_ss.at[t], img_rs.at[me], at(t, z))
        c.start()
        sends.append(c)
    own_side = jnp.where(me < 4, 1, 0)
    mine = [
        pltpu.make_async_copy(main_of(me), img.at[me], local_sem.at[6]),
        pltpu.make_async_copy(edge_of(jnp.where(me < 4, 2, 1), me), halo.at[me, own_side], local_sem.at[7]),
    ]
    for c in mine:
        c.start()

    loads[1].wait()

    def cut(g, carry):
        at_g = pl.ds(pl.multiple_of(g * PERIOD, 128), PERIOD)
        x = base[:, at_g]
        h, r = split(x)
        base3[0:MODES, at_g] = h
        base3[MODES : 2 * MODES, at_g] = r
        base3[2 * MODES :, at_g] = (x - h.astype(f32) - r.astype(f32)).astype(bf16)
        return carry

    lax.fori_loop(0, BOX // 8, cut, 0)
    for load in loads[3:]:
        load.wait()

    lane = lax.broadcasted_iota(jnp.int32, (8, 128), 1)
    mask = mask_v[LOW : LOW + BOX, 0:128].astype(f32)
    mask = pltpu.roll(mask, 128 - LOW, 1)
    mask = jnp.where(lax.broadcasted_iota(jnp.int32, (BOX, 128), 1) < BOX, mask, 0.0)
    area = jnp.sum(mask)
    intensity_scale = 1.0 / (SIDE * SIDE * area)
    dph[0:BOX, :] = mask

    for j in peers:
        remote(rows8(coef_send, j), rows8(coef_recv, j), coef_ss.at[j], coef_rs.at[j], at(j, z)).wait_recv()
    weights = coef_recv[pl.ds(0, GROUP, stride=8), :]
    w0 = weights.astype(bf16).astype(f32)
    w1 = (weights - w0).astype(bf16).astype(f32)
    w2 = weights - w0 - w1
    weights = jnp.concatenate([lanes(w, w[:, :MODES]) for w in (w0, w1, w2)]).astype(bf16)

    starts = [divmod(SIDE * r + LOW, 128) for r in range(8)]

    def pupils(g, carry):
        ph = mm(weights, base3[:, pl.ds(pl.multiple_of(g * PERIOD, 128), PERIOD)])
        ph = ph[0:8] + (ph[8:16] + ph[16:24])
        rows = []
        for tile, off in starts:
            x = ph[:, tile * 128 : tile * 128 + 128]
            if off:
                x = pltpu.roll(x, 128 - off, 1)
            if off + BOX > 128:
                y = pltpu.roll(ph[:, tile * 128 + 128 : tile * 128 + 256], 128 - off, 1)
                x = jnp.where(lane < 128 - off, x, y)
            rows.append(x)
        m = dph[pl.ds(pl.multiple_of(g * 8, 8), 8), :]
        m = jnp.concatenate([jnp.broadcast_to(m[r : r + 1], (8, 128)) for r in range(8)])
        sine, cosine = sine_cosine(jnp.concatenate(rows))
        at_g = pl.ds(pl.multiple_of(g * 64, 64), 64)
        pre[at_g, :] = m * cosine
        pim[at_g, :] = m * sine
        return carry

    lax.fori_loop(0, BOX // 8, pupils, 0, unroll=5)

    def of_frame(ref, f):
        return ref[pl.ds(f, BOX, stride=GROUP), :]

    def fold(x):
        return x[:BOX] + x[BOX:], x[:BOX] - x[BOX:]

    def stack(*parts):
        return jnp.concatenate(parts)

    def transfers(n, carry):
        fs = [n * UNROLL + m for m in range(UNROLL)]
        rows = []
        for f in fs:
            y = from_left("pupil_rows", lanes(of_frame(pre, f), of_frame(pim, f)))
            cr, ci, sr, si = y[:BOX, :128], y[:BOX, 128:], y[BOX:, :128], y[BOX:, 128:]
            rows += [cr + si, cr - si, ci - sr, ci + sr]
        y = from_right(stack(*rows), "pupil_columns")
        even, odd = [], []
        for m, f in enumerate(fs):
            r, i = y[4 * m * BOX : (4 * m + 2) * BOX], y[(4 * m + 2) * BOX : (4 * m + 4) * BOX]
            p_re, p_im = r[:, :128] + i[:, 128:], i[:, :128] - r[:, 128:]
            m_re, m_im = r[:, :128] - i[:, 128:], i[:, :128] + r[:, 128:]
            fpr[f], fpi[f], fmr[f], fmi[f] = p_re, p_im, m_re, m_im
            plus = (p_re * p_re + p_im * p_im) * intensity_scale
            minus = (m_re * m_re + m_im * m_im) * intensity_scale
            even += fold(plus + minus)
            odd += fold(plus - minus)
        x_re = from_right(stack(*even), "focal_columns", 0)
        x_im = from_right(stack(*odd), "focal_columns", 1)
        for m, f in enumerate(fs):
            x = lanes(x_re[2 * m * BOX : 2 * (m + 1) * BOX], x_im[2 * m * BOX : 2 * (m + 1) * BOX])
            c = from_left("focal_even", x[:BOX])
            s = from_left("focal_odd", x[BOX:])
            cr, ci, sr, si = c[:, :128], c[:, 128:], s[:, :128], s[:, 128:]
            tre[f] = stack(cr + si, cr - si)
            tim[f] = stack(ci - sr, ci + sr)
        return carry

    lax.fori_loop(0, GROUP // UNROLL, transfers, 0)

    for c in mine:
        c.wait()
    for j in range(GROUP):
        remote(edge_of(0, 0), halo.at[j, 1 - own_side], cross_ss.at[j], cross_rs.at[j], at(j, z, beside)).wait_recv()
    for j in peers:
        remote(edge_of(0, j), halo.at[j, own_side], own_ss.at[j], own_rs.at[j], at(j, z)).wait_recv()
    row = lax.broadcasted_iota(jnp.int32, (128, 256), 0)
    left_on = jnp.where(jnp.logical_and(strip == 0, me < 4), 0.0, 1.0)
    right_on = jnp.where(jnp.logical_and(strip == STRIPS - 1, me >= 4), 0.0, 1.0)
    rims = lanes(halo[...].reshape(128, SIDE), jnp.zeros((128, 256 - SIDE), f32))
    rims = rims * jnp.where(lax.rem(row, 16) < 8, left_on, right_on)
    rims = rims.T[:SIDE]
    for f in range(GROUP):
        turned[f] = pltpu.roll(rims, (128 - 16 * f) % 128, 1) if f else rims

    sums[...] = jnp.zeros_like(sums)

    def data(fs):
        h, r = split(stack(*[lanes(img[f], turned[f]) for f in fs]))
        x = mm3((h[:, :SIDE], r[:, :SIDE]), (table("data_columns"), table("data_columns_low")))
        n_re, n_im, power = sums[0], sums[1], sums[2]
        for m, f in enumerate(fs):
            h, r = split(x[m * SIDE : (m + 1) * SIDE])
            h = stack(h, r, h)
            y = mm(table("data_rows"), h[:256]) + mm(table("data_rows_end"), h[256:])
            cr, ci, sr, si = y[:BOX, :128], y[:BOX, 128:], y[BOX:, :128], y[BOX:, 128:]
            d_re, d_im = stack(cr + si, cr - si), stack(ci - sr, ci + sr)
            dre[f] = d_re
            dim_[f] = d_im
            t_re, t_im = tre[f], tim[f]
            n_re = n_re + (t_re * d_re + t_im * d_im)
            n_im = n_im + (t_re * d_im - t_im * d_re)
            power = power + (t_re * t_re + t_im * t_im)
        sums[0], sums[1], sums[2] = n_re, n_im, power

    def arrive(js):
        for j in js:
            remote(main_of(j), img.at[j], img_ss.at[j], img_rs.at[j], at(j, z)).wait_recv()

    arrive(close)
    data([me, *close])
    arrive(distant[:2])
    data(distant[:2])
    arrive(distant[2:])
    data(distant[2:])

    lane80 = lax.broadcasted_iota(jnp.int32, (BOX, 128), 1)
    lane40 = lax.broadcasted_iota(jnp.int32, (REST_ROWS, 128), 1)
    rest = jnp.zeros((REST_ROWS, 128), f32)
    for part in range(3):
        plus, minus = sums[part, :BOX], sums[part, BOX:]
        packed[part * BOX : (part + 1) * BOX, :] = jnp.where(lane80 < MAIN, plus, pltpu.roll(minus, MAIN, 1))
        for sign, x in enumerate((plus, minus)):
            j = (2 * part + sign) * REST
            x = pltpu.roll(x[:REST_ROWS], (j - MAIN) % 128, 1)
            rest = jnp.where(jnp.logical_and(lane40 >= j, lane40 < j + REST), x, rest)
    packed[3 * BOX :, :] = rest
    for d in range(DEPTH):
        for part in range(3):
            sum_send[d, part * CHUNK : (part + 1) * CHUNK, :] = packed[
                part * BOX + d * CHUNK : part * BOX + (d + 1) * CHUNK, :
            ]
        sum_send[d, 3 * CHUNK :, :] = packed[3 * BOX + d * REST_CHUNK : 3 * BOX + (d + 1) * REST_CHUNK, :]
    for d in FAR_FIRST:
        t = lax.rem(z + d, DEPTH)
        c = remote(sum_send.at[t], sum_recv.at[z], sum_ss.at[t], sum_rs.at[z], at(me, t))
        c.start()
        sends.append(c)
    sum_recv[z] = sum_send[z]
    for d in range(1, DEPTH):
        j = lax.rem(z + DEPTH - d, DEPTH)
        remote(sum_send.at[j], sum_recv.at[j], sum_ss.at[j], sum_rs.at[j], at(me, j)).wait_recv()
    total = sum_recv[0]
    for j in range(1, DEPTH):
        total = total + sum_recv[j]
    sum_v[...] = total
    power = sum_v[2 * CHUNK : 3 * CHUNK, :] + DAMPING
    obj_send[0:CHUNK, :] = sum_v[0:CHUNK, :] / power
    obj_send[CHUNK : 2 * CHUNK, :] = sum_v[CHUNK : 2 * CHUNK, :] / power
    rest = sum_v[3 * CHUNK :, :]
    lane5 = lax.broadcasted_iota(jnp.int32, (REST_CHUNK, 128), 1)
    power = jnp.where(lane5 < 2 * REST, pltpu.roll(rest, 128 - 4 * REST, 1), pltpu.roll(rest, 128 - 2 * REST, 1))
    power = jnp.where(lane5 < 4 * REST, power, 0.0) + DAMPING
    obj_send[2 * CHUNK :, :] = rest / power
    for d in FAR_FIRST:
        t = lax.rem(z + d, DEPTH)
        c = remote(obj_send, obj_all.at[z], obj_ss.at[t], obj_rs.at[z], at(me, t))
        c.start()
        sends.append(c)
    obj_all[z] = obj_send[...]
    for d in range(1, DEPTH):
        j = lax.rem(z + DEPTH - d, DEPTH)
        remote(obj_send, obj_all.at[j], obj_ss.at[j], obj_rs.at[j], at(me, j)).wait_recv()
    for d in range(DEPTH):
        for part in range(2):
            packed[part * BOX + d * CHUNK : part * BOX + (d + 1) * CHUNK, :] = obj_all[
                d, part * CHUNK : (part + 1) * CHUNK, :
            ]
        packed[3 * BOX + d * REST_CHUNK : 3 * BOX + (d + 1) * REST_CHUNK, :] = obj_all[d, 2 * CHUNK :, :]
    rest = packed[3 * BOX :, :]
    for part, ref in enumerate((ore, oim)):
        main = packed[part * BOX : (part + 1) * BOX, :]
        for sign in range(2):
            j = (2 * part + sign) * REST
            x = stack(pltpu.roll(rest, (MAIN - j) % 128, 1), jnp.zeros((BOX - REST_ROWS, 128), f32))
            x = jnp.where(lane80 < HALF, x, 0.0)
            ref[sign * BOX : (sign + 1) * BOX, :] = jnp.where(
                lane80 < MAIN, pltpu.roll(main, MAIN, 1) if sign else main, x
            )

    scale = 2.0 / (SIDE * SIDE)

    def back(n, carry):
        fs = [n * UNROLL + m for m in range(UNROLL)]
        o_re, o_im = ore[...], oim[...]
        h_re, h_im = [], []
        for f in fs:
            t_re, t_im = tre[f], tim[f]
            e_re = dre[f] - (o_re * t_re - o_im * t_im)
            e_im = dim_[f] - (o_re * t_im + o_im * t_re)
            re_even, re_odd = fold(-scale * (e_re * o_re + e_im * o_im))
            im_even, im_odd = fold(scale * (e_re * o_im - e_im * o_re))
            c = from_left("focal_even", lanes(re_even, im_even))
            s = from_left("focal_odd", lanes(re_odd, im_odd))
            cr, ci, sr, si = c[:, :128], c[:, 128:], s[:, :128], s[:, 128:]
            h_re += [cr - si, cr + si]
            h_im += [ci + sr, ci - sr]
        even = from_right(stack(*h_re), "focal_columns", 0) * (4.0 * intensity_scale)
        odd = from_right(stack(*h_im), "focal_columns", 1) * (4.0 * intensity_scale)
        sum_rows, gap_rows = [], []
        for m, f in enumerate(fs):
            at_m = slice(2 * m * BOX, 2 * (m + 1) * BOX)
            plus, minus = even[at_m] + odd[at_m], even[at_m] - odd[at_m]
            p_re, p_im, m_re, m_im = plus * fpr[f], plus * fpi[f], minus * fmr[f], minus * fmi[f]
            sum_rows += [p_re + m_re, p_im + m_im]
            gap_rows += [p_re - m_re, p_im - m_im]
        qc = from_right(stack(*sum_rows), "back_columns", 0)
        qs = from_right(stack(*gap_rows), "back_columns", 1)
        for m, f in enumerate(fs):
            at_re, at_im = slice(4 * m * BOX, (4 * m + 2) * BOX), slice((4 * m + 2) * BOX, (4 * m + 4) * BOX)
            re_even, re_odd = fold(qc[at_re] - qs[at_im])
            im_even, im_odd = fold(qc[at_im] + qs[at_re])
            c = from_left("back_even", lanes(re_even, im_even))
            s = from_left("back_odd", lanes(re_odd, im_odd))
            g_re, g_im = c[:, :128] - s[:, 128:], c[:, 128:] + s[:, :128]
            dph[pl.ds(f, BOX, stride=GROUP), :] = of_frame(pre, f) * g_im - of_frame(pim, f) * g_re
        return carry

    lax.fori_loop(0, GROUP // UNROLL, back, 0)

    def project(g, total):
        tiles = [jnp.zeros((8, 128), f32) for _ in range(9)]
        for r, (tile, off) in enumerate(starts):
            x = dph[pl.ds(pl.multiple_of(g * 64, 64) + 8 * r, 8), :]
            if off:
                x = pltpu.roll(x, off, 1)
            if off + BOX > 128:
                tiles[tile + 1] += jnp.where(lane < off, x, 0.0)
                x = jnp.where(lane < off, 0.0, x)
            tiles[tile] += x
        x = jnp.concatenate(split(lanes(*tiles)))
        modes = base3[0 : 2 * MODES, pl.ds(pl.multiple_of(g * PERIOD, 128), PERIOD)]
        return total + lax.dot_general(x, modes, (((1,), (1,)), ((), ())), preferred_element_type=f32)

    total = lax.fori_loop(0, BOX // 8, project, jnp.zeros((16, 128), f32), unroll=5)
    total = total[:8] + total[8:]
    gradient = total + pltpu.roll(total, MODES, 1)

    for j in range(GROUP):
        ret_send[j] = gradient[j : j + 1]
    part_send[0] = jnp.sum(gradient, axis=0, keepdims=True)

    groups = list(zip([*peers, me], (3, 2, 2, 2, 1, 1, 1, 0)))
    depths = [(z, 0)] + [(lax.rem(z + d, DEPTH), min(d, DEPTH - d)) for d in range(1, DEPTH)]
    ways = [(a + b, group, depth) for group, a in groups for depth, b in depths if a + b]
    for _, group, depth in sorted(ways, key=lambda way: -way[0]):
        remote(part_send, part_recv.at[pl.ds(place, 1)], part_sem.at[0], part_sem.at[1], at(group, depth)).start()
    for t in peers:
        c = remote(ret_send.at[t], ret_recv.at[me], ret_ss.at[t], ret_rs.at[me], at(t, z))
        c.start()
        sends.append(c)
    part_recv[place] = part_send[0]
    ret_recv[me] = ret_send[me]

    r_at = lax.broadcasted_iota(jnp.int32, (2 * SIDE, 2 * BOX), 0)
    c_at = lax.broadcasted_iota(jnp.int32, (2 * SIDE, 2 * BOX), 1)
    mirrored = r_at >= SIDE
    k = jnp.where(mirrored, r_at - SIDE, r_at)
    minus = (k >= HALF) != mirrored
    k = jnp.where(k >= HALF, SIDE - k, k) + jnp.where(minus, BOX, 0)
    pick_rows = jnp.where(k == c_at, 1.0, 0.0).astype(bf16)
    r_at = lax.broadcasted_iota(jnp.int32, (128, 256), 0)
    c_at = lax.broadcasted_iota(jnp.int32, (128, 256), 1)
    flip_columns = jnp.where(
        jnp.logical_and(r_at + c_at == SIDE, jnp.logical_and(c_at >= HALF, c_at < SIDE)), 1.0, 0.0
    ).astype(bf16)
    parts = [mm(pick_rows, part) for part in split(lanes(ore[...], oim[...]))]
    lane_full = lax.broadcasted_iota(jnp.int32, (SIDE, 128), 1)
    for n, sign in ((0, 1.0), (1, -1.0)):
        at_n = slice(n * 128, n * 128 + 128)
        half = parts[0][:SIDE, at_n] + parts[1][:SIDE, at_n]
        mirror = [mm(part[SIDE:, at_n].astype(bf16), flip_columns) for part in parts]
        mirror = sign * (mirror[0] + mirror[1])
        full[2 * n] = jnp.where(lane_full < HALF, half, mirror[:, :128])
        full[2 * n + 1] = mirror[:, 128:]
    first_row = z * 9 // 4
    for n in range(2):
        placed = [jnp.zeros((8, 128), f32) for _ in range(6)]
        for t in range(3):
            for piece in range(2):
                x = full[2 * n + piece, pl.ds(first_row + t, GROUP, stride=SIDE // GROUP), :]
                tile, off = divmod(SIDE * t + 128 * piece, 128)
                if off:
                    x = pltpu.roll(x, off, 1)
                    placed[tile + 1] += jnp.where(lane < off, x, 0.0)
                    x = jnp.where(lane < off, 0.0, x)
                placed[tile] += x
        placed = lanes(*placed)
        picked = jnp.zeros((8, 384), f32)
        for m in range(4):
            moved = pltpu.roll(placed, 768 - 36 * m, 1) if m else placed
            picked = picked + jnp.where(lax.rem(z, 4) == m, 1.0, 0.0) * moved[:, :384]
        for i in range(GROUP):
            out_send[i, n : n + 1, :] = picked[i : i + 1]
    for t in peers:
        c = remote(out_send.at[t], out_recv.at[me], out_ss.at[t], out_rs.at[me], at(t, z))
        c.start()
        sends.append(c)
    out_recv[me] = out_send[me]

    for j in peers:
        remote(out_send.at[j], out_recv.at[j], out_ss.at[j], out_rs.at[j], at(j, z)).wait_recv()
    for p in range(GROUP):
        object_out[p] = out_recv[p, 0:2, :SHARE]
    for j in peers:
        remote(ret_send.at[j], ret_recv.at[j], ret_ss.at[j], ret_rs.at[j], at(j, z)).wait_recv()
    arrived = part_recv.at[pl.ds(0, FRAMES - 1)]
    arrived = remote(arrived, arrived, part_sem.at[0], part_sem.at[1], at(peers[0], z))
    arrived.wait_recv()
    for p in range(GROUP):
        mean = part_recv[p * DEPTH]
        for n in range(1, DEPTH):
            mean = mean + part_recv[p * DEPTH + n]
        gradient_out[0, p : p + 1, :] = (ret_recv[p] - mean * (1.0 / FRAMES))[:, :MODES]
    arrived.wait_send()
    for c in sends:
        c.wait_send()


def body(sky_image, coefficients, mode_basis, aperture):
    vmem, dma = pltpu.VMEM, pltpu.SemaphoreType.DMA
    scratch = [
        vmem(TABLE.shape, bf16), vmem((640, 256), f32), vmem((GROUP, MODES), f32),
        vmem((64, 128), f32), vmem((64, 128), f32), vmem((SIDE, SIDE), jnp.int32), vmem((MODES, FLAT), f32),
        vmem((3 * MODES, FLAT), bf16),
        vmem((4, 4, 8, SIDE), f32), vmem((GROUP, SIDE, 128), f32), vmem((GROUP, 2, 8, SIDE), f32),
        vmem((GROUP, SIDE, 128), f32), vmem((8 * BOX, 128), f32), vmem((8 * BOX, 128), f32),
        *[vmem((GROUP, 2 * BOX, 128), f32)] * 8,
        vmem((3, 2 * BOX, 128), f32), vmem((3 * BOX + REST_ROWS, 128), f32),
        vmem((DEPTH, SUMS, 128), f32), vmem((DEPTH, SUMS, 128), f32), vmem((SUMS, 128), f32),
        vmem((OBJECTS, 128), f32), vmem((DEPTH, OBJECTS, 128), f32), vmem((2 * BOX, 128), f32), vmem((2 * BOX, 128), f32),
        vmem((8 * BOX, 128), f32), vmem((4, SIDE, 128), f32), vmem((GROUP, 8, 384), f32), vmem((GROUP, 8, 384), f32),
        vmem((1, 1, 128), f32), vmem((FRAMES, 1, 128), f32), vmem((GROUP, 1, 128), f32), vmem((GROUP, 1, 128), f32),
        *[dma((8,))] * 17, dma((2,)),
    ]
    return pl.pallas_call(
        kernel,
        out_shape=(
            pltpu.VMEM((1, GROUP, MODES), f32),
            pltpu.VMEM((GROUP, 2, SHARE), f32),
        ),
        in_specs=[pl.BlockSpec(memory_space=pl.ANY)] * 5,
        out_specs=[pl.BlockSpec(memory_space=pltpu.VMEM)] * 2,
        scratch_shapes=scratch,
        compiler_params=pltpu.CompilerParams(collective_id=0, has_side_effects=True, vmem_limit_bytes=60 * 2**20),
    )(sky_image, coefficients, mode_basis, aperture, jnp.asarray(TABLE))


def solution(mesh):
    in_specs = (P("frame", None, "patch"), P("frame", "patch", None), P(), P())
    out_specs = (P("frame", "patch", None), P("patch", None, "frame"))
    return jax.shard_map(body, mesh=mesh, in_specs=in_specs, out_specs=out_specs, check_vma=False)
```

```python
import math

import jax
import jax.numpy as jnp
import ml_dtypes
import numpy as np
from jax import lax
from jax.experimental import pallas as pl
from jax.experimental.pallas import tpu as pltpu
from jax.sharding import PartitionSpec as P

SIDE = 144
RIM = 8
TILE = SIDE - 2 * RIM
LOW, BOX = 32, 80
GROUP = 8
DEPTH = 8
STRIPS = 4
FRAMES = GROUP * DEPTH
HALF = SIDE // 2 + 1
FOLD = BOX // 2
CHUNK = FOLD // DEPTH
FLAT = BOX * SIDE
PERIOD = 8 * SIDE
MODES = 64
UNROLL = GROUP
SHARE = SIDE * SIDE // FRAMES
DAMPING = 0.02 * FRAMES
FAR_FIRST = (4, 3, 5, 2, 6, 1, 7)
MESH = pl.DeviceIdType.MESH
f32, bf16 = jnp.float32, jnp.bfloat16


def profile():
    at = np.arange(SIDE, dtype=np.float64)
    distance = np.minimum(at, SIDE - 1 - at)
    taper = 0.3 + 0.7 * np.sin(math.pi * (distance + 1.0) / (2.0 * (RIM + 1))) ** 2
    return np.where(distance < RIM, taper, 1.0)


def tables():
    k = np.arange(HALF)
    y = np.arange(SIDE)
    u = np.arange(BOX) + LOW - SIDE // 2
    weight = np.ones(HALF)
    weight[0] = weight[-1] = 0.5

    def pair(a, b):
        angle = 2.0 * math.pi / SIDE * (np.outer(a, b) % SIDE)
        return np.cos(angle), np.sin(angle)

    def cut(t):
        high = t.astype(ml_dtypes.bfloat16)
        return high, (t - high.astype(np.float64)).astype(ml_dtypes.bfloat16)

    def rows_of(*blocks):
        t = np.zeros((BOX * len(blocks), blocks[0].shape[1]))
        for n, block in enumerate(blocks):
            t[n * BOX : n * BOX + block.shape[0]] = block
        high, low = cut(t)
        return np.concatenate([high, high, low], axis=1)

    def columns_of(c, s):
        t = np.zeros((-(-c.shape[0] // 16) * 16, 256))
        t[: c.shape[0], : c.shape[1]], t[: c.shape[0], 128 : 128 + c.shape[1]] = c, s
        return cut(t)

    def twice(c, s):
        t = np.zeros((BOX, 256))
        t[: c.shape[0], : c.shape[1]], t[: c.shape[0], 128 : 128 + c.shape[1]] = c, s
        high, low = cut(t)
        return np.concatenate([high, high, low])

    parts = {}
    c, s = pair(k, u)
    parts["pupil_rows"] = rows_of(c, s)
    parts["pupil_columns"] = twice(c.T, s.T)
    parts["back_columns"] = twice(weight[:, None] * c, weight[:, None] * s)

    def wide(t):
        return np.pad(t, ((0, BOX - t.shape[0]), (0, BOX - t.shape[1])))

    parts["back_even"], parts["back_odd"] = rows_of(wide(c.T * weight)), rows_of(wide(s.T * weight))
    c, s = pair(k, k)
    parts["focal_columns"] = twice(weight[:, None] * c, -weight[:, None] * s)
    disc = np.concatenate([np.arange(37), [0] * 3, np.arange(72, 36, -1), [0] * 4])
    used = np.concatenate([np.ones(37), [0] * 3, np.ones(36), [0] * 4])
    parts["focal_even"] = rows_of(wide((c * weight)[disc] * used[:, None]))
    parts["focal_odd"] = rows_of(wide((s * weight)[disc] * used[:, None]))
    parts["disc_even"] = rows_of(wide((c * weight)[:, disc] * used))
    parts["disc_odd"] = rows_of(wide((s * weight)[:, disc] * used))
    w = profile()
    c, s = pair(k, y)
    t = rows_of((c * w / SIDE)[disc] * used[:, None], (s * w / SIDE)[disc] * used[:, None])
    parts["data_rows"], parts["data_rows_end"] = t[:, :256], t[:, 256:]
    order = np.concatenate([y[RIM:-RIM], y[:RIM], y[-RIM:]])
    parts["data_columns"], parts["data_columns_low"] = columns_of(
        (w[:, None] * c.T)[order], -(w[:, None] * s.T)[order]
    )
    first, rows, total = {}, [], 0
    for name, part in parts.items():
        first[name] = (total, *part.shape)
        total += part.shape[0]
        rows.append(np.pad(part, ((0, 0), (0, 256 - part.shape[1]))))
    return np.concatenate(rows), first


TABLE, FIRST = tables()


def split(x):
    high = x.astype(bf16)
    return high, (x - high.astype(f32)).astype(bf16)


def mm(a, b):
    return jnp.dot(a, b, preferred_element_type=f32)


def mm3(a, b):
    return mm(a[0], b[0]) + (mm(a[0], b[1]) + mm(a[1], b[0]))


def lanes(*parts):
    return jnp.concatenate(parts, axis=1)


def sine_cosine(x):
    quarter = jnp.floor(x * (2.0 / math.pi) + 0.5)
    r = x - quarter * 1.5703125
    r = r - quarter * 4.837512969970703125e-4
    r = r - quarter * 7.54978995489188216e-8
    z = r * r
    sine = ((-1.9515295891e-4 * z + 8.3321608736e-3) * z - 1.6666654611e-1) * z * r + r
    cosine = ((2.443315711809948e-5 * z - 1.388731625493765e-3) * z + 4.166664568298827e-2) * z * z - 0.5 * z + 1.0
    halves = jnp.floor(quarter * 0.5)
    odd = quarter - 2.0 * halves
    minus = 1.0 - 2.0 * (halves - 2.0 * jnp.floor(halves * 0.5))
    swap = odd > 0.5
    return (
        jnp.where(swap, cosine, sine) * minus,
        jnp.where(swap, -sine, cosine) * minus,
    )


def kernel(
    sky, coef, basis, aperture, table_hbm,
    gradient_out, object_out,
    tab, skyp, coef_v, coef_send, coef_recv, mask_v, base, base3,
    edges, img, halo, turned, pre, pim, fpr, fpi, fmr, fmi, tre, tim, dre, dim_,
    sums, packed, pow_send, pow_recv, sum_send, sum_recv, obj_send, obj_all, ore, oim, dph,
    full, out_send, out_recv, part_send, part_recv, ret_send, ret_recv,
    local_sem, coef_ss, coef_rs, img_ss, img_rs, own_ss, own_rs, cross_ss, cross_rs,
    pow_ss, pow_rs, sum_ss, sum_rs, obj_ss, obj_rs, out_ss, out_rs, ret_ss, ret_rs, part_sem,
):
    place, strip = lax.axis_index("frame"), lax.axis_index("patch")
    me, z = place // DEPTH, place % DEPTH

    y, x = me // 2, me % 2
    other = 1 - x
    near, far, back_y = y + 1 - 2 * (y % 2), 3 - y, (y + 2) % 4
    close = [near * 2 + x, far * 2 + x, y * 2 + other]
    distant = [near * 2 + other, far * 2 + other, back_y * 2 + x, back_y * 2 + other]
    peers = distant[::-1] + close[::-1]

    def at(group, depth, which=None):
        return {"frame": group * DEPTH + depth, "patch": strip if which is None else which}

    def remote(src, dst, send, recv, device):
        return pltpu.make_async_remote_copy(
            src_ref=src, dst_ref=dst, send_sem=send, recv_sem=recv, device_id=device, device_id_type=MESH
        )

    def table(name, half=None):
        row, count, width = FIRST[name]
        if half is None:
            return tab[row : row + count, :width]
        return tab[row : row + count, half * 128 : half * 128 + 128]

    def from_left(name, x):
        h, r = split(x)
        return mm(table(name), jnp.concatenate([h, r, h]))

    def from_right(x, name, half=None):
        h, r = split(x)
        return mm(lanes(h[:, :BOX], r[:, :BOX], h[:, :BOX]), table(name, half))

    loads = [
        pltpu.make_async_copy(coef.at[0], coef_v, local_sem.at[0]),
        pltpu.make_async_copy(basis.at[:, pl.ds(LOW * SIDE, FLAT)], base, local_sem.at[1]),
        pltpu.make_async_copy(sky.at[0], skyp.at[pl.ds(RIM, 512)], local_sem.at[2]),
        pltpu.make_async_copy(table_hbm, tab, local_sem.at[3]),
        pltpu.make_async_copy(aperture, mask_v, local_sem.at[4]),
    ]
    for load in loads:
        load.start()

    barrier = pltpu.get_barrier_semaphore()
    beside = lax.rem(strip + jnp.where(me < 4, STRIPS - 1, 1), STRIPS)

    def greet(device):
        pl.semaphore_signal(barrier, inc=1, device_id=device, device_id_type=MESH)

    for d in FAR_FIRST:
        greet(at(me, lax.rem(z + d, DEPTH)))
    for t in [*peers, me]:
        greet(at(t, z, beside))
    for t in peers:
        greet(at(t, z))

    skyp[pl.ds(0, RIM), :] = jnp.zeros((RIM, 256), f32)
    skyp[pl.ds(512 + RIM, 120), :] = jnp.zeros((120, 256), f32)
    loads[0].wait()
    for p in range(GROUP):
        row = coef_v[p : p + 1, :]
        coef_send[p] = lanes(row, row)
    loads[2].wait()
    for half in range(2):
        strip_t = skyp[:, half * 128 : half * 128 + 128].T
        for r in range(4):
            edges[2 * half, r] = strip_t[:8, r * TILE : r * TILE + SIDE]
            edges[2 * half + 1, r] = strip_t[120:, r * TILE : r * TILE + SIDE]
    pl.semaphore_wait(barrier, GROUP - 1 + DEPTH - 1 + GROUP)

    sends = []
    for t in peers:
        c = remote(coef_send.at[t], coef_recv.at[me], coef_ss.at[t], coef_rs.at[me], at(t, z))
        c.start()
        sends.append(c)
    coef_recv[me] = coef_send[me]

    def main_of(t):
        return skyp.at[
            pl.ds(pl.multiple_of(lax.rem(t, 4) * TILE, TILE), SIDE), pl.ds(pl.multiple_of((t // 4) * 128, 128), 128)
        ]

    def edge_of(kind, t):
        return edges.at[kind, lax.rem(t, 4)]

    for t in peers:
        kind, side = jnp.where(t < 4, 2, 1), jnp.where(t < 4, 1, 0)
        c = remote(edge_of(kind, t), halo.at[me, side], own_ss.at[t], own_rs.at[me], at(t, z))
        c.start()
        sends.append(c)
    for p in range(GROUP):
        kind, side, step = (3, 0, 1) if p < 4 else (0, 1, STRIPS - 1)
        c = remote(
            edge_of(kind, p), halo.at[me, side], cross_ss.at[p], cross_rs.at[me],
            at(p, z, lax.rem(strip + step, STRIPS)),
        )
        c.start()
        sends.append(c)
    for t in close + distant:
        c = remote(main_of(t), img.at[me], img_ss.at[t], img_rs.at[me], at(t, z))
        c.start()
        sends.append(c)
    own_side = jnp.where(me < 4, 1, 0)
    mine = [
        pltpu.make_async_copy(main_of(me), img.at[me], local_sem.at[6]),
        pltpu.make_async_copy(edge_of(jnp.where(me < 4, 2, 1), me), halo.at[me, own_side], local_sem.at[7]),
    ]
    for c in mine:
        c.start()

    loads[1].wait()

    def cut(g, carry):
        at_g = pl.ds(pl.multiple_of(g * PERIOD, 128), PERIOD)
        x = base[:, at_g]
        h, r = split(x)
        base3[0:MODES, at_g] = h
        base3[MODES : 2 * MODES, at_g] = r
        base3[2 * MODES :, at_g] = (x - h.astype(f32) - r.astype(f32)).astype(bf16)
        return carry

    lax.fori_loop(0, BOX // 8, cut, 0)
    for load in loads[3:]:
        load.wait()

    lane = lax.broadcasted_iota(jnp.int32, (8, 128), 1)
    mask = mask_v[LOW : LOW + BOX, 0:128].astype(f32)
    mask = pltpu.roll(mask, 128 - LOW, 1)
    mask = jnp.where(lax.broadcasted_iota(jnp.int32, (BOX, 128), 1) < BOX, mask, 0.0)
    area = jnp.sum(mask)
    intensity_scale = 1.0 / (SIDE * SIDE * area)
    dph[0:BOX, :] = mask

    for j in peers:
        remote(coef_send.at[j], coef_recv.at[j], coef_ss.at[j], coef_rs.at[j], at(j, z)).wait_recv()
    weights = jnp.concatenate([coef_recv[j] for j in range(GROUP)])
    w0 = weights.astype(bf16).astype(f32)
    w1 = (weights - w0).astype(bf16).astype(f32)
    w2 = weights - w0 - w1
    weights = jnp.concatenate([lanes(w, w[:, :MODES]) for w in (w0, w1, w2)]).astype(bf16)

    starts = [divmod(SIDE * r + LOW, 128) for r in range(8)]

    def pupils(g, carry):
        ph = mm(weights, base3[:, pl.ds(pl.multiple_of(g * PERIOD, 128), PERIOD)])
        ph = ph[0:8] + (ph[8:16] + ph[16:24])
        rows = []
        for tile, off in starts:
            x = ph[:, tile * 128 : tile * 128 + 128]
            if off:
                x = pltpu.roll(x, 128 - off, 1)
            if off + BOX > 128:
                y = pltpu.roll(ph[:, tile * 128 + 128 : tile * 128 + 256], 128 - off, 1)
                x = jnp.where(lane < 128 - off, x, y)
            rows.append(x)
        m = dph[pl.ds(pl.multiple_of(g * 8, 8), 8), :]
        m = jnp.concatenate([jnp.broadcast_to(m[r : r + 1], (8, 128)) for r in range(8)])
        sine, cosine = sine_cosine(jnp.concatenate(rows))
        at_g = pl.ds(pl.multiple_of(g * 64, 64), 64)
        pre[at_g, :] = m * cosine
        pim[at_g, :] = m * sine
        return carry

    lax.fori_loop(0, BOX // 8, pupils, 0, unroll=5)

    def of_frame(ref, f):
        return ref[pl.ds(f, BOX, stride=GROUP), :]

    def fold(x):
        return x[:BOX] + x[BOX:], x[:BOX] - x[BOX:]

    def stack(*parts):
        return jnp.concatenate(parts)

    def transfers(n, carry):
        fs = [n * UNROLL + m for m in range(UNROLL)]
        rows = []
        for f in fs:
            y = from_left("pupil_rows", lanes(of_frame(pre, f), of_frame(pim, f)))
            cr, ci, sr, si = y[:BOX, :128], y[:BOX, 128:], y[BOX:, :128], y[BOX:, 128:]
            rows += [cr + si, cr - si, ci - sr, ci + sr]
        y = from_right(stack(*rows), "pupil_columns")
        even, odd = [], []
        for m, f in enumerate(fs):
            r, i = y[4 * m * BOX : (4 * m + 2) * BOX], y[(4 * m + 2) * BOX : (4 * m + 4) * BOX]
            p_re, p_im = r[:, :128] + i[:, 128:], i[:, :128] - r[:, 128:]
            m_re, m_im = r[:, :128] - i[:, 128:], i[:, :128] + r[:, 128:]
            fpr[f], fpi[f], fmr[f], fmi[f] = p_re, p_im, m_re, m_im
            plus = (p_re * p_re + p_im * p_im) * intensity_scale
            minus = (m_re * m_re + m_im * m_im) * intensity_scale
            even += fold(plus + minus)
            odd += fold(plus - minus)
        x_re = from_right(stack(*even), "focal_columns", 0)
        x_im = from_right(stack(*odd), "focal_columns", 1)
        for m, f in enumerate(fs):
            x = lanes(x_re[2 * m * BOX : 2 * (m + 1) * BOX], x_im[2 * m * BOX : 2 * (m + 1) * BOX])
            c = from_left("focal_even", x[:BOX])
            s = from_left("focal_odd", x[BOX:])
            cr, ci, sr, si = c[:, :128], c[:, 128:], s[:, :128], s[:, 128:]
            tre[f] = stack(cr + si, cr - si)
            tim[f] = stack(ci - sr, ci + sr)
        return carry

    lax.fori_loop(0, GROUP // UNROLL, transfers, 0)

    lane40 = lax.broadcasted_iota(jnp.int32, (FOLD, 128), 1)
    row40 = lax.broadcasted_iota(jnp.int32, (FOLD, 128), 0)
    border = jnp.where(row40 < 24, 73, jnp.where(row40 < 32, 68, 65))

    def shifted(x, back):
        return stack(*[
            pltpu.roll(x[a:b], 128 - by if back else by, 1) for a, b, by in ((0, 24, 73), (24, 32, 68), (32, 40, 65))
        ])

    def pack(x, into, at_row):
        for sign in range(2):
            wide, narrow = x[sign * BOX : sign * BOX + FOLD], x[sign * BOX + FOLD : (sign + 1) * BOX]
            packed[...] = jnp.where(lane40 < border, wide, shifted(narrow, False))
            for d in range(DEPTH):
                into[d, at_row + sign * CHUNK : at_row + (sign + 1) * CHUNK, :] = packed[d * CHUNK : (d + 1) * CHUNK, :]

    power = jnp.zeros((2 * BOX, 128), f32)
    for f in range(GROUP):
        power = power + (tre[f] * tre[f] + tim[f] * tim[f])
    pack(power, pow_send, 0)
    for d in FAR_FIRST:
        t = lax.rem(z + d, DEPTH)
        c = remote(pow_send.at[t], pow_recv.at[z], pow_ss.at[t], pow_rs.at[z], at(me, t))
        c.start()
        sends.append(c)
    pow_recv[z] = pow_send[z]

    for c in mine:
        c.wait()
    for j in range(GROUP):
        remote(edge_of(0, 0), halo.at[j, 1 - own_side], cross_ss.at[j], cross_rs.at[j], at(j, z, beside)).wait_recv()
    for j in peers:
        remote(edge_of(0, j), halo.at[j, own_side], own_ss.at[j], own_rs.at[j], at(j, z)).wait_recv()
    row = lax.broadcasted_iota(jnp.int32, (128, 256), 0)
    left_on = jnp.where(jnp.logical_and(strip == 0, me < 4), 0.0, 1.0)
    right_on = jnp.where(jnp.logical_and(strip == STRIPS - 1, me >= 4), 0.0, 1.0)
    rims = lanes(halo[...].reshape(128, SIDE), jnp.zeros((128, 256 - SIDE), f32))
    rims = rims * jnp.where(lax.rem(row, 16) < 8, left_on, right_on)
    rims = rims.T[:SIDE]
    for f in range(GROUP):
        turned[f] = pltpu.roll(rims, (128 - 16 * f) % 128, 1) if f else rims

    sums[...] = jnp.zeros_like(sums)

    def data(fs):
        h, r = split(stack(*[lanes(img[f], turned[f]) for f in fs]))
        x = mm3((h[:, :SIDE], r[:, :SIDE]), (table("data_columns"), table("data_columns_low")))
        n_re, n_im = sums[0], sums[1]
        for m, f in enumerate(fs):
            h, r = split(x[m * SIDE : (m + 1) * SIDE])
            h = stack(h, r, h)
            y = mm(table("data_rows"), h[:256]) + mm(table("data_rows_end"), h[256:])
            cr, ci, sr, si = y[:BOX, :128], y[:BOX, 128:], y[BOX:, :128], y[BOX:, 128:]
            d_re, d_im = stack(cr + si, cr - si), stack(ci - sr, ci + sr)
            dre[f] = d_re
            dim_[f] = d_im
            t_re, t_im = tre[f], tim[f]
            n_re = n_re + (t_re * d_re + t_im * d_im)
            n_im = n_im + (t_re * d_im - t_im * d_re)
        sums[0], sums[1] = n_re, n_im

    def arrive(js):
        for j in js:
            remote(main_of(j), img.at[j], img_ss.at[j], img_rs.at[j], at(j, z)).wait_recv()

    arrive(close)
    data([me, *close])
    arrive(distant[:2])
    data(distant[:2])
    arrive(distant[2:])
    data(distant[2:])

    pack(sums[0], sum_send, 0)
    pack(sums[1], sum_send, 2 * CHUNK)
    for d in FAR_FIRST:
        t = lax.rem(z + d, DEPTH)
        c = remote(sum_send.at[t], sum_recv.at[z], sum_ss.at[t], sum_rs.at[z], at(me, t))
        c.start()
        sends.append(c)
    sum_recv[z] = sum_send[z]
    for d in range(1, DEPTH):
        j = lax.rem(z + DEPTH - d, DEPTH)
        remote(pow_send.at[j], pow_recv.at[j], pow_ss.at[j], pow_rs.at[j], at(me, j)).wait_recv()
    power = pow_recv[0]
    for j in range(1, DEPTH):
        power = power + pow_recv[j]
    power = power + DAMPING
    for d in range(1, DEPTH):
        j = lax.rem(z + DEPTH - d, DEPTH)
        remote(sum_send.at[j], sum_recv.at[j], sum_ss.at[j], sum_rs.at[j], at(me, j)).wait_recv()
    total = sum_recv[0]
    for j in range(1, DEPTH):
        total = total + sum_recv[j]
    obj_send[...] = total / stack(power, power)
    for d in FAR_FIRST:
        t = lax.rem(z + d, DEPTH)
        c = remote(obj_send, obj_all.at[z], obj_ss.at[t], obj_rs.at[z], at(me, t))
        c.start()
        sends.append(c)
    obj_all[z] = obj_send[...]
    for d in range(1, DEPTH):
        j = lax.rem(z + DEPTH - d, DEPTH)
        remote(obj_send, obj_all.at[j], obj_ss.at[j], obj_rs.at[j], at(me, j)).wait_recv()
    for part, ref in enumerate((ore, oim)):
        for sign in range(2):
            at_row = (2 * part + sign) * CHUNK
            for d in range(DEPTH):
                packed[d * CHUNK : (d + 1) * CHUNK, :] = obj_all[d, at_row : at_row + CHUNK, :]
            x = packed[...]
            ref[sign * BOX : sign * BOX + FOLD, :] = jnp.where(lane40 < jnp.minimum(border, HALF), x, 0.0)
            ref[sign * BOX + FOLD : (sign + 1) * BOX, :] = jnp.where(lane40 < 128 - border, shifted(x, True), 0.0)

    scale = 2.0 / (SIDE * SIDE)

    def back(n, carry):
        fs = [n * UNROLL + m for m in range(UNROLL)]
        o_re, o_im = ore[...], oim[...]
        h_re, h_im = [], []
        for f in fs:
            t_re, t_im = tre[f], tim[f]
            e_re = dre[f] - (o_re * t_re - o_im * t_im)
            e_im = dim_[f] - (o_re * t_im + o_im * t_re)
            re_even, re_odd = fold(-scale * (e_re * o_re + e_im * o_im))
            im_even, im_odd = fold(scale * (e_re * o_im - e_im * o_re))
            c = from_left("disc_even", lanes(re_even, im_even))
            s = from_left("disc_odd", lanes(re_odd, im_odd))
            cr, ci, sr, si = c[:, :128], c[:, 128:], s[:, :128], s[:, 128:]
            h_re += [cr - si, cr + si]
            h_im += [ci + sr, ci - sr]
        even = from_right(stack(*h_re), "focal_columns", 0) * (4.0 * intensity_scale)
        odd = from_right(stack(*h_im), "focal_columns", 1) * (4.0 * intensity_scale)
        sum_rows, gap_rows = [], []
        for m, f in enumerate(fs):
            at_m = slice(2 * m * BOX, 2 * (m + 1) * BOX)
            plus, minus = even[at_m] + odd[at_m], even[at_m] - odd[at_m]
            p_re, p_im, m_re, m_im = plus * fpr[f], plus * fpi[f], minus * fmr[f], minus * fmi[f]
            sum_rows += [p_re + m_re, p_im + m_im]
            gap_rows += [p_re - m_re, p_im - m_im]
        qc = from_right(stack(*sum_rows), "back_columns", 0)
        qs = from_right(stack(*gap_rows), "back_columns", 1)
        for m, f in enumerate(fs):
            at_re, at_im = slice(4 * m * BOX, (4 * m + 2) * BOX), slice((4 * m + 2) * BOX, (4 * m + 4) * BOX)
            re_even, re_odd = fold(qc[at_re] - qs[at_im])
            im_even, im_odd = fold(qc[at_im] + qs[at_re])
            c = from_left("back_even", lanes(re_even, im_even))
            s = from_left("back_odd", lanes(re_odd, im_odd))
            g_re, g_im = c[:, :128] - s[:, 128:], c[:, 128:] + s[:, :128]
            dph[pl.ds(f, BOX, stride=GROUP), :] = of_frame(pre, f) * g_im - of_frame(pim, f) * g_re
        return carry

    lax.fori_loop(0, GROUP // UNROLL, back, 0)

    def project(g, total):
        tiles = [jnp.zeros((8, 128), f32) for _ in range(9)]
        for r, (tile, off) in enumerate(starts):
            x = dph[pl.ds(pl.multiple_of(g * 64, 64) + 8 * r, 8), :]
            if off:
                x = pltpu.roll(x, off, 1)
            if off + BOX > 128:
                tiles[tile + 1] += jnp.where(lane < off, x, 0.0)
                x = jnp.where(lane < off, 0.0, x)
            tiles[tile] += x
        x = jnp.concatenate(split(lanes(*tiles)))
        modes = base3[0 : 2 * MODES, pl.ds(pl.multiple_of(g * PERIOD, 128), PERIOD)]
        return total + lax.dot_general(x, modes, (((1,), (1,)), ((), ())), preferred_element_type=f32)

    total = lax.fori_loop(0, BOX // 8, project, jnp.zeros((16, 128), f32), unroll=5)
    total = total[:8] + total[8:]
    gradient = total + pltpu.roll(total, MODES, 1)

    for j in range(GROUP):
        ret_send[j] = gradient[j : j + 1]
    part_send[0] = jnp.sum(gradient, axis=0, keepdims=True)

    groups = list(zip([*peers, me], (3, 2, 2, 2, 1, 1, 1, 0)))
    depths = [(z, 0)] + [(lax.rem(z + d, DEPTH), min(d, DEPTH - d)) for d in range(1, DEPTH)]
    ways = [(a + b, group, depth) for group, a in groups for depth, b in depths if a + b]
    for _, group, depth in sorted(ways, key=lambda way: -way[0]):
        remote(part_send, part_recv.at[pl.ds(place, 1)], part_sem.at[0], part_sem.at[1], at(group, depth)).start()
    for t in peers:
        c = remote(ret_send.at[t], ret_recv.at[me], ret_ss.at[t], ret_rs.at[me], at(t, z))
        c.start()
        sends.append(c)
    part_recv[place] = part_send[0]
    ret_recv[me] = ret_send[me]

    r_at = lax.broadcasted_iota(jnp.int32, (2 * SIDE, 2 * BOX), 0)
    c_at = lax.broadcasted_iota(jnp.int32, (2 * SIDE, 2 * BOX), 1)
    mirrored = r_at >= SIDE
    k = jnp.where(mirrored, r_at - SIDE, r_at)
    minus = (k >= HALF) != mirrored
    k = jnp.where(k >= HALF, SIDE - k, k)
    k = jnp.where(k > 36, FOLD + 72 - k, k) + jnp.where(minus, BOX, 0)
    pick_rows = jnp.where(k == c_at, 1.0, 0.0).astype(bf16)
    r_at = lax.broadcasted_iota(jnp.int32, (128, 256), 0)
    c_at = lax.broadcasted_iota(jnp.int32, (128, 256), 1)
    flip_columns = jnp.where(
        jnp.logical_and(r_at + c_at == SIDE, jnp.logical_and(c_at >= HALF, c_at < SIDE)), 1.0, 0.0
    ).astype(bf16)
    parts = [mm(pick_rows, part) for part in split(lanes(ore[...], oim[...]))]
    lane_full = lax.broadcasted_iota(jnp.int32, (SIDE, 128), 1)
    for n, sign in ((0, 1.0), (1, -1.0)):
        at_n = slice(n * 128, n * 128 + 128)
        half = parts[0][:SIDE, at_n] + parts[1][:SIDE, at_n]
        mirror = [mm(part[SIDE:, at_n].astype(bf16), flip_columns) for part in parts]
        mirror = sign * (mirror[0] + mirror[1])
        full[2 * n] = jnp.where(lane_full < HALF, half, mirror[:, :128])
        full[2 * n + 1] = mirror[:, 128:]
    first_row = z * 9 // 4
    for n in range(2):
        placed = [jnp.zeros((8, 128), f32) for _ in range(6)]
        for t in range(3):
            for piece in range(2):
                x = full[2 * n + piece, pl.ds(first_row + t, GROUP, stride=SIDE // GROUP), :]
                tile, off = divmod(SIDE * t + 128 * piece, 128)
                if off:
                    x = pltpu.roll(x, off, 1)
                    placed[tile + 1] += jnp.where(lane < off, x, 0.0)
                    x = jnp.where(lane < off, 0.0, x)
                placed[tile] += x
        placed = lanes(*placed)
        picked = jnp.zeros((8, 384), f32)
        for m in range(4):
            moved = pltpu.roll(placed, 768 - 36 * m, 1) if m else placed
            picked = picked + jnp.where(lax.rem(z, 4) == m, 1.0, 0.0) * moved[:, :384]
        for i in range(GROUP):
            out_send[i, n : n + 1, :] = picked[i : i + 1]
    for t in peers:
        c = remote(out_send.at[t], out_recv.at[me], out_ss.at[t], out_rs.at[me], at(t, z))
        c.start()
        sends.append(c)
    out_recv[me] = out_send[me]

    for j in peers:
        remote(out_send.at[j], out_recv.at[j], out_ss.at[j], out_rs.at[j], at(j, z)).wait_recv()
    for p in range(GROUP):
        object_out[p] = out_recv[p, 0:2, :SHARE]
    for j in peers:
        remote(ret_send.at[j], ret_recv.at[j], ret_ss.at[j], ret_rs.at[j], at(j, z)).wait_recv()
    arrived = part_recv.at[pl.ds(0, FRAMES - 1)]
    arrived = remote(arrived, arrived, part_sem.at[0], part_sem.at[1], at(peers[0], z))
    arrived.wait_recv()
    for p in range(GROUP):
        mean = part_recv[p * DEPTH]
        for n in range(1, DEPTH):
            mean = mean + part_recv[p * DEPTH + n]
        gradient_out[0, p : p + 1, :] = (ret_recv[p] - mean * (1.0 / FRAMES))[:, :MODES]
    arrived.wait_send()
    for c in sends:
        c.wait_send()


def body(sky_image, coefficients, mode_basis, aperture):
    vmem, dma = pltpu.VMEM, pltpu.SemaphoreType.DMA
    scratch = [
        vmem(TABLE.shape, bf16), vmem((640, 256), f32), vmem((GROUP, MODES), f32),
        vmem((GROUP, 1, 128), f32), vmem((GROUP, 1, 128), f32), vmem((SIDE, SIDE), jnp.int32), vmem((MODES, FLAT), f32),
        vmem((3 * MODES, FLAT), bf16),
        vmem((4, 4, 8, SIDE), f32), vmem((GROUP, SIDE, 128), f32), vmem((GROUP, 2, 8, SIDE), f32),
        vmem((GROUP, SIDE, 128), f32), vmem((8 * BOX, 128), f32), vmem((8 * BOX, 128), f32),
        *[vmem((GROUP, 2 * BOX, 128), f32)] * 8,
        vmem((2, 2 * BOX, 128), f32), vmem((FOLD, 128), f32),
        *[vmem((DEPTH, 2 * CHUNK, 128), f32)] * 2, *[vmem((DEPTH, 4 * CHUNK, 128), f32)] * 2,
        vmem((4 * CHUNK, 128), f32), vmem((DEPTH, 4 * CHUNK, 128), f32), vmem((2 * BOX, 128), f32), vmem((2 * BOX, 128), f32),
        vmem((8 * BOX, 128), f32), vmem((4, SIDE, 128), f32), vmem((GROUP, 8, 384), f32), vmem((GROUP, 8, 384), f32),
        vmem((1, 1, 128), f32), vmem((FRAMES, 1, 128), f32), vmem((GROUP, 1, 128), f32), vmem((GROUP, 1, 128), f32),
        *[dma((8,))] * 19, dma((2,)),
    ]
    return pl.pallas_call(
        kernel,
        out_shape=(
            pltpu.VMEM((1, GROUP, MODES), f32),
            pltpu.VMEM((GROUP, 2, SHARE), f32),
        ),
        in_specs=[pl.BlockSpec(memory_space=pl.ANY)] * 5,
        out_specs=[pl.BlockSpec(memory_space=pltpu.VMEM)] * 2,
        scratch_shapes=scratch,
        compiler_params=pltpu.CompilerParams(collective_id=0, has_side_effects=True, vmem_limit_bytes=60 * 2**20),
    )(sky_image, coefficients, mode_basis, aperture, jnp.asarray(TABLE))


def solution(mesh):
    in_specs = (P("frame", None, "patch"), P("frame", "patch", None), P(), P())
    out_specs = (P("frame", "patch", None), P("patch", None, "frame"))
    return jax.shard_map(body, mesh=mesh, in_specs=in_specs, out_specs=out_specs, check_vma=False)
```

```python
import math

import jax
import jax.numpy as jnp
import ml_dtypes
import numpy as np
from jax import lax
from jax.experimental import pallas as pl
from jax.experimental.pallas import tpu as pltpu
from jax.sharding import PartitionSpec as P

SIDE = 144
RIM = 8
TILE = SIDE - 2 * RIM
LOW, BOX = 32, 80
GROUP = 8
DEPTH = 8
STRIPS = 4
FRAMES = GROUP * DEPTH
HALF = SIDE // 2 + 1
FOLD = BOX // 2
CHUNK = FOLD // DEPTH
FLAT = BOX * SIDE
PERIOD = 8 * SIDE
MODES = 64
UNROLL = GROUP
SHARE = SIDE * SIDE // FRAMES
DAMPING = 0.02 * FRAMES
EXCHANGES = ("coef", "own", "cross", "img_close", "img_mid", "img_last", "pow", "sum", "obj", "out", "ret", "part")
FAR_FIRST = (4, 3, 5, 2, 6, 1, 7)
MESH = pl.DeviceIdType.MESH
f32, bf16 = jnp.float32, jnp.bfloat16


def profile():
    at = np.arange(SIDE, dtype=np.float64)
    distance = np.minimum(at, SIDE - 1 - at)
    taper = 0.3 + 0.7 * np.sin(math.pi * (distance + 1.0) / (2.0 * (RIM + 1))) ** 2
    return np.where(distance < RIM, taper, 1.0)


def tables():
    k = np.arange(HALF)
    y = np.arange(SIDE)
    u = np.arange(BOX) + LOW - SIDE // 2
    weight = np.ones(HALF)
    weight[0] = weight[-1] = 0.5

    def pair(a, b):
        angle = 2.0 * math.pi / SIDE * (np.outer(a, b) % SIDE)
        return np.cos(angle), np.sin(angle)

    def cut(t):
        high = t.astype(ml_dtypes.bfloat16)
        return high, (t - high.astype(np.float64)).astype(ml_dtypes.bfloat16)

    def rows_of(*blocks):
        t = np.zeros((BOX * len(blocks), blocks[0].shape[1]))
        for n, block in enumerate(blocks):
            t[n * BOX : n * BOX + block.shape[0]] = block
        high, low = cut(t)
        return np.concatenate([high, high, low], axis=1)

    def columns_of(c, s):
        t = np.zeros((-(-c.shape[0] // 16) * 16, 256))
        t[: c.shape[0], : c.shape[1]], t[: c.shape[0], 128 : 128 + c.shape[1]] = c, s
        return cut(t)

    def twice(c, s):
        t = np.zeros((BOX, 256))
        t[: c.shape[0], : c.shape[1]], t[: c.shape[0], 128 : 128 + c.shape[1]] = c, s
        high, low = cut(t)
        return np.concatenate([high, high, low])

    parts = {}
    c, s = pair(k, u)
    parts["pupil_rows"] = rows_of(c, s)
    parts["pupil_columns"] = twice(c.T, s.T)
    parts["back_columns"] = twice(weight[:, None] * c, weight[:, None] * s)

    def wide(t):
        return np.pad(t, ((0, BOX - t.shape[0]), (0, BOX - t.shape[1])))

    parts["back_even"], parts["back_odd"] = rows_of(wide(c.T * weight)), rows_of(wide(s.T * weight))
    c, s = pair(k, k)
    parts["focal_columns"] = twice(weight[:, None] * c, -weight[:, None] * s)
    disc = np.concatenate([np.arange(37), [0] * 3, np.arange(72, 36, -1), [0] * 4])
    used = np.concatenate([np.ones(37), [0] * 3, np.ones(36), [0] * 4])
    parts["focal_even"] = rows_of(wide((c * weight)[disc] * used[:, None]))
    parts["focal_odd"] = rows_of(wide((s * weight)[disc] * used[:, None]))
    parts["disc_even"] = rows_of(wide((c * weight)[:, disc] * used))
    parts["disc_odd"] = rows_of(wide((s * weight)[:, disc] * used))
    w = profile()
    c, s = pair(k, y)
    t = rows_of((c * w / SIDE)[disc] * used[:, None], (s * w / SIDE)[disc] * used[:, None])
    parts["data_rows"], parts["data_rows_end"] = t[:, :256], t[:, 256:]
    order = np.concatenate([y[RIM:-RIM], y[:RIM], y[-RIM:]])
    parts["data_columns"], parts["data_columns_low"] = columns_of(
        (w[:, None] * c.T)[order], -(w[:, None] * s.T)[order]
    )
    first, rows, total = {}, [], 0
    for name, part in parts.items():
        first[name] = (total, *part.shape)
        total += part.shape[0]
        rows.append(np.pad(part, ((0, 0), (0, 256 - part.shape[1]))))
    return np.concatenate(rows), first


TABLE, FIRST = tables()


def split(x):
    high = x.astype(bf16)
    return high, (x - high.astype(f32)).astype(bf16)


def mm(a, b):
    return jnp.dot(a, b, preferred_element_type=f32)


def mm3(a, b):
    return mm(a[0], b[0]) + (mm(a[0], b[1]) + mm(a[1], b[0]))


def lanes(*parts):
    return jnp.concatenate(parts, axis=1)


def sine_cosine(x):
    quarter = jnp.floor(x * (2.0 / math.pi) + 0.5)
    r = x - quarter * 1.5703125
    r = r - quarter * 4.837512969970703125e-4
    r = r - quarter * 7.54978995489188216e-8
    z = r * r
    sine = ((-1.9515295891e-4 * z + 8.3321608736e-3) * z - 1.6666654611e-1) * z * r + r
    cosine = ((2.443315711809948e-5 * z - 1.388731625493765e-3) * z + 4.166664568298827e-2) * z * z - 0.5 * z + 1.0
    halves = jnp.floor(quarter * 0.5)
    odd = quarter - 2.0 * halves
    minus = 1.0 - 2.0 * (halves - 2.0 * jnp.floor(halves * 0.5))
    swap = odd > 0.5
    return (
        jnp.where(swap, cosine, sine) * minus,
        jnp.where(swap, -sine, cosine) * minus,
    )


def kernel(
    sky, coef, basis, aperture, table_hbm,
    gradient_out, object_out,
    tab, skyp, coef_v, coef_send, coef_recv, mask_v, base, base3,
    edges, img, halo, turned, pre, pim, fpr, fpi, fmr, fmi, tre, tim, dre, dim_,
    sums, packed, pow_send, pow_recv, sum_send, sum_recv, obj_send, obj_all, ore, oim, dph,
    full, out_send, out_recv, part_send, part_recv, ret_send, ret_recv,
    local_sem, send_sem, recv_sem,
):
    place, strip = lax.axis_index("frame"), lax.axis_index("patch")
    me, z = place // DEPTH, place % DEPTH

    y, x = me // 2, me % 2
    other = 1 - x
    near, far, back_y = y + 1 - 2 * (y % 2), 3 - y, (y + 2) % 4
    close = [near * 2 + x, far * 2 + x, y * 2 + other]
    distant = [near * 2 + other, far * 2 + other, back_y * 2 + x, back_y * 2 + other]
    peers = distant[::-1] + close[::-1]

    def at(group, depth, which=None):
        return {"frame": group * DEPTH + depth, "patch": strip if which is None else which}

    def remote(src, dst, exchange, device):
        at_sem = EXCHANGES.index(exchange)
        return pltpu.make_async_remote_copy(
            src_ref=src, dst_ref=dst, send_sem=send_sem.at[at_sem], recv_sem=recv_sem.at[at_sem],
            device_id=device, device_id_type=MESH,
        )

    def everything(ref, exchange):
        return remote(ref, ref, exchange, at(peers[0], z))

    def table(name, half=None):
        row, count, width = FIRST[name]
        if half is None:
            return tab[row : row + count, :width]
        return tab[row : row + count, half * 128 : half * 128 + 128]

    def from_left(name, x):
        h, r = split(x)
        return mm(table(name), jnp.concatenate([h, r, h]))

    def from_right(x, name, half=None):
        h, r = split(x)
        return mm(lanes(h[:, :BOX], r[:, :BOX], h[:, :BOX]), table(name, half))

    loads = [
        pltpu.make_async_copy(coef.at[0], coef_v, local_sem.at[0]),
        pltpu.make_async_copy(basis.at[:, pl.ds(LOW * SIDE, FLAT)], base, local_sem.at[1]),
        pltpu.make_async_copy(sky.at[0], skyp.at[pl.ds(RIM, 512)], local_sem.at[2]),
        pltpu.make_async_copy(table_hbm, tab, local_sem.at[3]),
        pltpu.make_async_copy(aperture, mask_v, local_sem.at[4]),
    ]
    for load in loads:
        load.start()

    barrier = pltpu.get_barrier_semaphore()
    beside = lax.rem(strip + jnp.where(me < 4, STRIPS - 1, 1), STRIPS)

    def greet(device):
        pl.semaphore_signal(barrier, inc=1, device_id=device, device_id_type=MESH)

    for d in FAR_FIRST:
        greet(at(me, lax.rem(z + d, DEPTH)))
    for t in [*peers, me]:
        greet(at(t, z, beside))
    for t in peers:
        greet(at(t, z))

    skyp[pl.ds(0, RIM), :] = jnp.zeros((RIM, 256), f32)
    skyp[pl.ds(512 + RIM, 120), :] = jnp.zeros((120, 256), f32)
    loads[0].wait()
    for p in range(GROUP):
        row = coef_v[p : p + 1, :]
        coef_send[p] = lanes(row, row)
    loads[2].wait()
    for half in range(2):
        strip_t = skyp[:, half * 128 : half * 128 + 128].T
        for r in range(4):
            edges[2 * half, r] = strip_t[:8, r * TILE : r * TILE + SIDE]
            edges[2 * half + 1, r] = strip_t[120:, r * TILE : r * TILE + SIDE]
    pl.semaphore_wait(barrier, GROUP - 1 + DEPTH - 1 + GROUP)

    for t in peers:
        remote(coef_send.at[t], coef_recv.at[me], "coef", at(t, z)).start()
    coef_recv[me] = coef_send[me]

    def main_of(t):
        return skyp.at[
            pl.ds(pl.multiple_of(lax.rem(t, 4) * TILE, TILE), SIDE), pl.ds(pl.multiple_of((t // 4) * 128, 128), 128)
        ]

    def edge_of(kind, t):
        return edges.at[kind, lax.rem(t, 4)]

    for t in peers:
        kind, side = jnp.where(t < 4, 2, 1), jnp.where(t < 4, 1, 0)
        remote(edge_of(kind, t), halo.at[me, side], "own", at(t, z)).start()
    for p in range(GROUP):
        kind, side, step = (3, 0, 1) if p < 4 else (0, 1, STRIPS - 1)
        remote(edge_of(kind, p), halo.at[me, side], "cross", at(p, z, lax.rem(strip + step, STRIPS))).start()
    batches = {"img_close": close, "img_mid": distant[:2], "img_last": distant[2:]}
    for exchange, partners in batches.items():
        for t in partners:
            remote(main_of(t), img.at[me], exchange, at(t, z)).start()
    own_side = jnp.where(me < 4, 1, 0)
    mine = [
        pltpu.make_async_copy(main_of(me), img.at[me], local_sem.at[5]),
        pltpu.make_async_copy(edge_of(jnp.where(me < 4, 2, 1), me), halo.at[me, own_side], local_sem.at[6]),
    ]
    for c in mine:
        c.start()

    loads[1].wait()

    def cut(g, carry):
        at_g = pl.ds(pl.multiple_of(g * PERIOD, 128), PERIOD)
        x = base[:, at_g]
        h, r = split(x)
        base3[0:MODES, at_g] = h
        base3[MODES : 2 * MODES, at_g] = r
        base3[2 * MODES :, at_g] = (x - h.astype(f32) - r.astype(f32)).astype(bf16)
        return carry

    lax.fori_loop(0, BOX // 8, cut, 0)
    for load in loads[3:]:
        load.wait()

    lane = lax.broadcasted_iota(jnp.int32, (8, 128), 1)
    mask = mask_v[LOW : LOW + BOX, 0:128].astype(f32)
    mask = pltpu.roll(mask, 128 - LOW, 1)
    mask = jnp.where(lax.broadcasted_iota(jnp.int32, (BOX, 128), 1) < BOX, mask, 0.0)
    area = jnp.sum(mask)
    intensity_scale = 1.0 / (SIDE * SIDE * area)
    dph[0:BOX, :] = mask

    everything(coef_recv.at[pl.ds(0, GROUP - 1)], "coef").wait_recv()
    weights = jnp.concatenate([coef_recv[j] for j in range(GROUP)])
    w0 = weights.astype(bf16).astype(f32)
    w1 = (weights - w0).astype(bf16).astype(f32)
    w2 = weights - w0 - w1
    weights = jnp.concatenate([lanes(w, w[:, :MODES]) for w in (w0, w1, w2)]).astype(bf16)

    starts = [divmod(SIDE * r + LOW, 128) for r in range(8)]

    def pupils(g, carry):
        ph = mm(weights, base3[:, pl.ds(pl.multiple_of(g * PERIOD, 128), PERIOD)])
        ph = ph[0:8] + (ph[8:16] + ph[16:24])
        rows = []
        for tile, off in starts:
            x = ph[:, tile * 128 : tile * 128 + 128]
            if off:
                x = pltpu.roll(x, 128 - off, 1)
            if off + BOX > 128:
                y = pltpu.roll(ph[:, tile * 128 + 128 : tile * 128 + 256], 128 - off, 1)
                x = jnp.where(lane < 128 - off, x, y)
            rows.append(x)
        m = dph[pl.ds(pl.multiple_of(g * 8, 8), 8), :]
        m = jnp.concatenate([jnp.broadcast_to(m[r : r + 1], (8, 128)) for r in range(8)])
        sine, cosine = sine_cosine(jnp.concatenate(rows))
        at_g = pl.ds(pl.multiple_of(g * 64, 64), 64)
        pre[at_g, :] = m * cosine
        pim[at_g, :] = m * sine
        return carry

    lax.fori_loop(0, BOX // 8, pupils, 0, unroll=5)

    def of_frame(ref, f):
        return ref[pl.ds(f, BOX, stride=GROUP), :]

    def fold(x):
        return x[:BOX] + x[BOX:], x[:BOX] - x[BOX:]

    def stack(*parts):
        return jnp.concatenate(parts)

    def transfers(n, carry):
        fs = [n * UNROLL + m for m in range(UNROLL)]
        rows = []
        for f in fs:
            y = from_left("pupil_rows", lanes(of_frame(pre, f), of_frame(pim, f)))
            cr, ci, sr, si = y[:BOX, :128], y[:BOX, 128:], y[BOX:, :128], y[BOX:, 128:]
            rows += [cr + si, cr - si, ci - sr, ci + sr]
        y = from_right(stack(*rows), "pupil_columns")
        even, odd = [], []
        for m, f in enumerate(fs):
            r, i = y[4 * m * BOX : (4 * m + 2) * BOX], y[(4 * m + 2) * BOX : (4 * m + 4) * BOX]
            p_re, p_im = r[:, :128] + i[:, 128:], i[:, :128] - r[:, 128:]
            m_re, m_im = r[:, :128] - i[:, 128:], i[:, :128] + r[:, 128:]
            fpr[f], fpi[f], fmr[f], fmi[f] = p_re, p_im, m_re, m_im
            plus = (p_re * p_re + p_im * p_im) * intensity_scale
            minus = (m_re * m_re + m_im * m_im) * intensity_scale
            even += fold(plus + minus)
            odd += fold(plus - minus)
        x_re = from_right(stack(*even), "focal_columns", 0)
        x_im = from_right(stack(*odd), "focal_columns", 1)
        for m, f in enumerate(fs):
            x = lanes(x_re[2 * m * BOX : 2 * (m + 1) * BOX], x_im[2 * m * BOX : 2 * (m + 1) * BOX])
            c = from_left("focal_even", x[:BOX])
            s = from_left("focal_odd", x[BOX:])
            cr, ci, sr, si = c[:, :128], c[:, 128:], s[:, :128], s[:, 128:]
            tre[f] = stack(cr + si, cr - si)
            tim[f] = stack(ci - sr, ci + sr)
        return carry

    lax.fori_loop(0, GROUP // UNROLL, transfers, 0)

    lane40 = lax.broadcasted_iota(jnp.int32, (FOLD, 128), 1)
    row40 = lax.broadcasted_iota(jnp.int32, (FOLD, 128), 0)
    border = jnp.where(row40 < 24, 73, jnp.where(row40 < 32, 68, 65))

    def shifted(x, back):
        return stack(*[
            pltpu.roll(x[a:b], 128 - by if back else by, 1) for a, b, by in ((0, 24, 73), (24, 32, 68), (32, 40, 65))
        ])

    def pack(x, into, at_row):
        for sign in range(2):
            wide, narrow = x[sign * BOX : sign * BOX + FOLD], x[sign * BOX + FOLD : (sign + 1) * BOX]
            packed[...] = jnp.where(lane40 < border, wide, shifted(narrow, False))
            for d in range(DEPTH):
                into[d, at_row + sign * CHUNK : at_row + (sign + 1) * CHUNK, :] = packed[d * CHUNK : (d + 1) * CHUNK, :]

    power = jnp.zeros((2 * BOX, 128), f32)
    for f in range(GROUP):
        power = power + (tre[f] * tre[f] + tim[f] * tim[f])
    pack(power, pow_send, 0)
    for d in FAR_FIRST:
        t = lax.rem(z + d, DEPTH)
        remote(pow_send.at[t], pow_recv.at[z], "pow", at(me, t)).start()
    pow_recv[z] = pow_send[z]

    for c in mine:
        c.wait()
    all_own, all_cross = halo.at[pl.ds(0, GROUP - 1), 0], halo.at[:, 0]
    everything(all_cross, "cross").wait_recv()
    everything(all_own, "own").wait_recv()
    row = lax.broadcasted_iota(jnp.int32, (128, 256), 0)
    left_on = jnp.where(jnp.logical_and(strip == 0, me < 4), 0.0, 1.0)
    right_on = jnp.where(jnp.logical_and(strip == STRIPS - 1, me >= 4), 0.0, 1.0)
    rims = lanes(halo[...].reshape(128, SIDE), jnp.zeros((128, 256 - SIDE), f32))
    rims = rims * jnp.where(lax.rem(row, 16) < 8, left_on, right_on)
    rims = rims.T[:SIDE]
    for f in range(GROUP):
        turned[f] = pltpu.roll(rims, (128 - 16 * f) % 128, 1) if f else rims

    sums[...] = jnp.zeros_like(sums)

    def data(fs):
        h, r = split(stack(*[lanes(img[f], turned[f]) for f in fs]))
        x = mm3((h[:, :SIDE], r[:, :SIDE]), (table("data_columns"), table("data_columns_low")))
        n_re, n_im = sums[0], sums[1]
        for m, f in enumerate(fs):
            h, r = split(x[m * SIDE : (m + 1) * SIDE])
            h = stack(h, r, h)
            y = mm(table("data_rows"), h[:256]) + mm(table("data_rows_end"), h[256:])
            cr, ci, sr, si = y[:BOX, :128], y[:BOX, 128:], y[BOX:, :128], y[BOX:, 128:]
            d_re, d_im = stack(cr + si, cr - si), stack(ci - sr, ci + sr)
            dre[f] = d_re
            dim_[f] = d_im
            t_re, t_im = tre[f], tim[f]
            n_re = n_re + (t_re * d_re + t_im * d_im)
            n_im = n_im + (t_re * d_im - t_im * d_re)
        sums[0], sums[1] = n_re, n_im

    everything(img.at[pl.ds(0, 3)], "img_close").wait_recv()
    data([me, *close])
    everything(img.at[pl.ds(0, 2)], "img_mid").wait_recv()
    data(distant[:2])
    everything(img.at[pl.ds(0, 2)], "img_last").wait_recv()
    data(distant[2:])

    pack(sums[0], sum_send, 0)
    pack(sums[1], sum_send, 2 * CHUNK)
    for d in FAR_FIRST:
        t = lax.rem(z + d, DEPTH)
        remote(sum_send.at[t], sum_recv.at[z], "sum", at(me, t)).start()
    sum_recv[z] = sum_send[z]
    everything(pow_recv.at[pl.ds(0, DEPTH - 1)], "pow").wait_recv()
    power = pow_recv[0]
    for j in range(1, DEPTH):
        power = power + pow_recv[j]
    power = power + DAMPING
    everything(sum_recv.at[pl.ds(0, DEPTH - 1)], "sum").wait_recv()
    total = sum_recv[0]
    for j in range(1, DEPTH):
        total = total + sum_recv[j]
    obj_send[...] = total / stack(power, power)
    for d in FAR_FIRST:
        t = lax.rem(z + d, DEPTH)
        remote(obj_send, obj_all.at[z], "obj", at(me, t)).start()
    obj_all[z] = obj_send[...]
    everything(obj_all.at[pl.ds(0, DEPTH - 1)], "obj").wait_recv()
    for part, ref in enumerate((ore, oim)):
        for sign in range(2):
            at_row = (2 * part + sign) * CHUNK
            for d in range(DEPTH):
                packed[d * CHUNK : (d + 1) * CHUNK, :] = obj_all[d, at_row : at_row + CHUNK, :]
            x = packed[...]
            ref[sign * BOX : sign * BOX + FOLD, :] = jnp.where(lane40 < jnp.minimum(border, HALF), x, 0.0)
            ref[sign * BOX + FOLD : (sign + 1) * BOX, :] = jnp.where(lane40 < 128 - border, shifted(x, True), 0.0)

    scale = 2.0 / (SIDE * SIDE)

    def back(n, carry):
        fs = [n * UNROLL + m for m in range(UNROLL)]
        o_re, o_im = ore[...], oim[...]
        h_re, h_im = [], []
        for f in fs:
            t_re, t_im = tre[f], tim[f]
            e_re = dre[f] - (o_re * t_re - o_im * t_im)
            e_im = dim_[f] - (o_re * t_im + o_im * t_re)
            re_even, re_odd = fold(-scale * (e_re * o_re + e_im * o_im))
            im_even, im_odd = fold(scale * (e_re * o_im - e_im * o_re))
            c = from_left("disc_even", lanes(re_even, im_even))
            s = from_left("disc_odd", lanes(re_odd, im_odd))
            cr, ci, sr, si = c[:, :128], c[:, 128:], s[:, :128], s[:, 128:]
            h_re += [cr - si, cr + si]
            h_im += [ci + sr, ci - sr]
        even = from_right(stack(*h_re), "focal_columns", 0) * (4.0 * intensity_scale)
        odd = from_right(stack(*h_im), "focal_columns", 1) * (4.0 * intensity_scale)
        sum_rows, gap_rows = [], []
        for m, f in enumerate(fs):
            at_m = slice(2 * m * BOX, 2 * (m + 1) * BOX)
            plus, minus = even[at_m] + odd[at_m], even[at_m] - odd[at_m]
            p_re, p_im, m_re, m_im = plus * fpr[f], plus * fpi[f], minus * fmr[f], minus * fmi[f]
            sum_rows += [p_re + m_re, p_im + m_im]
            gap_rows += [p_re - m_re, p_im - m_im]
        qc = from_right(stack(*sum_rows), "back_columns", 0)
        qs = from_right(stack(*gap_rows), "back_columns", 1)
        for m, f in enumerate(fs):
            at_re, at_im = slice(4 * m * BOX, (4 * m + 2) * BOX), slice((4 * m + 2) * BOX, (4 * m + 4) * BOX)
            re_even, re_odd = fold(qc[at_re] - qs[at_im])
            im_even, im_odd = fold(qc[at_im] + qs[at_re])
            c = from_left("back_even", lanes(re_even, im_even))
            s = from_left("back_odd", lanes(re_odd, im_odd))
            g_re, g_im = c[:, :128] - s[:, 128:], c[:, 128:] + s[:, :128]
            dph[pl.ds(f, BOX, stride=GROUP), :] = of_frame(pre, f) * g_im - of_frame(pim, f) * g_re
        return carry

    lax.fori_loop(0, GROUP // UNROLL, back, 0)

    def project(g, total):
        tiles = [jnp.zeros((8, 128), f32) for _ in range(9)]
        for r, (tile, off) in enumerate(starts):
            x = dph[pl.ds(pl.multiple_of(g * 64, 64) + 8 * r, 8), :]
            if off:
                x = pltpu.roll(x, off, 1)
            if off + BOX > 128:
                tiles[tile + 1] += jnp.where(lane < off, x, 0.0)
                x = jnp.where(lane < off, 0.0, x)
            tiles[tile] += x
        x = jnp.concatenate(split(lanes(*tiles)))
        modes = base3[0 : 2 * MODES, pl.ds(pl.multiple_of(g * PERIOD, 128), PERIOD)]
        return total + lax.dot_general(x, modes, (((1,), (1,)), ((), ())), preferred_element_type=f32)

    total = lax.fori_loop(0, BOX // 8, project, jnp.zeros((16, 128), f32), unroll=5)
    total = total[:8] + total[8:]
    gradient = total + pltpu.roll(total, MODES, 1)

    for j in range(GROUP):
        ret_send[j] = gradient[j : j + 1]
    part_send[0] = jnp.sum(gradient, axis=0, keepdims=True)

    groups = list(zip([*peers, me], (3, 2, 2, 2, 1, 1, 1, 0)))
    depths = [(z, 0)] + [(lax.rem(z + d, DEPTH), min(d, DEPTH - d)) for d in range(1, DEPTH)]
    ways = [(a + b, group, depth) for group, a in groups for depth, b in depths if a + b]
    for _, group, depth in sorted(ways, key=lambda way: -way[0]):
        remote(part_send, part_recv.at[pl.ds(place, 1)], "part", at(group, depth)).start()
    for t in peers:
        remote(ret_send.at[t], ret_recv.at[me], "ret", at(t, z)).start()
    part_recv[place] = part_send[0]
    ret_recv[me] = ret_send[me]

    r_at = lax.broadcasted_iota(jnp.int32, (2 * SIDE, 2 * BOX), 0)
    c_at = lax.broadcasted_iota(jnp.int32, (2 * SIDE, 2 * BOX), 1)
    mirrored = r_at >= SIDE
    k = jnp.where(mirrored, r_at - SIDE, r_at)
    minus = (k >= HALF) != mirrored
    k = jnp.where(k >= HALF, SIDE - k, k)
    k = jnp.where(k > 36, FOLD + 72 - k, k) + jnp.where(minus, BOX, 0)
    pick_rows = jnp.where(k == c_at, 1.0, 0.0).astype(bf16)
    r_at = lax.broadcasted_iota(jnp.int32, (128, 256), 0)
    c_at = lax.broadcasted_iota(jnp.int32, (128, 256), 1)
    flip_columns = jnp.where(
        jnp.logical_and(r_at + c_at == SIDE, jnp.logical_and(c_at >= HALF, c_at < SIDE)), 1.0, 0.0
    ).astype(bf16)
    parts = [mm(pick_rows, part) for part in split(lanes(ore[...], oim[...]))]
    lane_full = lax.broadcasted_iota(jnp.int32, (SIDE, 128), 1)
    for n, sign in ((0, 1.0), (1, -1.0)):
        at_n = slice(n * 128, n * 128 + 128)
        half = parts[0][:SIDE, at_n] + parts[1][:SIDE, at_n]
        mirror = [mm(part[SIDE:, at_n].astype(bf16), flip_columns) for part in parts]
        mirror = sign * (mirror[0] + mirror[1])
        full[2 * n] = jnp.where(lane_full < HALF, half, mirror[:, :128])
        full[2 * n + 1] = mirror[:, 128:]
    first_row = z * 9 // 4
    for n in range(2):
        placed = [jnp.zeros((8, 128), f32) for _ in range(6)]
        for t in range(3):
            for piece in range(2):
                x = full[2 * n + piece, pl.ds(first_row + t, GROUP, stride=SIDE // GROUP), :]
                tile, off = divmod(SIDE * t + 128 * piece, 128)
                if off:
                    x = pltpu.roll(x, off, 1)
                    placed[tile + 1] += jnp.where(lane < off, x, 0.0)
                    x = jnp.where(lane < off, 0.0, x)
                placed[tile] += x
        placed = lanes(*placed)
        picked = jnp.zeros((8, 384), f32)
        for m in range(4):
            moved = pltpu.roll(placed, 768 - 36 * m, 1) if m else placed
            picked = picked + jnp.where(lax.rem(z, 4) == m, 1.0, 0.0) * moved[:, :384]
        for i in range(GROUP):
            out_send[i, n : n + 1, :] = picked[i : i + 1]
    for t in peers:
        remote(out_send.at[t], out_recv.at[me], "out", at(t, z)).start()
    out_recv[me] = out_send[me]

    rest = {
        "coef": coef_recv.at[pl.ds(0, GROUP - 1)],
        "own": all_own,
        "cross": all_cross,
        "img_close": img.at[pl.ds(0, 3)],
        "img_mid": img.at[pl.ds(0, 2)],
        "img_last": img.at[pl.ds(0, 2)],
        "pow": pow_recv.at[pl.ds(0, DEPTH - 1)],
        "sum": sum_recv.at[pl.ds(0, DEPTH - 1)],
        "obj": obj_all.at[pl.ds(0, DEPTH - 1)],
        "out": out_recv.at[pl.ds(0, GROUP - 1)],
        "ret": ret_recv.at[pl.ds(0, GROUP - 1)],
        "part": part_recv.at[pl.ds(0, FRAMES - 1)],
    }
    for exchange, ref in rest.items():
        everything(ref, exchange).wait_send()
    everything(rest["out"], "out").wait_recv()
    for p in range(GROUP):
        object_out[p] = out_recv[p, 0:2, :SHARE]
    everything(rest["ret"], "ret").wait_recv()
    everything(rest["part"], "part").wait_recv()
    for p in range(GROUP):
        mean = part_recv[p * DEPTH]
        for n in range(1, DEPTH):
            mean = mean + part_recv[p * DEPTH + n]
        gradient_out[0, p : p + 1, :] = (ret_recv[p] - mean * (1.0 / FRAMES))[:, :MODES]


def body(sky_image, coefficients, mode_basis, aperture):
    vmem, dma = pltpu.VMEM, pltpu.SemaphoreType.DMA
    scratch = [
        vmem(TABLE.shape, bf16), vmem((640, 256), f32), vmem((GROUP, MODES), f32),
        vmem((GROUP, 1, 128), f32), vmem((GROUP, 1, 128), f32), vmem((SIDE, SIDE), jnp.int32), vmem((MODES, FLAT), f32),
        vmem((3 * MODES, FLAT), bf16),
        vmem((4, 4, 8, SIDE), f32), vmem((GROUP, SIDE, 128), f32), vmem((GROUP, 2, 8, SIDE), f32),
        vmem((GROUP, SIDE, 128), f32), vmem((8 * BOX, 128), f32), vmem((8 * BOX, 128), f32),
        *[vmem((GROUP, 2 * BOX, 128), f32)] * 8,
        vmem((2, 2 * BOX, 128), f32), vmem((FOLD, 128), f32),
        *[vmem((DEPTH, 2 * CHUNK, 128), f32)] * 2, *[vmem((DEPTH, 4 * CHUNK, 128), f32)] * 2,
        vmem((4 * CHUNK, 128), f32), vmem((DEPTH, 4 * CHUNK, 128), f32), vmem((2 * BOX, 128), f32), vmem((2 * BOX, 128), f32),
        vmem((8 * BOX, 128), f32), vmem((4, SIDE, 128), f32), vmem((GROUP, 8, 384), f32), vmem((GROUP, 8, 384), f32),
        vmem((1, 1, 128), f32), vmem((FRAMES, 1, 128), f32), vmem((GROUP, 1, 128), f32), vmem((GROUP, 1, 128), f32),
        dma((7,)), dma((len(EXCHANGES),)), dma((len(EXCHANGES),)),
    ]
    return pl.pallas_call(
        kernel,
        out_shape=(
            pltpu.VMEM((1, GROUP, MODES), f32),
            pltpu.VMEM((GROUP, 2, SHARE), f32),
        ),
        in_specs=[pl.BlockSpec(memory_space=pl.ANY)] * 5,
        out_specs=[pl.BlockSpec(memory_space=pltpu.VMEM)] * 2,
        scratch_shapes=scratch,
        compiler_params=pltpu.CompilerParams(collective_id=0, has_side_effects=True, vmem_limit_bytes=60 * 2**20),
    )(sky_image, coefficients, mode_basis, aperture, jnp.asarray(TABLE))


def solution(mesh):
    in_specs = (P("frame", None, "patch"), P("frame", "patch", None), P(), P())
    out_specs = (P("frame", "patch", None), P("patch", None, "frame"))
    return jax.shard_map(body, mesh=mesh, in_specs=in_specs, out_specs=out_specs, check_vma=False)
```

```python
import math

import jax
import jax.numpy as jnp
import ml_dtypes
import numpy as np
from jax import lax
from jax.experimental import pallas as pl
from jax.experimental.pallas import tpu as pltpu
from jax.sharding import PartitionSpec as P

SIDE = 144
RIM = 8
TILE = SIDE - 2 * RIM
LOW, BOX = 32, 80
GROUP = 8
DEPTH = 8
STRIPS = 4
FRAMES = GROUP * DEPTH
HALF = SIDE // 2 + 1
FOLD = BOX // 2
CHUNK = FOLD // DEPTH
FLAT = BOX * SIDE
PERIOD = 8 * SIDE
MODES = 64
UNROLL = GROUP
SHARE = SIDE * SIDE // FRAMES
DAMPING = 0.02 * FRAMES
EXCHANGES = ("coef", "own", "cross", "img_close", "img_mid", "img_last", "pow", "sum", "obj", "out", "ret", "part")
FAR_FIRST = (4, 3, 5, 2, 6, 1, 7)
MESH = pl.DeviceIdType.MESH
f32, bf16 = jnp.float32, jnp.bfloat16


def profile():
    at = np.arange(SIDE, dtype=np.float64)
    distance = np.minimum(at, SIDE - 1 - at)
    taper = 0.3 + 0.7 * np.sin(math.pi * (distance + 1.0) / (2.0 * (RIM + 1))) ** 2
    return np.where(distance < RIM, taper, 1.0)


def tables():
    k = np.arange(HALF)
    y = np.arange(SIDE)
    u = np.arange(BOX) + LOW - SIDE // 2
    weight = np.ones(HALF)
    weight[0] = weight[-1] = 0.5

    def pair(a, b):
        angle = 2.0 * math.pi / SIDE * (np.outer(a, b) % SIDE)
        return np.cos(angle), np.sin(angle)

    def cut(t):
        high = t.astype(ml_dtypes.bfloat16)
        return high, (t - high.astype(np.float64)).astype(ml_dtypes.bfloat16)

    def rows_of(*blocks):
        t = np.zeros((BOX * len(blocks), blocks[0].shape[1]))
        for n, block in enumerate(blocks):
            t[n * BOX : n * BOX + block.shape[0]] = block
        high, low = cut(t)
        return np.concatenate([high, high, low], axis=1)

    def columns_of(c, s):
        t = np.zeros((-(-c.shape[0] // 16) * 16, 256))
        t[: c.shape[0], : c.shape[1]], t[: c.shape[0], 128 : 128 + c.shape[1]] = c, s
        return cut(t)

    def twice(c, s):
        t = np.zeros((BOX, 256))
        t[: c.shape[0], : c.shape[1]], t[: c.shape[0], 128 : 128 + c.shape[1]] = c, s
        high, low = cut(t)
        return np.concatenate([high, high, low])

    parts = {}
    c, s = pair(k, u)
    parts["pupil_rows"] = rows_of(c, s)
    parts["pupil_columns"] = twice(c.T, s.T)
    parts["back_columns"] = twice(weight[:, None] * c, weight[:, None] * s)

    def wide(t):
        return np.pad(t, ((0, BOX - t.shape[0]), (0, BOX - t.shape[1])))

    parts["back_even"], parts["back_odd"] = rows_of(wide(c.T * weight)), rows_of(wide(s.T * weight))
    c, s = pair(k, k)
    parts["focal_columns"] = twice(weight[:, None] * c, -weight[:, None] * s)
    disc = np.concatenate([np.arange(37), [0] * 3, np.arange(72, 36, -1), [0] * 4])
    used = np.concatenate([np.ones(37), [0] * 3, np.ones(36), [0] * 4])
    parts["focal_even"] = rows_of(wide((c * weight)[disc] * used[:, None]))
    parts["focal_odd"] = rows_of(wide((s * weight)[disc] * used[:, None]))
    parts["disc_even"] = rows_of(wide((c * weight)[:, disc] * used))
    parts["disc_odd"] = rows_of(wide((s * weight)[:, disc] * used))
    w = profile()
    c, s = pair(k, y)
    t = rows_of((c * w / SIDE)[disc] * used[:, None], (s * w / SIDE)[disc] * used[:, None])
    parts["data_rows"], parts["data_rows_end"] = t[:, :256], t[:, 256:]
    order = np.concatenate([y[RIM:-RIM], y[:RIM], y[-RIM:]])
    parts["data_columns"], parts["data_columns_low"] = columns_of(
        (w[:, None] * c.T)[order], -(w[:, None] * s.T)[order]
    )
    first, rows, total = {}, [], 0
    for name, part in parts.items():
        first[name] = (total, *part.shape)
        total += part.shape[0]
        rows.append(np.pad(part, ((0, 0), (0, 256 - part.shape[1]))))
    return np.concatenate(rows), first


TABLE, FIRST = tables()


def split(x):
    high = x.astype(bf16)
    return high, (x - high.astype(f32)).astype(bf16)


def mm(a, b):
    return jnp.dot(a, b, preferred_element_type=f32)


def mm3(a, b):
    return mm(a[0], b[0]) + (mm(a[0], b[1]) + mm(a[1], b[0]))


def lanes(*parts):
    return jnp.concatenate(parts, axis=1)


def sine_cosine(x):
    quarter = jnp.floor(x * (2.0 / math.pi) + 0.5)
    r = x - quarter * 1.5703125
    r = r - quarter * 4.837512969970703125e-4
    r = r - quarter * 7.54978995489188216e-8
    z = r * r
    sine = ((-1.9515295891e-4 * z + 8.3321608736e-3) * z - 1.6666654611e-1) * z * r + r
    cosine = ((2.443315711809948e-5 * z - 1.388731625493765e-3) * z + 4.166664568298827e-2) * z * z - 0.5 * z + 1.0
    halves = jnp.floor(quarter * 0.5)
    odd = quarter - 2.0 * halves
    minus = 1.0 - 2.0 * (halves - 2.0 * jnp.floor(halves * 0.5))
    swap = odd > 0.5
    return (
        jnp.where(swap, cosine, sine) * minus,
        jnp.where(swap, -sine, cosine) * minus,
    )


def kernel(
    sky, coef, basis, aperture, table_hbm,
    gradient_out, object_out,
    tab, skyp, coef_v, coef_send, coef_recv, mask_v, base, base3,
    edges, img, halo, turned, pre, pim, fpr, fpi, fmr, fmi, tre, tim, dre, dim_,
    sums, packed, pow_send, pow_recv, sum_send, sum_recv, obj_send, obj_all, ore, oim, dph,
    full, out_send, out_recv, part_send, part_recv, ret_send, ret_recv,
    local_sem, send_sem, recv_sem,
):
    place, strip = lax.axis_index("frame"), lax.axis_index("patch")
    me, z = place // DEPTH, place % DEPTH

    y, x = me // 2, me % 2
    other = 1 - x
    near, far, back_y = y + 1 - 2 * (y % 2), 3 - y, (y + 2) % 4
    close = [near * 2 + x, far * 2 + x, y * 2 + other]
    distant = [near * 2 + other, far * 2 + other, back_y * 2 + x, back_y * 2 + other]
    peers = distant[::-1] + close[::-1]

    def at(group, depth, which=None):
        return {"frame": group * DEPTH + depth, "patch": strip if which is None else which}

    def remote(src, dst, exchange, device):
        at_sem = EXCHANGES.index(exchange)
        return pltpu.make_async_remote_copy(
            src_ref=src, dst_ref=dst, send_sem=send_sem.at[at_sem], recv_sem=recv_sem.at[at_sem],
            device_id=device, device_id_type=MESH,
        )

    def everything(ref, exchange):
        return remote(ref, ref, exchange, at(peers[0], z))

    def table(name, half=None):
        row, count, width = FIRST[name]
        if half is None:
            return tab[row : row + count, :width]
        return tab[row : row + count, half * 128 : half * 128 + 128]

    def from_left(name, x):
        h, r = split(x)
        return mm(table(name), jnp.concatenate([h, r, h]))

    def from_right(x, name, half=None):
        h, r = split(x)
        return mm(lanes(h[:, :BOX], r[:, :BOX], h[:, :BOX]), table(name, half))

    loads = [
        pltpu.make_async_copy(coef.at[0], coef_v, local_sem.at[0]),
        pltpu.make_async_copy(basis.at[:, pl.ds(LOW * SIDE, FLAT)], base, local_sem.at[1]),
        pltpu.make_async_copy(sky.at[0], skyp.at[pl.ds(RIM, 512)], local_sem.at[2]),
        pltpu.make_async_copy(table_hbm, tab, local_sem.at[3]),
        pltpu.make_async_copy(aperture, mask_v, local_sem.at[4]),
    ]
    for load in loads:
        load.start()

    barrier = pltpu.get_barrier_semaphore()
    beside = lax.rem(strip + jnp.where(me < 4, STRIPS - 1, 1), STRIPS)

    def greet(device):
        pl.semaphore_signal(barrier, inc=1, device_id=device, device_id_type=MESH)

    for d in FAR_FIRST:
        greet(at(me, lax.rem(z + d, DEPTH)))
    for t in [*peers, me]:
        greet(at(t, z, beside))
    for t in peers:
        greet(at(t, z))

    skyp[pl.ds(0, RIM), :] = jnp.zeros((RIM, 256), f32)
    skyp[pl.ds(512 + RIM, 120), :] = jnp.zeros((120, 256), f32)
    loads[0].wait()
    for p in range(GROUP):
        row = coef_v[p : p + 1, :]
        coef_send[p] = lanes(row, row)
    loads[2].wait()
    for half in range(2):
        strip_t = skyp[:, half * 128 : half * 128 + 128].T
        for r in range(4):
            edges[2 * half, r] = strip_t[:8, r * TILE : r * TILE + SIDE]
            edges[2 * half + 1, r] = strip_t[120:, r * TILE : r * TILE + SIDE]
    pl.semaphore_wait(barrier, GROUP - 1 + DEPTH - 1 + GROUP)

    for t in peers:
        remote(coef_send.at[t], coef_recv.at[me], "coef", at(t, z)).start()
    coef_recv[me] = coef_send[me]

    def main_of(t):
        return skyp.at[
            pl.ds(pl.multiple_of(lax.rem(t, 4) * TILE, TILE), SIDE), pl.ds(pl.multiple_of((t // 4) * 128, 128), 128)
        ]

    def edge_of(kind, t):
        return edges.at[kind, lax.rem(t, 4)]

    for t in peers:
        kind, side = jnp.where(t < 4, 2, 1), jnp.where(t < 4, 1, 0)
        remote(edge_of(kind, t), halo.at[me, side], "own", at(t, z)).start()
    for p in range(GROUP):
        kind, side, step = (3, 0, 1) if p < 4 else (0, 1, STRIPS - 1)
        remote(edge_of(kind, p), halo.at[me, side], "cross", at(p, z, lax.rem(strip + step, STRIPS))).start()
    batches = {"img_close": close, "img_mid": distant[:2], "img_last": distant[2:]}
    for exchange, partners in batches.items():
        for t in partners:
            remote(main_of(t), img.at[me], exchange, at(t, z)).start()
    own_side = jnp.where(me < 4, 1, 0)
    mine = [
        pltpu.make_async_copy(main_of(me), img.at[me], local_sem.at[5]),
        pltpu.make_async_copy(edge_of(jnp.where(me < 4, 2, 1), me), halo.at[me, own_side], local_sem.at[6]),
    ]
    for c in mine:
        c.start()

    loads[1].wait()

    def cut(g, carry):
        at_g = pl.ds(pl.multiple_of(g * PERIOD, 128), PERIOD)
        x = base[:, at_g]
        h, r = split(x)
        base3[0:MODES, at_g] = h
        base3[MODES : 2 * MODES, at_g] = r
        base3[2 * MODES :, at_g] = (x - h.astype(f32) - r.astype(f32)).astype(bf16)
        return carry

    lax.fori_loop(0, BOX // 8, cut, 0)
    for load in loads[3:]:
        load.wait()

    lane = lax.broadcasted_iota(jnp.int32, (8, 128), 1)
    mask = mask_v[LOW : LOW + BOX, 0:128].astype(f32)
    mask = pltpu.roll(mask, 128 - LOW, 1)
    mask = jnp.where(lax.broadcasted_iota(jnp.int32, (BOX, 128), 1) < BOX, mask, 0.0)
    dph[0:BOX, :] = mask * jnp.sqrt(jnp.full((BOX, 128), 1.0 / (SIDE * SIDE), f32) / jnp.sum(mask))

    everything(coef_recv.at[pl.ds(0, GROUP - 1)], "coef").wait_recv()
    weights = jnp.concatenate([coef_recv[j] for j in range(GROUP)])
    w0 = weights.astype(bf16).astype(f32)
    w1 = (weights - w0).astype(bf16).astype(f32)
    w2 = weights - w0 - w1
    weights = jnp.concatenate([lanes(w, w[:, :MODES]) for w in (w0, w1, w2)]).astype(bf16)

    starts = [divmod(SIDE * r + LOW, 128) for r in range(8)]

    def pupils(g, carry):
        ph = mm(weights, base3[:, pl.ds(pl.multiple_of(g * PERIOD, 128), PERIOD)])
        ph = ph[0:8] + (ph[8:16] + ph[16:24])
        rows = []
        for tile, off in starts:
            x = ph[:, tile * 128 : tile * 128 + 128]
            if off:
                x = pltpu.roll(x, 128 - off, 1)
            if off + BOX > 128:
                y = pltpu.roll(ph[:, tile * 128 + 128 : tile * 128 + 256], 128 - off, 1)
                x = jnp.where(lane < 128 - off, x, y)
            rows.append(x)
        m = dph[pl.ds(pl.multiple_of(g * 8, 8), 8), :]
        m = jnp.concatenate([jnp.broadcast_to(m[r : r + 1], (8, 128)) for r in range(8)])
        sine, cosine = sine_cosine(jnp.concatenate(rows))
        at_g = pl.ds(pl.multiple_of(g * 64, 64), 64)
        pre[at_g, :] = m * cosine
        pim[at_g, :] = m * sine
        return carry

    lax.fori_loop(0, BOX // 8, pupils, 0, unroll=5)

    def of_frame(ref, f):
        return ref[pl.ds(f, BOX, stride=GROUP), :]

    def fold(x):
        return x[:BOX] + x[BOX:], x[:BOX] - x[BOX:]

    def stack(*parts):
        return jnp.concatenate(parts)

    def transfers(n, carry):
        fs = [n * UNROLL + m for m in range(UNROLL)]
        rows = []
        for f in fs:
            y = from_left("pupil_rows", lanes(of_frame(pre, f), of_frame(pim, f)))
            cr, ci, sr, si = y[:BOX, :128], y[:BOX, 128:], y[BOX:, :128], y[BOX:, 128:]
            rows += [cr + si, cr - si, ci - sr, ci + sr]
        y = from_right(stack(*rows), "pupil_columns")
        even, odd = [], []
        for m, f in enumerate(fs):
            r, i = y[4 * m * BOX : (4 * m + 2) * BOX], y[(4 * m + 2) * BOX : (4 * m + 4) * BOX]
            p_re, p_im = r[:, :128] + i[:, 128:], i[:, :128] - r[:, 128:]
            m_re, m_im = r[:, :128] - i[:, 128:], i[:, :128] + r[:, 128:]
            fpr[f], fpi[f], fmr[f], fmi[f] = p_re, p_im, m_re, m_im
            plus = p_re * p_re + p_im * p_im
            minus = m_re * m_re + m_im * m_im
            even += fold(plus + minus)
            odd += fold(plus - minus)
        x_re = from_right(stack(*even), "focal_columns", 0)
        x_im = from_right(stack(*odd), "focal_columns", 1)
        for m, f in enumerate(fs):
            x = lanes(x_re[2 * m * BOX : 2 * (m + 1) * BOX], x_im[2 * m * BOX : 2 * (m + 1) * BOX])
            c = from_left("focal_even", x[:BOX])
            s = from_left("focal_odd", x[BOX:])
            cr, ci, sr, si = c[:, :128], c[:, 128:], s[:, :128], s[:, 128:]
            tre[f] = stack(cr + si, cr - si)
            tim[f] = stack(ci - sr, ci + sr)
        return carry

    lax.fori_loop(0, GROUP // UNROLL, transfers, 0)

    lane40 = lax.broadcasted_iota(jnp.int32, (FOLD, 128), 1)
    row40 = lax.broadcasted_iota(jnp.int32, (FOLD, 128), 0)
    border = jnp.where(row40 < 24, 73, jnp.where(row40 < 32, 68, 65))

    def shifted(x, back):
        return stack(*[
            pltpu.roll(x[a:b], 128 - by if back else by, 1) for a, b, by in ((0, 24, 73), (24, 32, 68), (32, 40, 65))
        ])

    def pack(x, into, at_row):
        for sign in range(2):
            wide, narrow = x[sign * BOX : sign * BOX + FOLD], x[sign * BOX + FOLD : (sign + 1) * BOX]
            packed[...] = jnp.where(lane40 < border, wide, shifted(narrow, False))
            for d in range(DEPTH):
                into[d, at_row + sign * CHUNK : at_row + (sign + 1) * CHUNK, :] = packed[d * CHUNK : (d + 1) * CHUNK, :]

    power = jnp.zeros((2 * BOX, 128), f32)
    for f in range(GROUP):
        power = power + (tre[f] * tre[f] + tim[f] * tim[f])
    pack(power, pow_send, 0)
    for d in FAR_FIRST:
        t = lax.rem(z + d, DEPTH)
        remote(pow_send.at[t], pow_recv.at[z], "pow", at(me, t)).start()
    pow_recv[z] = pow_send[z]

    for c in mine:
        c.wait()
    all_own, all_cross = halo.at[pl.ds(0, GROUP - 1), 0], halo.at[:, 0]
    everything(all_cross, "cross").wait_recv()
    everything(all_own, "own").wait_recv()
    row = lax.broadcasted_iota(jnp.int32, (128, 256), 0)
    left_on = jnp.where(jnp.logical_and(strip == 0, me < 4), 0.0, 1.0)
    right_on = jnp.where(jnp.logical_and(strip == STRIPS - 1, me >= 4), 0.0, 1.0)
    rims = lanes(halo[...].reshape(128, SIDE), jnp.zeros((128, 256 - SIDE), f32))
    rims = rims * jnp.where(lax.rem(row, 16) < 8, left_on, right_on)
    rims = rims.T[:SIDE]
    for f in range(GROUP):
        turned[f] = pltpu.roll(rims, (128 - 16 * f) % 128, 1) if f else rims

    sums[...] = jnp.zeros_like(sums)

    def data(fs):
        h, r = split(stack(*[lanes(img[f], turned[f]) for f in fs]))
        x = mm3((h[:, :SIDE], r[:, :SIDE]), (table("data_columns"), table("data_columns_low")))
        n_re, n_im = sums[0], sums[1]
        for m, f in enumerate(fs):
            h, r = split(x[m * SIDE : (m + 1) * SIDE])
            h = stack(h, r, h)
            y = mm(table("data_rows"), h[:256]) + mm(table("data_rows_end"), h[256:])
            cr, ci, sr, si = y[:BOX, :128], y[:BOX, 128:], y[BOX:, :128], y[BOX:, 128:]
            d_re, d_im = stack(cr + si, cr - si), stack(ci - sr, ci + sr)
            dre[f] = d_re
            dim_[f] = d_im
            t_re, t_im = tre[f], tim[f]
            n_re = n_re + (t_re * d_re + t_im * d_im)
            n_im = n_im + (t_re * d_im - t_im * d_re)
        sums[0], sums[1] = n_re, n_im

    everything(img.at[pl.ds(0, 3)], "img_close").wait_recv()
    data([me, *close])
    everything(img.at[pl.ds(0, 2)], "img_mid").wait_recv()
    data(distant[:2])
    everything(img.at[pl.ds(0, 2)], "img_last").wait_recv()
    data(distant[2:])

    pack(sums[0], sum_send, 0)
    pack(sums[1], sum_send, 2 * CHUNK)
    for d in FAR_FIRST:
        t = lax.rem(z + d, DEPTH)
        remote(sum_send.at[t], sum_recv.at[z], "sum", at(me, t)).start()
    sum_recv[z] = sum_send[z]
    everything(pow_recv.at[pl.ds(0, DEPTH - 1)], "pow").wait_recv()
    power = pow_recv[0]
    for j in range(1, DEPTH):
        power = power + pow_recv[j]
    power = power + DAMPING
    everything(sum_recv.at[pl.ds(0, DEPTH - 1)], "sum").wait_recv()
    total = sum_recv[0]
    for j in range(1, DEPTH):
        total = total + sum_recv[j]
    obj_send[...] = total / stack(power, power)
    for d in FAR_FIRST:
        t = lax.rem(z + d, DEPTH)
        remote(obj_send, obj_all.at[z], "obj", at(me, t)).start()
    obj_all[z] = obj_send[...]
    everything(obj_all.at[pl.ds(0, DEPTH - 1)], "obj").wait_recv()
    for part, ref in enumerate((ore, oim)):
        for sign in range(2):
            at_row = (2 * part + sign) * CHUNK
            for d in range(DEPTH):
                packed[d * CHUNK : (d + 1) * CHUNK, :] = obj_all[d, at_row : at_row + CHUNK, :]
            x = packed[...]
            ref[sign * BOX : sign * BOX + FOLD, :] = jnp.where(lane40 < jnp.minimum(border, HALF), x, 0.0)
            ref[sign * BOX + FOLD : (sign + 1) * BOX, :] = jnp.where(lane40 < 128 - border, shifted(x, True), 0.0)

    scale = 4.0 * 2.0 / (SIDE * SIDE)

    def back(n, carry):
        fs = [n * UNROLL + m for m in range(UNROLL)]
        o_re, o_im = -scale * ore[...], -scale * oim[...]
        o_square = scale * (ore[...] * ore[...] + oim[...] * oim[...])
        h_re, h_im = [], []
        for f in fs:
            d_re, d_im = dre[f], dim_[f]
            re_even, re_odd = fold(d_re * o_re + d_im * o_im + o_square * tre[f])
            im_even, im_odd = fold(d_im * o_re - d_re * o_im + o_square * tim[f])
            c = from_left("disc_even", lanes(re_even, im_even))
            s = from_left("disc_odd", lanes(re_odd, im_odd))
            cr, ci, sr, si = c[:, :128], c[:, 128:], s[:, :128], s[:, 128:]
            h_re += [cr - si, cr + si]
            h_im += [ci + sr, ci - sr]
        even = from_right(stack(*h_re), "focal_columns", 0)
        odd = from_right(stack(*h_im), "focal_columns", 1)
        sum_rows, gap_rows = [], []
        for m, f in enumerate(fs):
            at_m = slice(2 * m * BOX, 2 * (m + 1) * BOX)
            plus, minus = even[at_m] + odd[at_m], even[at_m] - odd[at_m]
            p_re, p_im, m_re, m_im = plus * fpr[f], plus * fpi[f], minus * fmr[f], minus * fmi[f]
            sum_rows += [p_re + m_re, p_im + m_im]
            gap_rows += [p_re - m_re, p_im - m_im]
        qc = from_right(stack(*sum_rows), "back_columns", 0)
        qs = from_right(stack(*gap_rows), "back_columns", 1)
        for m, f in enumerate(fs):
            at_re, at_im = slice(4 * m * BOX, (4 * m + 2) * BOX), slice((4 * m + 2) * BOX, (4 * m + 4) * BOX)
            re_even, re_odd = fold(qc[at_re] - qs[at_im])
            im_even, im_odd = fold(qc[at_im] + qs[at_re])
            c = from_left("back_even", lanes(re_even, im_even))
            s = from_left("back_odd", lanes(re_odd, im_odd))
            g_re, g_im = c[:, :128] - s[:, 128:], c[:, 128:] + s[:, :128]
            dph[pl.ds(f, BOX, stride=GROUP), :] = of_frame(pre, f) * g_im - of_frame(pim, f) * g_re
        return carry

    lax.fori_loop(0, GROUP // UNROLL, back, 0)

    def project(g, total):
        tiles = [jnp.zeros((8, 128), f32) for _ in range(9)]
        for r, (tile, off) in enumerate(starts):
            x = dph[pl.ds(pl.multiple_of(g * 64, 64) + 8 * r, 8), :]
            if off:
                x = pltpu.roll(x, off, 1)
            if off + BOX > 128:
                tiles[tile + 1] += jnp.where(lane < off, x, 0.0)
                x = jnp.where(lane < off, 0.0, x)
            tiles[tile] += x
        x = jnp.concatenate(split(lanes(*tiles)))
        modes = base3[0 : 2 * MODES, pl.ds(pl.multiple_of(g * PERIOD, 128), PERIOD)]
        return total + lax.dot_general(x, modes, (((1,), (1,)), ((), ())), preferred_element_type=f32)

    total = lax.fori_loop(0, BOX // 8, project, jnp.zeros((16, 128), f32), unroll=5)
    total = total[:8] + total[8:]
    gradient = total + pltpu.roll(total, MODES, 1)

    for j in range(GROUP):
        ret_send[j] = gradient[j : j + 1]
    part_send[0] = jnp.sum(gradient, axis=0, keepdims=True)

    groups = list(zip([*peers, me], (3, 2, 2, 2, 1, 1, 1, 0)))
    depths = [(z, 0)] + [(lax.rem(z + d, DEPTH), min(d, DEPTH - d)) for d in range(1, DEPTH)]
    ways = [(a + b, group, depth) for group, a in groups for depth, b in depths if a + b]
    for _, group, depth in sorted(ways, key=lambda way: -way[0]):
        remote(part_send, part_recv.at[pl.ds(place, 1)], "part", at(group, depth)).start()
    for t in peers:
        remote(ret_send.at[t], ret_recv.at[me], "ret", at(t, z)).start()
    part_recv[place] = part_send[0]
    ret_recv[me] = ret_send[me]

    r_at = lax.broadcasted_iota(jnp.int32, (2 * SIDE, 2 * BOX), 0)
    c_at = lax.broadcasted_iota(jnp.int32, (2 * SIDE, 2 * BOX), 1)
    mirrored = r_at >= SIDE
    k = jnp.where(mirrored, r_at - SIDE, r_at)
    minus = (k >= HALF) != mirrored
    k = jnp.where(k >= HALF, SIDE - k, k)
    k = jnp.where(k > 36, FOLD + 72 - k, k) + jnp.where(minus, BOX, 0)
    pick_rows = jnp.where(k == c_at, 1.0, 0.0).astype(bf16)
    r_at = lax.broadcasted_iota(jnp.int32, (128, 256), 0)
    c_at = lax.broadcasted_iota(jnp.int32, (128, 256), 1)
    flip_columns = jnp.where(
        jnp.logical_and(r_at + c_at == SIDE, jnp.logical_and(c_at >= HALF, c_at < SIDE)), 1.0, 0.0
    ).astype(bf16)
    parts = [mm(pick_rows, part) for part in split(lanes(ore[...], oim[...]))]
    lane_full = lax.broadcasted_iota(jnp.int32, (SIDE, 128), 1)
    for n, sign in ((0, 1.0), (1, -1.0)):
        at_n = slice(n * 128, n * 128 + 128)
        half = parts[0][:SIDE, at_n] + parts[1][:SIDE, at_n]
        mirror = [mm(part[SIDE:, at_n].astype(bf16), flip_columns) for part in parts]
        mirror = sign * (mirror[0] + mirror[1])
        full[2 * n] = jnp.where(lane_full < HALF, half, mirror[:, :128])
        full[2 * n + 1] = mirror[:, 128:]
    first_row = z * 9 // 4
    for n in range(2):
        placed = [jnp.zeros((8, 128), f32) for _ in range(6)]
        for t in range(3):
            for piece in range(2):
                x = full[2 * n + piece, pl.ds(first_row + t, GROUP, stride=SIDE // GROUP), :]
                tile, off = divmod(SIDE * t + 128 * piece, 128)
                if off:
                    x = pltpu.roll(x, off, 1)
                    placed[tile + 1] += jnp.where(lane < off, x, 0.0)
                    x = jnp.where(lane < off, 0.0, x)
                placed[tile] += x
        placed = lanes(*placed)
        picked = jnp.zeros((8, 384), f32)
        for m in range(4):
            moved = pltpu.roll(placed, 768 - 36 * m, 1) if m else placed
            picked = picked + jnp.where(lax.rem(z, 4) == m, 1.0, 0.0) * moved[:, :384]
        for i in range(GROUP):
            out_send[i, n : n + 1, :] = picked[i : i + 1]
    for t in peers:
        remote(out_send.at[t], out_recv.at[me], "out", at(t, z)).start()
    out_recv[me] = out_send[me]

    rest = {
        "coef": coef_recv.at[pl.ds(0, GROUP - 1)],
        "own": all_own,
        "cross": all_cross,
        "img_close": img.at[pl.ds(0, 3)],
        "img_mid": img.at[pl.ds(0, 2)],
        "img_last": img.at[pl.ds(0, 2)],
        "pow": pow_recv.at[pl.ds(0, DEPTH - 1)],
        "sum": sum_recv.at[pl.ds(0, DEPTH - 1)],
        "obj": obj_all.at[pl.ds(0, DEPTH - 1)],
        "out": out_recv.at[pl.ds(0, GROUP - 1)],
        "ret": ret_recv.at[pl.ds(0, GROUP - 1)],
        "part": part_recv.at[pl.ds(0, FRAMES - 1)],
    }
    for exchange, ref in rest.items():
        everything(ref, exchange).wait_send()
    everything(rest["out"], "out").wait_recv()
    for p in range(GROUP):
        object_out[p] = out_recv[p, 0:2, :SHARE]
    everything(rest["ret"], "ret").wait_recv()
    everything(rest["part"], "part").wait_recv()
    for p in range(GROUP):
        mean = part_recv[p * DEPTH]
        for n in range(1, DEPTH):
            mean = mean + part_recv[p * DEPTH + n]
        gradient_out[0, p : p + 1, :] = (ret_recv[p] - mean * (1.0 / FRAMES))[:, :MODES]


def body(sky_image, coefficients, mode_basis, aperture):
    vmem, dma = pltpu.VMEM, pltpu.SemaphoreType.DMA
    scratch = [
        vmem(TABLE.shape, bf16), vmem((640, 256), f32), vmem((GROUP, MODES), f32),
        vmem((GROUP, 1, 128), f32), vmem((GROUP, 1, 128), f32), vmem((SIDE, SIDE), jnp.int32), vmem((MODES, FLAT), f32),
        vmem((3 * MODES, FLAT), bf16),
        vmem((4, 4, 8, SIDE), f32), vmem((GROUP, SIDE, 128), f32), vmem((GROUP, 2, 8, SIDE), f32),
        vmem((GROUP, SIDE, 128), f32), vmem((8 * BOX, 128), f32), vmem((8 * BOX, 128), f32),
        *[vmem((GROUP, 2 * BOX, 128), f32)] * 8,
        vmem((2, 2 * BOX, 128), f32), vmem((FOLD, 128), f32),
        *[vmem((DEPTH, 2 * CHUNK, 128), f32)] * 2, *[vmem((DEPTH, 4 * CHUNK, 128), f32)] * 2,
        vmem((4 * CHUNK, 128), f32), vmem((DEPTH, 4 * CHUNK, 128), f32), vmem((2 * BOX, 128), f32), vmem((2 * BOX, 128), f32),
        vmem((8 * BOX, 128), f32), vmem((4, SIDE, 128), f32), vmem((GROUP, 8, 384), f32), vmem((GROUP, 8, 384), f32),
        vmem((1, 1, 128), f32), vmem((FRAMES, 1, 128), f32), vmem((GROUP, 1, 128), f32), vmem((GROUP, 1, 128), f32),
        dma((7,)), dma((len(EXCHANGES),)), dma((len(EXCHANGES),)),
    ]
    return pl.pallas_call(
        kernel,
        out_shape=(
            pltpu.VMEM((1, GROUP, MODES), f32),
            pltpu.VMEM((GROUP, 2, SHARE), f32),
        ),
        in_specs=[pl.BlockSpec(memory_space=pl.ANY)] * 5,
        out_specs=[pl.BlockSpec(memory_space=pltpu.VMEM)] * 2,
        scratch_shapes=scratch,
        compiler_params=pltpu.CompilerParams(collective_id=0, has_side_effects=True, vmem_limit_bytes=60 * 2**20),
    )(sky_image, coefficients, mode_basis, aperture, jnp.asarray(TABLE))


def solution(mesh):
    in_specs = (P("frame", None, "patch"), P("frame", "patch", None), P(), P())
    out_specs = (P("frame", "patch", None), P("patch", None, "frame"))
    return jax.shard_map(body, mesh=mesh, in_specs=in_specs, out_specs=out_specs, check_vma=False)
```

```python
import math

import jax
import jax.numpy as jnp
import ml_dtypes
import numpy as np
from jax import lax
from jax.experimental import pallas as pl
from jax.experimental.pallas import tpu as pltpu
from jax.sharding import PartitionSpec as P

SIDE = 144
RIM = 8
TILE = SIDE - 2 * RIM
LOW, BOX = 32, 80
GROUP = 8
DEPTH = 8
STRIPS = 4
FRAMES = GROUP * DEPTH
HALF = SIDE // 2 + 1
FOLD = BOX // 2
CHUNK = FOLD // DEPTH
FLAT = BOX * SIDE
PERIOD = 8 * SIDE
MODES = 64
UNROLL = GROUP
SHARE = SIDE * SIDE // FRAMES
DAMPING = 0.02 * FRAMES
EXCHANGES = ("coef", "own", "cross", "img_close", "img_mid", "img_last", "pow", "sum", "obj", "out", "ret", "part")
FAR_FIRST = (4, 3, 5, 2, 6, 1, 7)
MESH = pl.DeviceIdType.MESH
f32, bf16 = jnp.float32, jnp.bfloat16


def profile():
    at = np.arange(SIDE, dtype=np.float64)
    distance = np.minimum(at, SIDE - 1 - at)
    taper = 0.3 + 0.7 * np.sin(math.pi * (distance + 1.0) / (2.0 * (RIM + 1))) ** 2
    return np.where(distance < RIM, taper, 1.0)


def tables():
    k = np.arange(HALF)
    y = np.arange(SIDE)
    u = np.arange(BOX) + LOW - SIDE // 2
    weight = np.ones(HALF)
    weight[0] = weight[-1] = 0.5

    def pair(a, b):
        angle = 2.0 * math.pi / SIDE * (np.outer(a, b) % SIDE)
        return np.cos(angle), np.sin(angle)

    def cut(t):
        high = t.astype(ml_dtypes.bfloat16)
        return high, (t - high.astype(np.float64)).astype(ml_dtypes.bfloat16)

    def rows_of(*blocks):
        t = np.zeros((BOX * len(blocks), blocks[0].shape[1]))
        for n, block in enumerate(blocks):
            t[n * BOX : n * BOX + block.shape[0]] = block
        high, low = cut(t)
        return np.concatenate([high, high, low], axis=1)

    def columns_of(c, s):
        t = np.zeros((-(-c.shape[0] // 16) * 16, 256))
        t[: c.shape[0], : c.shape[1]], t[: c.shape[0], 128 : 128 + c.shape[1]] = c, s
        return cut(t)

    def twice(c, s):
        t = np.zeros((BOX, 256))
        t[: c.shape[0], : c.shape[1]], t[: c.shape[0], 128 : 128 + c.shape[1]] = c, s
        high, low = cut(t)
        return np.concatenate([high, high, low])

    parts = {}
    c, s = pair(k, u)
    parts["pupil_rows"] = rows_of(c, s)
    parts["pupil_columns"] = twice(c.T, s.T)
    parts["back_columns"] = twice(weight[:, None] * c, weight[:, None] * s)

    def wide(t):
        return np.pad(t, ((0, BOX - t.shape[0]), (0, BOX - t.shape[1])))

    parts["back_even"], parts["back_odd"] = rows_of(wide(c.T * weight)), rows_of(wide(s.T * weight))
    c, s = pair(k, k)
    parts["focal_columns"] = twice(weight[:, None] * c, -weight[:, None] * s)
    disc = np.concatenate([np.arange(37), [0] * 3, np.arange(72, 36, -1), [0] * 4])
    used = np.concatenate([np.ones(37), [0] * 3, np.ones(36), [0] * 4])
    parts["focal_even"] = rows_of(wide((c * weight)[disc] * used[:, None]))
    parts["focal_odd"] = rows_of(wide((s * weight)[disc] * used[:, None]))
    parts["disc_even"] = rows_of(wide((c * weight)[:, disc] * used))
    parts["disc_odd"] = rows_of(wide((s * weight)[:, disc] * used))
    w = profile()
    c, s = pair(k, y)
    t = rows_of((c * w / SIDE)[disc] * used[:, None], (s * w / SIDE)[disc] * used[:, None])
    parts["data_rows"], parts["data_rows_end"] = t[:, :256], t[:, 256:]
    order = np.concatenate([y[RIM:-RIM], y[:RIM], y[-RIM:]])
    parts["data_columns"], parts["data_columns_low"] = columns_of(
        (w[:, None] * c.T)[order], -(w[:, None] * s.T)[order]
    )
    first, rows, total = {}, [], 0
    for name, part in parts.items():
        first[name] = (total, *part.shape)
        total += part.shape[0]
        rows.append(np.pad(part, ((0, 0), (0, 256 - part.shape[1]))))
    return np.concatenate(rows), first


TABLE, FIRST = tables()


def split(x):
    high = x.astype(bf16)
    return high, (x - high.astype(f32)).astype(bf16)


def mm(a, b):
    return jnp.dot(a, b, preferred_element_type=f32)


def mm3(a, b):
    return mm(a[0], b[0]) + (mm(a[0], b[1]) + mm(a[1], b[0]))


def lanes(*parts):
    return jnp.concatenate(parts, axis=1)


def sine_cosine(x):
    quarter = jnp.floor(x * (2.0 / math.pi) + 0.5)
    r = x - quarter * 1.5703125
    r = r - quarter * 4.837512969970703125e-4
    r = r - quarter * 7.54978995489188216e-8
    z = r * r
    sine = ((-1.9515295891e-4 * z + 8.3321608736e-3) * z - 1.6666654611e-1) * z * r + r
    cosine = ((2.443315711809948e-5 * z - 1.388731625493765e-3) * z + 4.166664568298827e-2) * z * z - 0.5 * z + 1.0
    halves = jnp.floor(quarter * 0.5)
    odd = quarter - 2.0 * halves
    minus = 1.0 - 2.0 * (halves - 2.0 * jnp.floor(halves * 0.5))
    swap = odd > 0.5
    return (
        jnp.where(swap, cosine, sine) * minus,
        jnp.where(swap, -sine, cosine) * minus,
    )


def kernel(
    sky, coef, basis, aperture, table_hbm,
    gradient_out, object_out,
    tab, skyp, coef_v, coef_send, coef_recv, mask_v, base, base3,
    edges, img, halo, turned, pre, pim, fpr, fpi, fmr, fmi, tre, tim, dre, dim_,
    sums, packed, pow_send, pow_recv, sum_send, sum_recv, obj_send, obj_all, ore, oim, dph,
    full, out_send, out_recv, part_send, part_recv, ret_send, ret_recv,
    local_sem, send_sem, recv_sem,
):
    place, strip = lax.axis_index("frame"), lax.axis_index("patch")
    me, z = place // DEPTH, place % DEPTH

    y, x = me // 2, me % 2
    other = 1 - x
    near, far, back_y = y + 1 - 2 * (y % 2), 3 - y, (y + 2) % 4
    close = [near * 2 + x, far * 2 + x, y * 2 + other]
    distant = [near * 2 + other, far * 2 + other, back_y * 2 + x, back_y * 2 + other]
    peers = distant[::-1] + close[::-1]

    def at(group, depth, which=None):
        return {"frame": group * DEPTH + depth, "patch": strip if which is None else which}

    def remote(src, dst, exchange, device):
        at_sem = EXCHANGES.index(exchange)
        return pltpu.make_async_remote_copy(
            src_ref=src, dst_ref=dst, send_sem=send_sem.at[at_sem], recv_sem=recv_sem.at[at_sem],
            device_id=device, device_id_type=MESH,
        )

    def everything(ref, exchange):
        return remote(ref, ref, exchange, at(peers[0], z))

    def table(name, half=None):
        row, count, width = FIRST[name]
        if half is None:
            return tab[row : row + count, :width]
        return tab[row : row + count, half * 128 : half * 128 + 128]

    def from_left(name, x):
        h, r = split(x)
        return mm(table(name), jnp.concatenate([h, r, h]))

    def from_right(x, name, half=None):
        h, r = split(x)
        return mm(lanes(h[:, :BOX], r[:, :BOX], h[:, :BOX]), table(name, half))

    loads = [
        pltpu.make_async_copy(coef.at[0], coef_v, local_sem.at[0]),
        pltpu.make_async_copy(basis.at[:, pl.ds(LOW * SIDE, FLAT)], base, local_sem.at[1]),
        pltpu.make_async_copy(sky.at[0], skyp.at[pl.ds(RIM, 512)], local_sem.at[2]),
        pltpu.make_async_copy(table_hbm, tab, local_sem.at[3]),
        pltpu.make_async_copy(aperture, mask_v, local_sem.at[4]),
    ]
    for load in loads:
        load.start()

    barrier = pltpu.get_barrier_semaphore()
    beside = lax.rem(strip + jnp.where(me < 4, STRIPS - 1, 1), STRIPS)

    def greet(device):
        pl.semaphore_signal(barrier, inc=1, device_id=device, device_id_type=MESH)

    for d in FAR_FIRST:
        greet(at(me, lax.rem(z + d, DEPTH)))
    for t in [*peers, me]:
        greet(at(t, z, beside))
    for t in peers:
        greet(at(t, z))

    skyp[pl.ds(0, RIM), :] = jnp.zeros((RIM, 256), f32)
    skyp[pl.ds(512 + RIM, 120), :] = jnp.zeros((120, 256), f32)
    loads[0].wait()
    for p in range(GROUP):
        row = coef_v[p : p + 1, :]
        coef_send[p] = lanes(row, row)
    loads[2].wait()
    for half in range(2):
        strip_t = skyp[:, half * 128 : half * 128 + 128].T
        for r in range(4):
            edges[2 * half, r] = strip_t[:8, r * TILE : r * TILE + SIDE]
            edges[2 * half + 1, r] = strip_t[120:, r * TILE : r * TILE + SIDE]
    pl.semaphore_wait(barrier, GROUP - 1 + DEPTH - 1 + GROUP)

    for t in peers:
        remote(coef_send.at[t], coef_recv.at[me], "coef", at(t, z)).start()
    coef_recv[me] = coef_send[me]

    def main_of(t):
        return skyp.at[
            pl.ds(pl.multiple_of(lax.rem(t, 4) * TILE, TILE), SIDE), pl.ds(pl.multiple_of((t // 4) * 128, 128), 128)
        ]

    def edge_of(kind, t):
        return edges.at[kind, lax.rem(t, 4)]

    for t in peers:
        kind, side = jnp.where(t < 4, 2, 1), jnp.where(t < 4, 1, 0)
        remote(edge_of(kind, t), halo.at[me, side], "own", at(t, z)).start()
    for p in range(GROUP):
        kind, side, step = (3, 0, 1) if p < 4 else (0, 1, STRIPS - 1)
        remote(edge_of(kind, p), halo.at[me, side], "cross", at(p, z, lax.rem(strip + step, STRIPS))).start()
    batches = {"img_close": close, "img_mid": distant[:2], "img_last": distant[2:]}
    for exchange, partners in batches.items():
        for t in partners:
            remote(main_of(t), img.at[me], exchange, at(t, z)).start()
    own_side = jnp.where(me < 4, 1, 0)
    mine = [
        pltpu.make_async_copy(main_of(me), img.at[me], local_sem.at[5]),
        pltpu.make_async_copy(edge_of(jnp.where(me < 4, 2, 1), me), halo.at[me, own_side], local_sem.at[6]),
    ]
    for c in mine:
        c.start()

    loads[1].wait()

    def cut(g, carry):
        at_g = pl.ds(pl.multiple_of(g * PERIOD, 128), PERIOD)
        x = base[:, at_g]
        h, r = split(x)
        base3[0:MODES, at_g] = h
        base3[MODES : 2 * MODES, at_g] = r
        base3[2 * MODES :, at_g] = (x - h.astype(f32) - r.astype(f32)).astype(bf16)
        return carry

    lax.fori_loop(0, BOX // 8, cut, 0)
    for load in loads[3:]:
        load.wait()

    lane = lax.broadcasted_iota(jnp.int32, (8, 128), 1)
    mask = mask_v[LOW : LOW + BOX, 0:128].astype(f32)
    mask = pltpu.roll(mask, 128 - LOW, 1)
    mask = jnp.where(lax.broadcasted_iota(jnp.int32, (BOX, 128), 1) < BOX, mask, 0.0)
    dph[0:BOX, :] = mask * jnp.sqrt(jnp.full((BOX, 128), 1.0 / (SIDE * SIDE), f32) / jnp.sum(mask))

    everything(coef_recv.at[pl.ds(0, GROUP - 1)], "coef").wait_recv()
    weights = jnp.concatenate([coef_recv[j] for j in range(GROUP)])
    w0 = weights.astype(bf16).astype(f32)
    w1 = (weights - w0).astype(bf16).astype(f32)
    w2 = weights - w0 - w1
    weights = jnp.concatenate([lanes(w, w[:, :MODES]) for w in (w0, w1, w2)]).astype(bf16)

    starts = [divmod(SIDE * r + LOW, 128) for r in range(8)]

    def pupils(g, carry):
        ph = mm(weights, base3[:, pl.ds(pl.multiple_of(g * PERIOD, 128), PERIOD)])
        ph = ph[0:8] + (ph[8:16] + ph[16:24])
        rows = []
        for tile, off in starts:
            x = ph[:, tile * 128 : tile * 128 + 128]
            if off:
                x = pltpu.roll(x, 128 - off, 1)
            if off + BOX > 128:
                y = pltpu.roll(ph[:, tile * 128 + 128 : tile * 128 + 256], 128 - off, 1)
                x = jnp.where(lane < 128 - off, x, y)
            rows.append(x)
        m = dph[pl.ds(pl.multiple_of(g * 8, 8), 8), :]
        m = jnp.concatenate([jnp.broadcast_to(m[r : r + 1], (8, 128)) for r in range(8)])
        sine, cosine = sine_cosine(jnp.concatenate(rows))
        at_g = pl.ds(pl.multiple_of(g * 64, 64), 64)
        pre[at_g, :] = m * cosine
        pim[at_g, :] = m * sine
        return carry

    lax.fori_loop(0, BOX // 8, pupils, 0, unroll=5)

    def of_frame(ref, f):
        return ref[pl.ds(f, BOX, stride=GROUP), :]

    def fold(x):
        return x[:BOX] + x[BOX:], x[:BOX] - x[BOX:]

    def stack(*parts):
        return jnp.concatenate(parts)

    def transfers(n, carry):
        fs = [n * UNROLL + m for m in range(UNROLL)]
        rows = []
        for f in fs:
            y = from_left("pupil_rows", lanes(of_frame(pre, f), of_frame(pim, f)))
            cr, ci, sr, si = y[:BOX, :128], y[:BOX, 128:], y[BOX:, :128], y[BOX:, 128:]
            rows += [cr + si, cr - si, ci - sr, ci + sr]
        y = from_right(stack(*rows), "pupil_columns")
        even, odd = [], []
        for m, f in enumerate(fs):
            r, i = y[4 * m * BOX : (4 * m + 2) * BOX], y[(4 * m + 2) * BOX : (4 * m + 4) * BOX]
            p_re, p_im = r[:, :128] + i[:, 128:], i[:, :128] - r[:, 128:]
            m_re, m_im = r[:, :128] - i[:, 128:], i[:, :128] + r[:, 128:]
            fpr[f], fpi[f], fmr[f], fmi[f] = p_re, p_im, m_re, m_im
            plus = p_re * p_re + p_im * p_im
            minus = m_re * m_re + m_im * m_im
            even += fold(plus + minus)
            odd += fold(plus - minus)
        x_re = from_right(stack(*even), "focal_columns", 0)
        x_im = from_right(stack(*odd), "focal_columns", 1)
        for m, f in enumerate(fs):
            x = lanes(x_re[2 * m * BOX : 2 * (m + 1) * BOX], x_im[2 * m * BOX : 2 * (m + 1) * BOX])
            c = from_left("focal_even", x[:BOX])
            s = from_left("focal_odd", x[BOX:])
            cr, ci, sr, si = c[:, :128], c[:, 128:], s[:, :128], s[:, 128:]
            tre[f] = stack(cr + si, cr - si)
            tim[f] = stack(ci - sr, ci + sr)
        return carry

    lax.fori_loop(0, GROUP // UNROLL, transfers, 0)

    lane40 = lax.broadcasted_iota(jnp.int32, (FOLD, 128), 1)
    row40 = lax.broadcasted_iota(jnp.int32, (FOLD, 128), 0)
    border = jnp.where(row40 < 24, 73, jnp.where(row40 < 32, 68, 65))

    def shifted(x, back):
        return stack(*[
            pltpu.roll(x[a:b], 128 - by if back else by, 1) for a, b, by in ((0, 24, 73), (24, 32, 68), (32, 40, 65))
        ])

    def pack(x, into, at_row):
        for sign in range(2):
            wide, narrow = x[sign * BOX : sign * BOX + FOLD], x[sign * BOX + FOLD : (sign + 1) * BOX]
            packed[...] = jnp.where(lane40 < border, wide, shifted(narrow, False))
            for d in range(DEPTH):
                into[d, at_row + sign * CHUNK : at_row + (sign + 1) * CHUNK, :] = packed[d * CHUNK : (d + 1) * CHUNK, :]

    power = jnp.zeros((2 * BOX, 128), f32)
    for f in range(GROUP):
        power = power + (tre[f] * tre[f] + tim[f] * tim[f])
    pack(power, pow_send, 0)
    for d in FAR_FIRST:
        t = lax.rem(z + d, DEPTH)
        remote(pow_send.at[t], pow_recv.at[z], "pow", at(me, t)).start()
    pow_recv[z] = pow_send[z]

    for c in mine:
        c.wait()
    all_own, all_cross = halo.at[pl.ds(0, GROUP - 1), 0], halo.at[:, 0]
    everything(all_cross, "cross").wait_recv()
    everything(all_own, "own").wait_recv()
    row = lax.broadcasted_iota(jnp.int32, (128, 256), 0)
    left_on = jnp.where(jnp.logical_and(strip == 0, me < 4), 0.0, 1.0)
    right_on = jnp.where(jnp.logical_and(strip == STRIPS - 1, me >= 4), 0.0, 1.0)
    rims = lanes(halo[...].reshape(128, SIDE), jnp.zeros((128, 256 - SIDE), f32))
    rims = rims * jnp.where(lax.rem(row, 16) < 8, left_on, right_on)
    rims = rims.T[:SIDE]
    for f in range(GROUP):
        turned[f] = pltpu.roll(rims, (128 - 16 * f) % 128, 1) if f else rims

    sums[...] = jnp.zeros_like(sums)

    def data(fs):
        h, r = split(stack(*[lanes(img[f], turned[f]) for f in fs]))
        x = mm3((h[:, :SIDE], r[:, :SIDE]), (table("data_columns"), table("data_columns_low")))
        n_re, n_im = sums[0], sums[1]
        for m, f in enumerate(fs):
            h, r = split(x[m * SIDE : (m + 1) * SIDE])
            h = stack(h, r, h)
            y = mm(table("data_rows"), h[:256]) + mm(table("data_rows_end"), h[256:])
            cr, ci, sr, si = y[:BOX, :128], y[:BOX, 128:], y[BOX:, :128], y[BOX:, 128:]
            d_re, d_im = stack(cr + si, cr - si), stack(ci - sr, ci + sr)
            dre[f] = d_re
            dim_[f] = d_im
            t_re, t_im = tre[f], tim[f]
            n_re = n_re + (t_re * d_re + t_im * d_im)
            n_im = n_im + (t_re * d_im - t_im * d_re)
        sums[0], sums[1] = n_re, n_im

    everything(img.at[pl.ds(0, 3)], "img_close").wait_recv()
    data([me, *close])
    everything(img.at[pl.ds(0, 2)], "img_mid").wait_recv()
    data(distant[:2])
    everything(img.at[pl.ds(0, 2)], "img_last").wait_recv()
    data(distant[2:])

    pack(sums[0], sum_send, 0)
    pack(sums[1], sum_send, 2 * CHUNK)
    for d in FAR_FIRST:
        t = lax.rem(z + d, DEPTH)
        remote(sum_send.at[t], sum_recv.at[z], "sum", at(me, t)).start()
    sum_recv[z] = sum_send[z]
    everything(pow_recv.at[pl.ds(0, DEPTH - 1)], "pow").wait_recv()
    power = pow_recv[0]
    for j in range(1, DEPTH):
        power = power + pow_recv[j]
    power = power + DAMPING
    everything(sum_recv.at[pl.ds(0, DEPTH - 1)], "sum").wait_recv()
    total = sum_recv[0]
    for j in range(1, DEPTH):
        total = total + sum_recv[j]
    obj_send[...] = total / stack(power, power)
    for d in FAR_FIRST:
        t = lax.rem(z + d, DEPTH)
        remote(obj_send, obj_all.at[z], "obj", at(me, t)).start()
    obj_all[z] = obj_send[...]
    everything(obj_all.at[pl.ds(0, DEPTH - 1)], "obj").wait_recv()
    for part, ref in enumerate((ore, oim)):
        for sign in range(2):
            at_row = (2 * part + sign) * CHUNK
            for d in range(DEPTH):
                packed[d * CHUNK : (d + 1) * CHUNK, :] = obj_all[d, at_row : at_row + CHUNK, :]
            x = packed[...]
            ref[sign * BOX : sign * BOX + FOLD, :] = jnp.where(lane40 < jnp.minimum(border, HALF), x, 0.0)
            ref[sign * BOX + FOLD : (sign + 1) * BOX, :] = jnp.where(lane40 < 128 - border, shifted(x, True), 0.0)

    scale = 4.0 * 2.0 / (SIDE * SIDE)

    def back(n, carry):
        fs = [n * UNROLL + m for m in range(UNROLL)]
        o_re, o_im = -scale * ore[...], -scale * oim[...]
        o_square = scale * (ore[...] * ore[...] + oim[...] * oim[...])
        h_re, h_im = [], []
        for f in fs:
            d_re, d_im = dre[f], dim_[f]
            re_even, re_odd = fold(d_re * o_re + d_im * o_im + o_square * tre[f])
            im_even, im_odd = fold(d_im * o_re - d_re * o_im + o_square * tim[f])
            c = from_left("disc_even", lanes(re_even, im_even))
            s = from_left("disc_odd", lanes(re_odd, im_odd))
            cr, ci, sr, si = c[:, :128], c[:, 128:], s[:, :128], s[:, 128:]
            h_re += [cr - si, cr + si]
            h_im += [ci + sr, ci - sr]
        even = from_right(stack(*h_re), "focal_columns", 0)
        odd = from_right(stack(*h_im), "focal_columns", 1)
        sum_rows, gap_rows = [], []
        for m, f in enumerate(fs):
            at_m = slice(2 * m * BOX, 2 * (m + 1) * BOX)
            plus, minus = even[at_m] + odd[at_m], even[at_m] - odd[at_m]
            p_re, p_im, m_re, m_im = plus * fpr[f], plus * fpi[f], minus * fmr[f], minus * fmi[f]
            sum_rows += [p_re + m_re, p_im + m_im]
            gap_rows += [p_re - m_re, p_im - m_im]
        qc = from_right(stack(*sum_rows), "back_columns", 0)
        qs = from_right(stack(*gap_rows), "back_columns", 1)
        for m, f in enumerate(fs):
            at_re, at_im = slice(4 * m * BOX, (4 * m + 2) * BOX), slice((4 * m + 2) * BOX, (4 * m + 4) * BOX)
            re_even, re_odd = fold(qc[at_re] - qs[at_im])
            im_even, im_odd = fold(qc[at_im] + qs[at_re])
            c = from_left("back_even", lanes(re_even, im_even))
            s = from_left("back_odd", lanes(re_odd, im_odd))
            g_re, g_im = c[:, :128] - s[:, 128:], c[:, 128:] + s[:, :128]
            dph[pl.ds(f, BOX, stride=GROUP), :] = of_frame(pre, f) * g_im - of_frame(pim, f) * g_re
        return carry

    lax.fori_loop(0, GROUP // UNROLL, back, 0)

    def project(g, total):
        tiles = [jnp.zeros((8, 128), f32) for _ in range(9)]
        for r, (tile, off) in enumerate(starts):
            x = dph[pl.ds(pl.multiple_of(g * 64, 64) + 8 * r, 8), :]
            if off:
                x = pltpu.roll(x, off, 1)
            if off + BOX > 128:
                tiles[tile + 1] += jnp.where(lane < off, x, 0.0)
                x = jnp.where(lane < off, 0.0, x)
            tiles[tile] += x
        x = jnp.concatenate(split(lanes(*tiles)))
        modes = base3[0 : 2 * MODES, pl.ds(pl.multiple_of(g * PERIOD, 128), PERIOD)]
        return total + lax.dot_general(x, modes, (((1,), (1,)), ((), ())), preferred_element_type=f32)

    total = lax.fori_loop(0, BOX // 8, project, jnp.zeros((16, 128), f32), unroll=5)
    total = total[:8] + total[8:]
    gradient = total + pltpu.roll(total, MODES, 1)

    for j in range(GROUP):
        ret_send[j] = gradient[j : j + 1]
    part_send[0] = jnp.sum(gradient, axis=0, keepdims=True)

    groups = list(zip([*peers, me], (3, 2, 2, 2, 1, 1, 1, 0)))
    depths = [(z, 0)] + [(lax.rem(z + d, DEPTH), min(d, DEPTH - d)) for d in range(1, DEPTH)]
    ways = [(a + b, group, depth) for group, a in groups for depth, b in depths if a + b]
    for _, group, depth in sorted(ways, key=lambda way: -way[0]):
        remote(part_send, part_recv.at[pl.ds(place, 1)], "part", at(group, depth)).start()
    for t in peers:
        remote(ret_send.at[t], ret_recv.at[me], "ret", at(t, z)).start()
    part_recv[place] = part_send[0]
    ret_recv[me] = ret_send[me]

    r_at = lax.broadcasted_iota(jnp.int32, (2 * SIDE, 2 * BOX), 0)
    c_at = lax.broadcasted_iota(jnp.int32, (2 * SIDE, 2 * BOX), 1)
    mirrored = r_at >= SIDE
    k = jnp.where(mirrored, r_at - SIDE, r_at)
    minus = (k >= HALF) != mirrored
    k = jnp.where(k >= HALF, SIDE - k, k)
    k = jnp.where(k > 36, FOLD + 72 - k, k) + jnp.where(minus, BOX, 0)
    pick_rows = jnp.where(k == c_at, 1.0, 0.0).astype(bf16)
    r_at = lax.broadcasted_iota(jnp.int32, (128, 256), 0)
    c_at = lax.broadcasted_iota(jnp.int32, (128, 256), 1)
    flip_columns = jnp.where(
        jnp.logical_and(r_at + c_at == SIDE, jnp.logical_and(c_at >= HALF, c_at < SIDE)), 1.0, 0.0
    ).astype(bf16)
    parts = [mm(pick_rows, part) for part in split(lanes(ore[...], oim[...]))]
    lane_full = lax.broadcasted_iota(jnp.int32, (SIDE, 128), 1)
    for n, sign in ((0, 1.0), (1, -1.0)):
        at_n = slice(n * 128, n * 128 + 128)
        half = parts[0][:SIDE, at_n] + parts[1][:SIDE, at_n]
        mirror = [mm(part[SIDE:, at_n].astype(bf16), flip_columns) for part in parts]
        mirror = sign * (mirror[0] + mirror[1])
        full[2 * n] = jnp.where(lane_full < HALF, half, mirror[:, :128])
        full[2 * n + 1] = mirror[:, 128:]
    first_row = z * 9 // 4
    for n in range(2):
        placed = [jnp.zeros((8, 128), f32) for _ in range(6)]
        for t in range(3):
            for piece in range(2):
                x = full[2 * n + piece, pl.ds(first_row + t, GROUP, stride=SIDE // GROUP), :]
                tile, off = divmod(SIDE * t + 128 * piece, 128)
                if off:
                    x = pltpu.roll(x, off, 1)
                    placed[tile + 1] += jnp.where(lane < off, x, 0.0)
                    x = jnp.where(lane < off, 0.0, x)
                placed[tile] += x
        placed = lanes(*placed)
        picked = jnp.zeros((8, 384), f32)
        for m in range(4):
            moved = pltpu.roll(placed, 768 - 36 * m, 1) if m else placed
            picked = picked + jnp.where(lax.rem(z, 4) == m, 1.0, 0.0) * moved[:, :384]
        for i in range(GROUP):
            out_send[i, n : n + 1, :] = picked[i : i + 1]
    for t in peers:
        remote(out_send.at[t], out_recv.at[me], "out", at(t, z)).start()
    out_recv[me] = out_send[me]

    rest = {
        "coef": coef_recv.at[pl.ds(0, GROUP - 1)],
        "own": all_own,
        "cross": all_cross,
        "img_close": img.at[pl.ds(0, 3)],
        "img_mid": img.at[pl.ds(0, 2)],
        "img_last": img.at[pl.ds(0, 2)],
        "pow": pow_recv.at[pl.ds(0, DEPTH - 1)],
        "sum": sum_recv.at[pl.ds(0, DEPTH - 1)],
        "obj": obj_all.at[pl.ds(0, DEPTH - 1)],
        "out": out_recv.at[pl.ds(0, GROUP - 1)],
        "ret": ret_recv.at[pl.ds(0, GROUP - 1)],
        "part": part_recv.at[pl.ds(0, FRAMES - 1)],
    }
    for exchange, ref in rest.items():
        everything(ref, exchange).wait_send()
    everything(rest["out"], "out").wait_recv()
    for p in range(GROUP):
        object_out[p] = out_recv[p, :, :SHARE]
    everything(rest["ret"], "ret").wait_recv()
    everything(rest["part"], "part").wait_recv()
    for p in range(GROUP):
        mean = part_recv[p * DEPTH]
        for n in range(1, DEPTH):
            mean = mean + part_recv[p * DEPTH + n]
        gradient_out[0, p : p + 1, :] = (ret_recv[p] - mean * (1.0 / FRAMES))[:, :MODES]


def body(sky_image, coefficients, mode_basis, aperture):
    vmem, dma = pltpu.VMEM, pltpu.SemaphoreType.DMA
    scratch = [
        vmem(TABLE.shape, bf16), vmem((640, 256), f32), vmem((GROUP, MODES), f32),
        vmem((GROUP, 1, 128), f32), vmem((GROUP, 1, 128), f32), vmem((SIDE, SIDE), jnp.int32), vmem((MODES, FLAT), f32),
        vmem((3 * MODES, FLAT), bf16),
        vmem((4, 4, 8, SIDE), f32), vmem((GROUP, SIDE, 128), f32), vmem((GROUP, 2, 8, SIDE), f32),
        vmem((GROUP, SIDE, 128), f32), vmem((8 * BOX, 128), f32), vmem((8 * BOX, 128), f32),
        *[vmem((GROUP, 2 * BOX, 128), f32)] * 8,
        vmem((2, 2 * BOX, 128), f32), vmem((FOLD, 128), f32),
        *[vmem((DEPTH, 2 * CHUNK, 128), f32)] * 2, *[vmem((DEPTH, 4 * CHUNK, 128), f32)] * 2,
        vmem((4 * CHUNK, 128), f32), vmem((DEPTH, 4 * CHUNK, 128), f32), vmem((2 * BOX, 128), f32), vmem((2 * BOX, 128), f32),
        vmem((8 * BOX, 128), f32), vmem((4, SIDE, 128), f32), vmem((GROUP, 2, 384), f32), vmem((GROUP, 2, 384), f32),
        vmem((1, 1, 128), f32), vmem((FRAMES, 1, 128), f32), vmem((GROUP, 1, 128), f32), vmem((GROUP, 1, 128), f32),
        dma((7,)), dma((len(EXCHANGES),)), dma((len(EXCHANGES),)),
    ]
    return pl.pallas_call(
        kernel,
        out_shape=(
            pltpu.VMEM((1, GROUP, MODES), f32),
            pltpu.VMEM((GROUP, 2, SHARE), f32),
        ),
        in_specs=[pl.BlockSpec(memory_space=pl.ANY)] * 5,
        out_specs=[pl.BlockSpec(memory_space=pltpu.VMEM)] * 2,
        scratch_shapes=scratch,
        compiler_params=pltpu.CompilerParams(collective_id=0, has_side_effects=True, vmem_limit_bytes=60 * 2**20),
    )(sky_image, coefficients, mode_basis, aperture, jnp.asarray(TABLE))


def solution(mesh):
    in_specs = (P("frame", None, "patch"), P("frame", "patch", None), P(), P())
    out_specs = (P("frame", "patch", None), P("patch", None, "frame"))
    return jax.shard_map(body, mesh=mesh, in_specs=in_specs, out_specs=out_specs, check_vma=False)
```

```python
import math

import jax
import jax.numpy as jnp
import ml_dtypes
import numpy as np
from jax import lax
from jax.experimental import pallas as pl
from jax.experimental.pallas import tpu as pltpu
from jax.sharding import PartitionSpec as P

SIDE = 144
RIM = 8
TILE = SIDE - 2 * RIM
LOW, BOX = 32, 80
GROUP = 8
DEPTH = 8
STRIPS = 4
FRAMES = GROUP * DEPTH
HALF = SIDE // 2 + 1
FOLD = BOX // 2
CHUNK = FOLD // DEPTH
FLAT = BOX * SIDE
PERIOD = 8 * SIDE
MODES = 64
UNROLL = GROUP
SHARE = SIDE * SIDE // FRAMES
DAMPING = 0.02 * FRAMES
EXCHANGES = ("coef", "own", "cross", "img_close", "img_mid", "img_last", "pow", "sum", "obj", "out", "ret", "part")
FAR_FIRST = (4, 3, 5, 2, 6, 1, 7)
MESH = pl.DeviceIdType.MESH
f32, bf16 = jnp.float32, jnp.bfloat16


def profile():
    at = np.arange(SIDE, dtype=np.float64)
    distance = np.minimum(at, SIDE - 1 - at)
    taper = 0.3 + 0.7 * np.sin(math.pi * (distance + 1.0) / (2.0 * (RIM + 1))) ** 2
    return np.where(distance < RIM, taper, 1.0)


def tables():
    k = np.arange(HALF)
    y = np.arange(SIDE)
    u = np.arange(BOX) + LOW - SIDE // 2
    weight = np.ones(HALF)
    weight[0] = weight[-1] = 0.5

    def pair(a, b):
        angle = 2.0 * math.pi / SIDE * (np.outer(a, b) % SIDE)
        return np.cos(angle), np.sin(angle)

    def cut(t):
        high = t.astype(ml_dtypes.bfloat16)
        return high, (t - high.astype(np.float64)).astype(ml_dtypes.bfloat16)

    def rows_of(*blocks):
        t = np.zeros((BOX * len(blocks), blocks[0].shape[1]))
        for n, block in enumerate(blocks):
            t[n * BOX : n * BOX + block.shape[0]] = block
        high, low = cut(t)
        return np.concatenate([high, high, low], axis=1)

    def columns_of(c, s):
        t = np.zeros((-(-c.shape[0] // 16) * 16, 256))
        t[: c.shape[0], : c.shape[1]], t[: c.shape[0], 128 : 128 + c.shape[1]] = c, s
        return cut(t)

    def twice(c, s):
        t = np.zeros((BOX, 256))
        t[: c.shape[0], : c.shape[1]], t[: c.shape[0], 128 : 128 + c.shape[1]] = c, s
        high, low = cut(t)
        return np.concatenate([high, high, low])

    parts = {}
    c, s = pair(k, u)
    parts["pupil_rows"] = rows_of(c, s)
    parts["pupil_columns"] = twice(c.T, s.T)
    parts["back_columns"] = twice(weight[:, None] * c, weight[:, None] * s)

    def wide(t):
        return np.pad(t, ((0, BOX - t.shape[0]), (0, BOX - t.shape[1])))

    parts["back_even"], parts["back_odd"] = rows_of(wide(c.T * weight)), rows_of(wide(s.T * weight))
    c, s = pair(k, k)
    parts["focal_columns"] = twice(weight[:, None] * c, -weight[:, None] * s)
    disc = np.concatenate([np.arange(37), [0] * 3, np.arange(72, 36, -1), [0] * 4])
    used = np.concatenate([np.ones(37), [0] * 3, np.ones(36), [0] * 4])
    parts["focal_even"] = rows_of(wide((c * weight)[disc] * used[:, None]))
    parts["focal_odd"] = rows_of(wide((s * weight)[disc] * used[:, None]))
    parts["disc_even"] = rows_of(wide((c * weight)[:, disc] * used))
    parts["disc_odd"] = rows_of(wide((s * weight)[:, disc] * used))
    w = profile()
    c, s = pair(k, y)
    t = rows_of((c * w / SIDE)[disc] * used[:, None], (s * w / SIDE)[disc] * used[:, None])
    parts["data_rows"], parts["data_rows_end"] = t[:, :256], t[:, 256:]
    order = np.concatenate([y[RIM:-RIM], y[:RIM], y[-RIM:]])
    parts["data_columns"], parts["data_columns_low"] = columns_of(
        (w[:, None] * c.T)[order], -(w[:, None] * s.T)[order]
    )
    first, rows, total = {}, [], 0
    for name, part in parts.items():
        first[name] = (total, *part.shape)
        total += part.shape[0]
        rows.append(np.pad(part, ((0, 0), (0, 256 - part.shape[1]))))
    return np.concatenate(rows), first


TABLE, FIRST = tables()


def split(x):
    high = x.astype(bf16)
    return high, (x - high.astype(f32)).astype(bf16)


def mm(a, b):
    return jnp.dot(a, b, preferred_element_type=f32)


def mm3(a, b):
    return mm(a[0], b[0]) + (mm(a[0], b[1]) + mm(a[1], b[0]))


def lanes(*parts):
    return jnp.concatenate(parts, axis=1)


def sine_cosine(x):
    quarter = jnp.floor(x * (2.0 / math.pi) + 0.5)
    r = x - quarter * 1.5703125
    r = r - quarter * 4.837512969970703125e-4
    r = r - quarter * 7.54978995489188216e-8
    z = r * r
    sine = ((-1.9515295891e-4 * z + 8.3321608736e-3) * z - 1.6666654611e-1) * z * r + r
    cosine = ((2.443315711809948e-5 * z - 1.388731625493765e-3) * z + 4.166664568298827e-2) * z * z - 0.5 * z + 1.0
    halves = jnp.floor(quarter * 0.5)
    odd = quarter - 2.0 * halves
    minus = 1.0 - 2.0 * (halves - 2.0 * jnp.floor(halves * 0.5))
    swap = odd > 0.5
    return (
        jnp.where(swap, cosine, sine) * minus,
        jnp.where(swap, -sine, cosine) * minus,
    )


def kernel(
    sky, coef, basis, aperture, table_hbm,
    gradient_out, object_out,
    tab, skyp, coef_v, coef_send, coef_recv, mask_v, base, base3,
    edges, img, halo, turned, pre, pim, fpr, fpi, fmr, fmi, tre, tim, dre, dim_,
    sums, packed, pow_send, pow_recv, sum_send, sum_recv, obj_send, obj_all, ore, oim, dph,
    full, out_send, out_recv, part_send, part_recv, ret_send, ret_recv,
    local_sem, send_sem, recv_sem,
):
    place, strip = lax.axis_index("frame"), lax.axis_index("patch")
    me, z = place // DEPTH, place % DEPTH

    y, x = me // 2, me % 2
    other = 1 - x
    near, far, back_y = y + 1 - 2 * (y % 2), 3 - y, (y + 2) % 4
    close = [near * 2 + x, far * 2 + x, y * 2 + other]
    distant = [near * 2 + other, far * 2 + other, back_y * 2 + x, back_y * 2 + other]
    peers = distant[::-1] + close[::-1]

    def at(group, depth, which=None):
        return {"frame": group * DEPTH + depth, "patch": strip if which is None else which}

    def remote(src, dst, exchange, device):
        at_sem = EXCHANGES.index(exchange)
        return pltpu.make_async_remote_copy(
            src_ref=src, dst_ref=dst, send_sem=send_sem.at[at_sem], recv_sem=recv_sem.at[at_sem],
            device_id=device, device_id_type=MESH,
        )

    def everything(ref, exchange):
        return remote(ref, ref, exchange, at(peers[0], z))

    def table(name, half=None):
        row, count, width = FIRST[name]
        if half is None:
            return tab[row : row + count, :width]
        return tab[row : row + count, half * 128 : half * 128 + 128]

    def from_left(name, x):
        h, r = split(x)
        return mm(table(name), jnp.concatenate([h, r, h]))

    def from_right(x, name, half=None):
        h, r = split(x)
        return mm(lanes(h[:, :BOX], r[:, :BOX], h[:, :BOX]), table(name, half))

    loads = [
        pltpu.make_async_copy(coef.at[0], coef_v, local_sem.at[0]),
        pltpu.make_async_copy(basis.at[:, pl.ds(LOW * SIDE, FLAT)], base, local_sem.at[1]),
        pltpu.make_async_copy(sky.at[0], skyp.at[pl.ds(RIM, 512)], local_sem.at[2]),
        pltpu.make_async_copy(table_hbm, tab, local_sem.at[3]),
        pltpu.make_async_copy(aperture, mask_v, local_sem.at[4]),
    ]
    for load in loads:
        load.start()

    barrier = pltpu.get_barrier_semaphore()
    beside = lax.rem(strip + jnp.where(me < 4, STRIPS - 1, 1), STRIPS)

    def greet(device):
        pl.semaphore_signal(barrier, inc=1, device_id=device, device_id_type=MESH)

    for d in FAR_FIRST:
        greet(at(me, lax.rem(z + d, DEPTH)))
    for t in [*peers, me]:
        greet(at(t, z, beside))
    for t in peers:
        greet(at(t, z))

    skyp[pl.ds(0, RIM), :] = jnp.zeros((RIM, 256), f32)
    skyp[pl.ds(512 + RIM, 120), :] = jnp.zeros((120, 256), f32)
    loads[0].wait()
    for p in range(GROUP):
        row = coef_v[p : p + 1, :]
        coef_send[p] = lanes(row, row)
    loads[2].wait()
    for half in range(2):
        strip_t = skyp[:, half * 128 : half * 128 + 128].T
        for r in range(4):
            edges[2 * half, r] = strip_t[:8, r * TILE : r * TILE + SIDE]
            edges[2 * half + 1, r] = strip_t[120:, r * TILE : r * TILE + SIDE]
    pl.semaphore_wait(barrier, GROUP - 1 + DEPTH - 1 + GROUP)

    for t in peers:
        remote(coef_send.at[t], coef_recv.at[me], "coef", at(t, z)).start()
    coef_recv[me] = coef_send[me]

    def main_of(t):
        return skyp.at[
            pl.ds(pl.multiple_of(lax.rem(t, 4) * TILE, TILE), SIDE), pl.ds(pl.multiple_of((t // 4) * 128, 128), 128)
        ]

    def edge_of(kind, t):
        return edges.at[kind, lax.rem(t, 4)]

    for t in peers:
        kind, side = jnp.where(t < 4, 2, 1), jnp.where(t < 4, 1, 0)
        remote(edge_of(kind, t), halo.at[me, side], "own", at(t, z)).start()
    for p in range(GROUP):
        kind, side, step = (3, 0, 1) if p < 4 else (0, 1, STRIPS - 1)
        remote(edge_of(kind, p), halo.at[me, side], "cross", at(p, z, lax.rem(strip + step, STRIPS))).start()
    batches = {"img_close": close, "img_mid": distant[:2], "img_last": distant[2:]}
    for exchange, partners in batches.items():
        for t in partners:
            remote(main_of(t), img.at[me], exchange, at(t, z)).start()
    own_side = jnp.where(me < 4, 1, 0)
    mine = [
        pltpu.make_async_copy(main_of(me), img.at[me], local_sem.at[5]),
        pltpu.make_async_copy(edge_of(jnp.where(me < 4, 2, 1), me), halo.at[me, own_side], local_sem.at[6]),
    ]
    for c in mine:
        c.start()

    loads[1].wait()

    def cut(g, carry):
        at_g = pl.ds(pl.multiple_of(g * PERIOD, 128), PERIOD)
        x = base[:, at_g]
        h, r = split(x)
        base3[0:MODES, at_g] = h
        base3[MODES : 2 * MODES, at_g] = r
        base3[2 * MODES :, at_g] = (x - h.astype(f32) - r.astype(f32)).astype(bf16)
        return carry

    lax.fori_loop(0, BOX // 8, cut, 0)
    for load in loads[3:]:
        load.wait()

    lane = lax.broadcasted_iota(jnp.int32, (8, 128), 1)
    mask = mask_v[LOW : LOW + BOX, 0:128].astype(f32)
    mask = pltpu.roll(mask, 128 - LOW, 1)
    mask = jnp.where(lax.broadcasted_iota(jnp.int32, (BOX, 128), 1) < BOX, mask, 0.0)
    dph[0:BOX, :] = mask * jnp.sqrt(jnp.full((BOX, 128), 1.0 / (SIDE * SIDE), f32) / jnp.sum(mask))

    everything(coef_recv.at[pl.ds(0, GROUP - 1)], "coef").wait_recv()
    weights = jnp.concatenate([coef_recv[j] for j in range(GROUP)])
    w0 = weights.astype(bf16).astype(f32)
    w1 = (weights - w0).astype(bf16).astype(f32)
    w2 = weights - w0 - w1
    weights = jnp.concatenate([lanes(w, w[:, :MODES]) for w in (w0, w1, w2)]).astype(bf16)

    starts = [divmod(SIDE * r + LOW, 128) for r in range(8)]

    def pupils(g, carry):
        ph = mm(weights, base3[:, pl.ds(pl.multiple_of(g * PERIOD, 128), PERIOD)])
        ph = ph[0:8] + (ph[8:16] + ph[16:24])
        rows = []
        for tile, off in starts:
            x = ph[:, tile * 128 : tile * 128 + 128]
            if off:
                x = pltpu.roll(x, 128 - off, 1)
            if off + BOX > 128:
                y = pltpu.roll(ph[:, tile * 128 + 128 : tile * 128 + 256], 128 - off, 1)
                x = jnp.where(lane < 128 - off, x, y)
            rows.append(x)
        m = dph[pl.ds(pl.multiple_of(g * 8, 8), 8), :]
        m = jnp.concatenate([jnp.broadcast_to(m[r : r + 1], (8, 128)) for r in range(8)])
        sine, cosine = sine_cosine(jnp.concatenate(rows))
        at_g = pl.ds(pl.multiple_of(g * 64, 64), 64)
        pre[at_g, :] = m * cosine
        pim[at_g, :] = m * sine
        return carry

    lax.fori_loop(0, BOX // 8, pupils, 0, unroll=5)

    def of_frame(ref, f):
        return ref[pl.ds(f, BOX, stride=GROUP), :]

    def fold(x):
        return x[:BOX] + x[BOX:], x[:BOX] - x[BOX:]

    def stack(*parts):
        return jnp.concatenate(parts)

    def transfers(n, carry):
        fs = [n * UNROLL + m for m in range(UNROLL)]
        rows = []
        for f in fs:
            y = from_left("pupil_rows", lanes(of_frame(pre, f), of_frame(pim, f)))
            cr, ci, sr, si = y[:BOX, :128], y[:BOX, 128:], y[BOX:, :128], y[BOX:, 128:]
            rows += [cr + si, cr - si, ci - sr, ci + sr]
        y = from_right(stack(*rows), "pupil_columns")
        even, odd = [], []
        for m, f in enumerate(fs):
            r, i = y[4 * m * BOX : (4 * m + 2) * BOX], y[(4 * m + 2) * BOX : (4 * m + 4) * BOX]
            p_re, p_im = r[:, :128] + i[:, 128:], i[:, :128] - r[:, 128:]
            m_re, m_im = r[:, :128] - i[:, 128:], i[:, :128] + r[:, 128:]
            fpr[f], fpi[f], fmr[f], fmi[f] = p_re, p_im, m_re, m_im
            plus = p_re * p_re + p_im * p_im
            minus = m_re * m_re + m_im * m_im
            even += fold(plus + minus)
            odd += fold(plus - minus)
        x_re = from_right(stack(*even), "focal_columns", 0)
        x_im = from_right(stack(*odd), "focal_columns", 1)
        for m, f in enumerate(fs):
            x = lanes(x_re[2 * m * BOX : 2 * (m + 1) * BOX], x_im[2 * m * BOX : 2 * (m + 1) * BOX])
            c = from_left("focal_even", x[:BOX])
            s = from_left("focal_odd", x[BOX:])
            cr, ci, sr, si = c[:, :128], c[:, 128:], s[:, :128], s[:, 128:]
            tre[f] = stack(cr + si, cr - si)
            tim[f] = stack(ci - sr, ci + sr)
        return carry

    lax.fori_loop(0, GROUP // UNROLL, transfers, 0)

    lane40 = lax.broadcasted_iota(jnp.int32, (FOLD, 128), 1)
    row40 = lax.broadcasted_iota(jnp.int32, (FOLD, 128), 0)
    border = jnp.where(row40 < 24, 73, jnp.where(row40 < 32, 68, 65))

    def shifted(x, back):
        return stack(*[
            pltpu.roll(x[a:b], 128 - by if back else by, 1) for a, b, by in ((0, 24, 73), (24, 32, 68), (32, 40, 65))
        ])

    def pack(x, into, at_row):
        for sign in range(2):
            wide, narrow = x[sign * BOX : sign * BOX + FOLD], x[sign * BOX + FOLD : (sign + 1) * BOX]
            packed[...] = jnp.where(lane40 < border, wide, shifted(narrow, False))
            for d in range(DEPTH):
                into[d, at_row + sign * CHUNK : at_row + (sign + 1) * CHUNK, :] = packed[d * CHUNK : (d + 1) * CHUNK, :]

    power = jnp.zeros((2 * BOX, 128), f32)
    for f in range(GROUP):
        power = power + (tre[f] * tre[f] + tim[f] * tim[f])
    pack(power, pow_send, 0)
    for d in FAR_FIRST:
        t = lax.rem(z + d, DEPTH)
        remote(pow_send.at[t], pow_recv.at[z], "pow", at(me, t)).start()
    pow_recv[z] = pow_send[z]

    for c in mine:
        c.wait()
    all_own, all_cross = halo.at[pl.ds(0, GROUP - 1), 0], halo.at[:, 0]
    everything(all_cross, "cross").wait_recv()
    everything(all_own, "own").wait_recv()
    row = lax.broadcasted_iota(jnp.int32, (128, 256), 0)
    left_on = jnp.where(jnp.logical_and(strip == 0, me < 4), 0.0, 1.0)
    right_on = jnp.where(jnp.logical_and(strip == STRIPS - 1, me >= 4), 0.0, 1.0)
    rims = lanes(halo[...].reshape(128, SIDE), jnp.zeros((128, 256 - SIDE), f32))
    rims = rims * jnp.where(lax.rem(row, 16) < 8, left_on, right_on)
    rims = rims.T[:SIDE]
    for f in range(GROUP):
        turned[f] = pltpu.roll(rims, (128 - 16 * f) % 128, 1) if f else rims

    sums[...] = jnp.zeros_like(sums)

    def data(fs):
        h, r = split(stack(*[lanes(img[f], turned[f]) for f in fs]))
        x = mm3((h[:, :SIDE], r[:, :SIDE]), (table("data_columns"), table("data_columns_low")))
        n_re, n_im = sums[0], sums[1]
        for m, f in enumerate(fs):
            h, r = split(x[m * SIDE : (m + 1) * SIDE])
            h = stack(h, r, h)
            y = mm(table("data_rows"), h[:256]) + mm(table("data_rows_end"), h[256:])
            cr, ci, sr, si = y[:BOX, :128], y[:BOX, 128:], y[BOX:, :128], y[BOX:, 128:]
            d_re, d_im = stack(cr + si, cr - si), stack(ci - sr, ci + sr)
            dre[f] = d_re
            dim_[f] = d_im
            t_re, t_im = tre[f], tim[f]
            n_re = n_re + (t_re * d_re + t_im * d_im)
            n_im = n_im + (t_re * d_im - t_im * d_re)
        sums[0], sums[1] = n_re, n_im

    everything(img.at[pl.ds(0, 3)], "img_close").wait_recv()
    data([me, *close])
    everything(img.at[pl.ds(0, 2)], "img_mid").wait_recv()
    data(distant[:2])
    everything(img.at[pl.ds(0, 2)], "img_last").wait_recv()
    data(distant[2:])

    pack(sums[0], sum_send, 0)
    pack(sums[1], sum_send, 2 * CHUNK)
    for d in FAR_FIRST:
        t = lax.rem(z + d, DEPTH)
        remote(sum_send.at[t], sum_recv.at[z], "sum", at(me, t)).start()
    sum_recv[z] = sum_send[z]
    everything(pow_recv.at[pl.ds(0, DEPTH - 1)], "pow").wait_recv()
    power = pow_recv[0]
    for j in range(1, DEPTH):
        power = power + pow_recv[j]
    power = power + DAMPING
    everything(sum_recv.at[pl.ds(0, DEPTH - 1)], "sum").wait_recv()
    total = sum_recv[0]
    for j in range(1, DEPTH):
        total = total + sum_recv[j]
    obj_send[...] = total / stack(power, power)
    for d in FAR_FIRST:
        t = lax.rem(z + d, DEPTH)
        remote(obj_send, obj_all.at[z], "obj", at(me, t)).start()
    obj_all[z] = obj_send[...]
    everything(obj_all.at[pl.ds(0, DEPTH - 1)], "obj").wait_recv()
    for part, ref in enumerate((ore, oim)):
        for sign in range(2):
            at_row = (2 * part + sign) * CHUNK
            for d in range(DEPTH):
                packed[d * CHUNK : (d + 1) * CHUNK, :] = obj_all[d, at_row : at_row + CHUNK, :]
            x = packed[...]
            ref[sign * BOX : sign * BOX + FOLD, :] = jnp.where(lane40 < jnp.minimum(border, HALF), x, 0.0)
            ref[sign * BOX + FOLD : (sign + 1) * BOX, :] = jnp.where(lane40 < 128 - border, shifted(x, True), 0.0)

    scale = 4.0 * 2.0 / (SIDE * SIDE)

    def back(n, carry):
        fs = [n * UNROLL + m for m in range(UNROLL)]
        o_re, o_im = -scale * ore[...], -scale * oim[...]
        o_square = scale * (ore[...] * ore[...] + oim[...] * oim[...])
        h_re, h_im = [], []
        for f in fs:
            d_re, d_im = dre[f], dim_[f]
            re_even, re_odd = fold(d_re * o_re + d_im * o_im + o_square * tre[f])
            im_even, im_odd = fold(d_im * o_re - d_re * o_im + o_square * tim[f])
            c = from_left("disc_even", lanes(re_even, im_even))
            s = from_left("disc_odd", lanes(re_odd, im_odd))
            cr, ci, sr, si = c[:, :128], c[:, 128:], s[:, :128], s[:, 128:]
            h_re += [cr - si, cr + si]
            h_im += [ci + sr, ci - sr]
        even = from_right(stack(*h_re), "focal_columns", 0)
        odd = from_right(stack(*h_im), "focal_columns", 1)
        sum_rows, gap_rows = [], []
        for m, f in enumerate(fs):
            at_m = slice(2 * m * BOX, 2 * (m + 1) * BOX)
            plus, minus = even[at_m] + odd[at_m], even[at_m] - odd[at_m]
            p_re, p_im, m_re, m_im = plus * fpr[f], plus * fpi[f], minus * fmr[f], minus * fmi[f]
            sum_rows += [p_re + m_re, p_im + m_im]
            gap_rows += [p_re - m_re, p_im - m_im]
        qc = from_right(stack(*sum_rows), "back_columns", 0)
        qs = from_right(stack(*gap_rows), "back_columns", 1)
        for m, f in enumerate(fs):
            at_re, at_im = slice(4 * m * BOX, (4 * m + 2) * BOX), slice((4 * m + 2) * BOX, (4 * m + 4) * BOX)
            re_even, re_odd = fold(qc[at_re] - qs[at_im])
            im_even, im_odd = fold(qc[at_im] + qs[at_re])
            c = from_left("back_even", lanes(re_even, im_even))
            s = from_left("back_odd", lanes(re_odd, im_odd))
            g_re, g_im = c[:, :128] - s[:, 128:], c[:, 128:] + s[:, :128]
            dph[pl.ds(f, BOX, stride=GROUP), :] = of_frame(pre, f) * g_im - of_frame(pim, f) * g_re
        return carry

    lax.fori_loop(0, GROUP // UNROLL, back, 0)

    def project(g, total):
        tiles = [jnp.zeros((8, 128), f32) for _ in range(9)]
        for r, (tile, off) in enumerate(starts):
            x = dph[pl.ds(pl.multiple_of(g * 64, 64) + 8 * r, 8), :]
            if off:
                x = pltpu.roll(x, off, 1)
            if off + BOX > 128:
                tiles[tile + 1] += jnp.where(lane < off, x, 0.0)
                x = jnp.where(lane < off, 0.0, x)
            tiles[tile] += x
        x = jnp.concatenate(split(lanes(*tiles)))
        modes = base3[0 : 2 * MODES, pl.ds(pl.multiple_of(g * PERIOD, 128), PERIOD)]
        return total + lax.dot_general(x, modes, (((1,), (1,)), ((), ())), preferred_element_type=f32)

    total = lax.fori_loop(0, BOX // 8, project, jnp.zeros((16, 128), f32), unroll=5)
    total = total[:8] + total[8:]
    gradient = total + pltpu.roll(total, MODES, 1)

    part_send[0] = jnp.sum(gradient, axis=0, keepdims=True)

    groups = list(zip([*peers, me], (3, 2, 2, 2, 1, 1, 1, 0)))
    depths = [(z, 0)] + [(lax.rem(z + d, DEPTH), min(d, DEPTH - d)) for d in range(1, DEPTH)]
    ways = [(a + b, group, depth) for group, a in groups for depth, b in depths if a + b]
    for _, group, depth in sorted(ways, key=lambda way: -way[0]):
        remote(part_send, part_recv.at[pl.ds(place, 1)], "part", at(group, depth)).start()
    for j in range(GROUP):
        ret_send[j] = gradient[j : j + 1]
    for t in peers:
        remote(ret_send.at[t], ret_recv.at[me], "ret", at(t, z)).start()
    part_recv[place] = part_send[0]
    ret_recv[me] = ret_send[me]

    r_at = lax.broadcasted_iota(jnp.int32, (2 * SIDE, 2 * BOX), 0)
    c_at = lax.broadcasted_iota(jnp.int32, (2 * SIDE, 2 * BOX), 1)
    mirrored = r_at >= SIDE
    k = jnp.where(mirrored, r_at - SIDE, r_at)
    minus = (k >= HALF) != mirrored
    k = jnp.where(k >= HALF, SIDE - k, k)
    k = jnp.where(k > 36, FOLD + 72 - k, k) + jnp.where(minus, BOX, 0)
    pick_rows = jnp.where(k == c_at, 1.0, 0.0).astype(bf16)
    r_at = lax.broadcasted_iota(jnp.int32, (128, 256), 0)
    c_at = lax.broadcasted_iota(jnp.int32, (128, 256), 1)
    flip_columns = jnp.where(
        jnp.logical_and(r_at + c_at == SIDE, jnp.logical_and(c_at >= HALF, c_at < SIDE)), 1.0, 0.0
    ).astype(bf16)
    parts = [mm(pick_rows, part) for part in split(lanes(ore[...], oim[...]))]
    lane_full = lax.broadcasted_iota(jnp.int32, (SIDE, 128), 1)
    for n, sign in ((0, 1.0), (1, -1.0)):
        at_n = slice(n * 128, n * 128 + 128)
        half = parts[0][:SIDE, at_n] + parts[1][:SIDE, at_n]
        mirror = [mm(part[SIDE:, at_n].astype(bf16), flip_columns) for part in parts]
        mirror = sign * (mirror[0] + mirror[1])
        full[2 * n] = jnp.where(lane_full < HALF, half, mirror[:, :128])
        full[2 * n + 1] = mirror[:, 128:]
    first_row = z * 9 // 4
    for n in range(2):
        placed = [jnp.zeros((8, 128), f32) for _ in range(6)]
        for t in range(3):
            for piece in range(2):
                x = full[2 * n + piece, pl.ds(first_row + t, GROUP, stride=SIDE // GROUP), :]
                tile, off = divmod(SIDE * t + 128 * piece, 128)
                if off:
                    x = pltpu.roll(x, off, 1)
                    placed[tile + 1] += jnp.where(lane < off, x, 0.0)
                    x = jnp.where(lane < off, 0.0, x)
                placed[tile] += x
        placed = lanes(*placed)
        picked = jnp.zeros((8, 384), f32)
        for m in range(4):
            moved = pltpu.roll(placed, 768 - 36 * m, 1) if m else placed
            picked = picked + jnp.where(lax.rem(z, 4) == m, 1.0, 0.0) * moved[:, :384]
        for i in range(GROUP):
            out_send[i, n : n + 1, :] = picked[i : i + 1]
    for t in peers:
        remote(out_send.at[t], out_recv.at[me], "out", at(t, z)).start()
    out_recv[me] = out_send[me]

    rest = {
        "coef": coef_recv.at[pl.ds(0, GROUP - 1)],
        "own": all_own,
        "cross": all_cross,
        "img_close": img.at[pl.ds(0, 3)],
        "img_mid": img.at[pl.ds(0, 2)],
        "img_last": img.at[pl.ds(0, 2)],
        "pow": pow_recv.at[pl.ds(0, DEPTH - 1)],
        "sum": sum_recv.at[pl.ds(0, DEPTH - 1)],
        "obj": obj_all.at[pl.ds(0, DEPTH - 1)],
        "out": out_recv.at[pl.ds(0, GROUP - 1)],
        "ret": ret_recv.at[pl.ds(0, GROUP - 1)],
        "part": part_recv.at[pl.ds(0, FRAMES - 1)],
    }
    for exchange, ref in rest.items():
        everything(ref, exchange).wait_send()
    everything(rest["out"], "out").wait_recv()
    for p in range(GROUP):
        object_out[p] = out_recv[p, :, :SHARE]
    everything(rest["ret"], "ret").wait_recv()
    everything(rest["part"], "part").wait_recv()
    for p in range(GROUP):
        mean = part_recv[p * DEPTH]
        for n in range(1, DEPTH):
            mean = mean + part_recv[p * DEPTH + n]
        gradient_out[0, p : p + 1, :] = (ret_recv[p] - mean * (1.0 / FRAMES))[:, :MODES]


def body(sky_image, coefficients, mode_basis, aperture):
    vmem, dma = pltpu.VMEM, pltpu.SemaphoreType.DMA
    scratch = [
        vmem(TABLE.shape, bf16), vmem((640, 256), f32), vmem((GROUP, MODES), f32),
        vmem((GROUP, 1, 128), f32), vmem((GROUP, 1, 128), f32), vmem((SIDE, SIDE), jnp.int32), vmem((MODES, FLAT), f32),
        vmem((3 * MODES, FLAT), bf16),
        vmem((4, 4, 8, SIDE), f32), vmem((GROUP, SIDE, 128), f32), vmem((GROUP, 2, 8, SIDE), f32),
        vmem((GROUP, SIDE, 128), f32), vmem((8 * BOX, 128), f32), vmem((8 * BOX, 128), f32),
        *[vmem((GROUP, 2 * BOX, 128), f32)] * 8,
        vmem((2, 2 * BOX, 128), f32), vmem((FOLD, 128), f32),
        *[vmem((DEPTH, 2 * CHUNK, 128), f32)] * 2, *[vmem((DEPTH, 4 * CHUNK, 128), f32)] * 2,
        vmem((4 * CHUNK, 128), f32), vmem((DEPTH, 4 * CHUNK, 128), f32), vmem((2 * BOX, 128), f32), vmem((2 * BOX, 128), f32),
        vmem((8 * BOX, 128), f32), vmem((4, SIDE, 128), f32), vmem((GROUP, 2, 384), f32), vmem((GROUP, 2, 384), f32),
        vmem((1, 1, 128), f32), vmem((FRAMES, 1, 128), f32), vmem((GROUP, 1, 128), f32), vmem((GROUP, 1, 128), f32),
        dma((7,)), dma((len(EXCHANGES),)), dma((len(EXCHANGES),)),
    ]
    return pl.pallas_call(
        kernel,
        out_shape=(
            pltpu.VMEM((1, GROUP, MODES), f32),
            pltpu.VMEM((GROUP, 2, SHARE), f32),
        ),
        in_specs=[pl.BlockSpec(memory_space=pl.ANY)] * 5,
        out_specs=[pl.BlockSpec(memory_space=pltpu.VMEM)] * 2,
        scratch_shapes=scratch,
        compiler_params=pltpu.CompilerParams(collective_id=0, has_side_effects=True, vmem_limit_bytes=60 * 2**20),
    )(sky_image, coefficients, mode_basis, aperture, jnp.asarray(TABLE))


def solution(mesh):
    in_specs = (P("frame", None, "patch"), P("frame", "patch", None), P(), P())
    out_specs = (P("frame", "patch", None), P("patch", None, "frame"))
    return jax.shard_map(body, mesh=mesh, in_specs=in_specs, out_specs=out_specs, check_vma=False)
```
